32 devices in a mesh: dp: 2 (over x), ctx: 4 (over z), tp: 4 (over y, core).
Axes of the slice: x: 2, y: 2, z: 4, core: 2. Of those that a mesh axis runs over, the one named last changes fastest.
Arguments:
- tokens: bfloat16 [2, 2048, 4096], P('dp', 'ctx'), may hold values from -6 to 6
- norm_gain: float32 [4096], replicated, may hold values from 0.25 to 1.75
- zx_weight: bfloat16 [4096, 2, 8192], P(('dp', 'ctx'), None, 'tp'), may hold values from -0.09375 to 0.09375
- bc_weight: bfloat16 [4096, 2, 1024], P(('dp', 'ctx'), None, 'tp'), may hold values from -0.09375 to 0.09375
- dt_weight: bfloat16 [4096, 128], P(('dp', 'ctx'), 'tp'), may hold values from -0.09375 to 0.09375
- conv_x: float32 [5, 8192], P(None, 'tp'), may hold values from -3 to 3
- conv_bc: float32 [5, 2, 1024], P(None, None, 'tp'), may hold values from -3 to 3
- head_params: float32 [3, 128], P(None, 'tp'), may hold values from -12 to 4
- gate_gain: float32 [8192], P('tp'), may hold values from 0.25 to 1.75
- out_weight: bfloat16 [4096, 8192], P(('dp', 'ctx'), 'tp'), may hold values from -0.0625 to 0.0625
- cotangent: bfloat16 [2, 2048, 4096], P('dp', 'ctx'), may hold values from -6 to 6
Outputs:
- mixed: bfloat16 [2, 2048, 4096], P('dp', 'ctx')
- tokens_grad: float32 [2, 2048, 4096], P('dp', 'ctx')
- norm_gain_grad: float32 [4096], replicated
- zx_weight_grad: float32 [4096, 2, 8192], P(('dp', 'ctx'), None, 'tp')
- bc_weight_grad: float32 [4096, 2, 1024], P(('dp', 'ctx'), None, 'tp')
- dt_weight_grad: float32 [4096, 128], P(('dp', 'ctx'), 'tp')
- conv_x_grad: float32 [5, 8192], P(None, 'tp')
- conv_bc_grad: float32 [5, 2, 1024], P(None, None, 'tp')
- head_params_grad: float32 [3, 128], P(None, 'tp')
- gate_gain_grad: float32 [8192], P('tp')
- out_weight_grad: float32 [4096, 8192], P(('dp', 'ctx'), 'tp')
The draws below stay inside these ranges and needn't reach their ends.
All inputs are finite; a program needn't handle non-finite values.
Results may differ from the reference program's by a relative error of at most 0.0049.
The reference program's roundings to bfloat16 on the way count: a program that leaves them out, or rounds other values in their place, can miss the bound.
Values may be sent and summed in bfloat16 or wider, within the bound.
A program may use at most 448 MiB of HBM per device.

```python
import jax
import jax.numpy as jnp
from jax import lax

D = 4096
H = 128
P_SIZE = 64
G = 8
N = 128
STRETCH = 256
CONV = 4
DI = 8192
LEN = 2048
NSEQ = 2


def draw_head_params(key, part):
    key_step, key_pick, key_slow, key_fast, key_skip = jax.random.split(key, 5)
    length = LEN * 1.0
    slow_share = 0.5
    base_step = jnp.exp(jax.random.uniform(key_step, (H,), jnp.float32, jnp.log(0.01), jnp.log(0.1)))
    slow_pick = jax.random.uniform(key_pick, (H,), jnp.float32) < slow_share
    slow_rate = jnp.exp(jax.random.uniform(key_slow, (H,), jnp.float32, jnp.log(0.2 / length), jnp.log(1.2 / length)))
    fast_rate = jnp.exp(jax.random.uniform(key_fast, (H,), jnp.float32, jnp.log(1.2 / length), jnp.log(max(0.03, 8.0 / length))))
    decay_rate = jnp.where(slow_pick, slow_rate, fast_rate)
    step_bias = jnp.log(jnp.expm1(base_step))
    decay_log = jnp.log(decay_rate / base_step)
    skip_weight = jax.random.uniform(key_skip, (H,), jnp.float32, 0.5, 1.5)
    return jnp.stack([step_bias, decay_log, skip_weight]).astype(jnp.float32)


def levels(stream_key, dims, cuts, least, top_value):
    gain = 1.0
    for position, parts in cuts:
        steps = jax.random.uniform(jax.random.fold_in(jax.random.fold_in(stream_key, 6), position), (parts,), jnp.float32, least / len(cuts), top_value / len(cuts))
        gain = gain * jnp.repeat(jnp.exp(steps), dims[position] // parts).reshape((-1,) + (1,) * (len(dims) - 1 - position))
    return gain


def gaussian(rng, dims, spread, bound, cuts=(), dtype=jnp.bfloat16):
    drawn = jax.random.normal(rng, dims, jnp.float32) * spread
    if len(cuts) > 0:
        drawn = levels(rng, dims, cuts, -0.22, 0.18) * drawn
    return jnp.clip(drawn, min=-bound, max=bound).astype(dtype)


def setup_inputs(seed: int = 0) -> dict:
    key_list = jax.random.split(jax.random.key(seed), 12)
    tokens = gaussian(key_list[0], (NSEQ, LEN, D), 1.0, 6.0, ((0, 2), (1, 4)))
    norm_gain = jnp.clip(1.0 + 0.15 * jax.random.normal(key_list[1], (D,), jnp.float32), 0.25, 1.75)
    zx_weight = gaussian(key_list[2], (D, 2, DI), D ** -0.5, 0.09375, ((0, 8), (2, 4)))
    bc_weight = gaussian(key_list[3], (D, 2, G * N), D ** -0.5, 0.09375, ((0, 8), (2, 4)))
    dt_weight = gaussian(key_list[4], (D, H), D ** -0.5, 0.09375, ((0, 8), (1, 4)))
    conv_x = gaussian(key_list[5], (CONV + 1, DI), CONV ** -0.5, 3.0, ((1, 4),), jnp.float32)
    conv_bc = gaussian(key_list[6], (CONV + 1, 2, G * N), CONV ** -0.5, 3.0, ((2, 4),), jnp.float32)
    head_params = draw_head_params(jax.random.fold_in(key_list[11], 71), 0)
    gate_gain = jnp.clip(1.0 + 0.15 * jax.random.normal(key_list[8], (DI,), jnp.float32), 0.25, 1.75)
    out_weight = gaussian(key_list[9], (D, DI), DI ** -0.5, 0.0625, ((0, 8), (1, 4)))
    cotangent = gaussian(key_list[10], (NSEQ, LEN, D), 1.0, 6.0, ((0, 2), (1, 4)))
    return dict(tokens=tokens, norm_gain=norm_gain, zx_weight=zx_weight, bc_weight=bc_weight, dt_weight=dt_weight, conv_x=conv_x, conv_bc=conv_bc, head_params=head_params, gate_gain=gate_gain, out_weight=out_weight, cotangent=cotangent)


EPS = 1e-05
HIGH = lax.Precision.HIGHEST

@jax.custom_vjp
def low(v):
    return lax.optimization_barrier(v.astype(jnp.bfloat16)).astype(jnp.float32)

@jax.custom_vjp
def low_back(v):
    return v

def low_keep(v):
    return (low(v), None)

def low_pass(kept, grad):
    return (grad,)

def back_keep(v):
    return (v, None)

def back_low(kept, grad):
    return (low(grad),)
low.defvjp(low_keep, low_pass)
low_back.defvjp(back_keep, back_low)

def matmul_high(left_side, right_side):
    return jnp.dot(left_side, right_side, precision=HIGH, preferred_element_type=jnp.float32)

def conv_silu(padded, kernel):
    tap_count = kernel.shape[0] - 1
    length = padded.shape[0] - tap_count + 1
    running = kernel[tap_count] + kernel[0] * padded[0:length]
    for offset in range(1, tap_count):
        running = running + kernel[offset] * padded[offset:offset + length]
    return jax.nn.silu(running)

def block_step(memory, pieces, log_decay):
    x_heads, step_sizes, inject, readout = pieces
    block_len = x_heads.shape[0]
    groups = inject.shape[1]
    per_group = x_heads.shape[1] // groups
    head_dim = x_heads.shape[2]
    cumulative = jnp.cumsum(step_sizes * log_decay, axis=0)
    gap_matrix = cumulative[:, None, :] - cumulative[None, :, :]
    causal = jnp.tril(jnp.ones((block_len, block_len), jnp.float32))
    decays = jnp.exp(jnp.minimum(gap_matrix, 0.0)) * causal[:, :, None]
    scores = jnp.einsum('ign,jgn->ijg', readout, inject, precision=HIGH)
    mixing = decays.reshape(block_len, block_len, groups, per_group) * scores[:, :, :, None]
    scaled = (x_heads * step_sizes[:, :, None]).reshape(block_len, groups, per_group, head_dim)
    local_out = jnp.einsum('ijgh,jghp->ighp', mixing, scaled, precision=HIGH)
    carried = jnp.einsum('ign,ghpn->ighp', readout, memory, precision=HIGH)
    carried = carried * jnp.exp(cumulative).reshape(block_len, groups, per_group)[:, :, :, None]
    to_end = jnp.exp(cumulative[-1] - cumulative).reshape(block_len, groups, per_group)
    new_memory = memory * jnp.exp(cumulative[-1]).reshape(groups, per_group)[:, :, None, None]
    new_memory = new_memory + jnp.einsum('jgn,jghp->ghpn', inject, scaled * to_end[:, :, :, None], precision=HIGH)
    return (new_memory, (local_out + carried).reshape(block_len, groups * per_group, head_dim))

def ssd_scan(x_heads, step_sizes, log_decay, inject, readout):
    length, head_count, head_dim = x_heads.shape
    groups, state_dim = (inject.shape[1], inject.shape[2])
    block_count = length // STRETCH
    pieces = (x_heads.reshape(block_count, STRETCH, head_count, head_dim), step_sizes.reshape(block_count, STRETCH, head_count), inject.reshape(block_count, STRETCH, groups, state_dim), readout.reshape(block_count, STRETCH, groups, state_dim))
    zero_memory = jnp.zeros((groups, head_count // groups, head_dim, state_dim), jnp.float32)
    advance = jax.checkpoint(lambda memory, piece_set: block_step(memory, piece_set, log_decay))
    last_memory, outputs = lax.scan(advance, zero_memory, pieces)
    return outputs.reshape(length, head_count, head_dim)

def layer(hidden, norm_gain, zx_weight, bc_weight, dt_weight, conv_x, conv_bc, head_params, gate_gain, out_weight):
    length = hidden.shape[0]
    inner_width = H * P_SIZE
    pair_width = G * N
    rscale = lax.rsqrt(lax.optimization_barrier(jnp.mean(hidden * hidden, axis=-1, keepdims=True)) + EPS)
    normed = low(hidden * rscale * norm_gain)
    proj_zx = low_back(matmul_high(normed, zx_weight.reshape(D, 2 * inner_width)))
    proj_bc = low_back(matmul_high(normed, bc_weight.reshape(D, 2 * pair_width)))
    raw_dt = low_back(matmul_high(normed, dt_weight))
    gate_pre = proj_zx[:, :inner_width]
    conv_input = low(jnp.concatenate([proj_zx[:, inner_width:], proj_bc], axis=1))
    kernel = jnp.concatenate([conv_x, conv_bc.reshape(CONV + 1, 2 * pair_width)], axis=1)
    padded = jnp.concatenate([jnp.zeros((CONV - 1, conv_input.shape[1]), jnp.float32), conv_input], axis=0)
    conv_out = low(conv_silu(padded, kernel))
    x_heads = conv_out[:, :inner_width].reshape(length, H, P_SIZE)
    inject = conv_out[:, inner_width:inner_width + pair_width].reshape(length, G, N)
    readout = conv_out[:, inner_width + pair_width:].reshape(length, G, N)
    step_sizes = jax.nn.softplus(raw_dt + head_params[0])
    log_decay = -jnp.exp(head_params[1])
    outputs = ssd_scan(x_heads, step_sizes, log_decay, inject, readout)
    outputs = outputs + head_params[2][:, None] * x_heads
    gated = outputs.reshape(length, inner_width) * jax.nn.silu(gate_pre)
    grouped = gated.reshape(length, G, inner_width // G)
    grouped = grouped * lax.rsqrt(lax.optimization_barrier(jnp.mean(grouped * grouped, axis=-1, keepdims=True)) + EPS)
    gated_norm = low(grouped.reshape(length, inner_width) * gate_gain)
    return hidden + matmul_high(gated_norm, out_weight.T)

def reference(tokens, norm_gain, zx_weight, bc_weight, dt_weight, conv_x, conv_bc, head_params, gate_gain, out_weight, cotangent):
    weights = tuple((item.astype(jnp.float32) for item in (norm_gain, zx_weight, bc_weight, dt_weight, conv_x, conv_bc, head_params, gate_gain, out_weight)))

    def per_sequence(totals, inputs_pair):
        seq_tokens, seq_grad = inputs_pair
        out_value, back_fn = jax.vjp(layer, seq_tokens.astype(jnp.float32), *weights)
        grad_list = back_fn(seq_grad.astype(jnp.float32))
        new_totals = tuple((first + second for first, second in zip(totals, grad_list[1:])))
        return (new_totals, (out_value.astype(jnp.bfloat16), grad_list[0]))
    zero_totals = tuple((jnp.zeros_like(item) for item in weights))
    totals, (mixed, tokens_grad) = lax.scan(per_sequence, zero_totals, (tokens, cotangent))
    return (mixed, tokens_grad, totals[0], totals[1], totals[2], totals[3], totals[4], totals[5], totals[6], totals[7], totals[8])
```

```python
import jax
import jax.numpy as jnp
from jax import lax
from jax.sharding import PartitionSpec as P

P_SIZE = 64
N = 128
STRETCH = 256
EPS = 1e-05
HIGH = lax.Precision.HIGHEST
F32 = jnp.float32
BF16 = jnp.bfloat16


def dot_last(left_side, right_side):
    return lax.dot_general(left_side, right_side, (((1,), (1,)), ((), ())), preferred_element_type=F32)


def dot_first(left_side, right_side):
    return lax.dot_general(left_side, right_side, (((0,), (0,)), ((), ())), preferred_element_type=F32)


def conv_silu(padded, kernel):
    tap_count = kernel.shape[0] - 1
    length = padded.shape[0] - tap_count + 1
    running = kernel[tap_count] + kernel[0] * padded[0:length]
    for offset in range(1, tap_count):
        running = running + kernel[offset] * padded[offset : offset + length]
    return jax.nn.silu(running)


def block_step(memory, pieces, log_decay):
    x_heads, step_sizes, inject, readout = pieces
    block_len = x_heads.shape[0]
    cumulative = jnp.cumsum(step_sizes * log_decay, axis=0)
    gap_matrix = cumulative[:, None, :] - cumulative[None, :, :]
    causal = jnp.tril(jnp.ones((block_len, block_len), F32))
    decays = jnp.exp(jnp.minimum(gap_matrix, 0.0)) * causal[:, :, None]
    scores = jnp.einsum("in,jn->ij", readout, inject, precision=HIGH)
    mixing = decays * scores[:, :, None]
    scaled = x_heads * step_sizes[:, :, None]
    local_out = jnp.einsum("ijh,jhp->ihp", mixing, scaled, precision=HIGH)
    carried = jnp.einsum("in,hpn->ihp", readout, memory, precision=HIGH)
    carried = carried * jnp.exp(cumulative)[:, :, None]
    to_end = jnp.exp(cumulative[-1] - cumulative)
    new_memory = memory * jnp.exp(cumulative[-1])[:, None, None]
    new_memory = new_memory + jnp.einsum("jn,jhp->hpn", inject, scaled * to_end[:, :, None], precision=HIGH)
    return (new_memory, local_out + carried)


def mixer(x_flat, maps, raw_dt, head_params):
    length, width = x_flat.shape
    heads = head_params.shape[1]
    count = length // STRETCH
    step_sizes = jax.nn.softplus(raw_dt + head_params[0])
    log_decay = -jnp.exp(head_params[1])
    x_heads = x_flat.reshape(length, heads, P_SIZE)
    pieces = (
        x_heads.reshape(count, STRETCH, heads, P_SIZE),
        step_sizes.reshape(count, STRETCH, heads),
        maps[:, :N].reshape(count, STRETCH, N),
        maps[:, N:].reshape(count, STRETCH, N),
    )
    zero_memory = jnp.zeros((heads, P_SIZE, N), F32)
    advance = jax.checkpoint(lambda memory, piece_set: block_step(memory, piece_set, log_decay))
    _, outputs = lax.scan(advance, zero_memory, pieces)
    outputs = outputs.reshape(length, heads, P_SIZE) + head_params[2][:, None] * x_heads
    return outputs.reshape(length, width)


def spread_rows(value):
    part = value.shape[0] // lax.axis_size("tp")
    mine = lax.dynamic_slice_in_dim(value, lax.axis_index("tp") * part, part, 0)
    along = lax.all_gather(mine, "ctx", axis=0)
    return lax.all_gather(along, "tp", axis=1).reshape(-1, value.shape[1])


def fetch_weight(packed):
    mine = lax.all_to_all(packed, "ctx", 0, 0, tiled=True)
    return lax.all_gather(mine.reshape(-1, packed.shape[2]), "dp", axis=0, tiled=True)


def return_grad(grad, rows):
    ndp, nctx = lax.axis_size("dp"), lax.axis_size("ctx")
    parts = grad.astype(BF16).reshape(ndp, nctx * rows, grad.shape[1])
    summed = jnp.sum(lax.all_to_all(parts, "dp", 0, 0, tiled=True).astype(F32), axis=0)
    back = lax.all_to_all(summed.astype(BF16).reshape(nctx, rows, grad.shape[1]), "ctx", 0, 0, tiled=True)
    return back.astype(F32)


def sum_rows(partial):
    return lax.psum_scatter(partial.astype(BF16), ("ctx", "tp"), scatter_dimension=0, tiled=True).astype(F32)


def shards(tokens, norm_gain, zx_weight, bc_weight, dt_weight, conv_x, conv_bc, head_params, gate_gain, out_weight, cotangent):
    seq_count, length, model_width = tokens.shape
    assert seq_count == 1
    nctx, ntp, ndp = lax.axis_size("ctx"), lax.axis_size("tp"), lax.axis_size("dp")
    ctx = lax.axis_index("ctx")
    rows = dt_weight.shape[0]
    inner = conv_x.shape[1]
    groups = bc_weight.shape[2] // N
    share = nctx // groups
    assert share == 2 and groups * share == nctx
    width = inner // nctx
    heads = dt_weight.shape[1] // nctx
    taps = conv_x.shape[0] - 1
    group_width = inner // groups

    def mine(value):
        return lax.dynamic_index_in_dim(value, ctx, 0, False)

    def partner(value):
        return lax.ppermute(value, "ctx", [(i, i ^ 1) for i in range(nctx)])

    hidden = tokens.astype(F32).reshape(length, model_width)
    cot = cotangent.reshape(length, model_width)
    rscale = lax.rsqrt(jnp.mean(hidden * hidden, axis=-1, keepdims=True) + EPS)
    normed = (hidden * rscale * norm_gain).astype(BF16)

    zx = zx_weight.reshape(rows, 2, nctx, width)
    bc = jnp.repeat(bc_weight.reshape(rows, 2, groups, N), share, axis=2)
    packed = jnp.concatenate(
        [zx[:, 0], zx[:, 1], bc[:, 0], bc[:, 1], dt_weight.reshape(rows, nctx, heads)], axis=2
    ).transpose(1, 0, 2)
    weight_in = fetch_weight(packed)
    weight_out = fetch_weight(out_weight.reshape(rows, nctx, width).transpose(1, 0, 2))
    normed_all = spread_rows(normed)
    cot_all = spread_rows(cot)

    proj = jnp.dot(normed_all, weight_in, preferred_element_type=F32)
    gate_pre = proj[:, :width]
    conv_width = width + 2 * N
    conv_input = proj[:, width : width + conv_width].astype(BF16)
    raw_dt = proj[:, width + conv_width :]
    padded = jnp.concatenate([jnp.zeros((taps - 1, conv_width), BF16), conv_input], axis=0).astype(F32)
    kernel_x = mine(conv_x.reshape(taps + 1, nctx, width).transpose(1, 0, 2))
    kernel_bc = conv_bc.reshape(taps + 1, 2, groups, N)
    kernel_bc = lax.dynamic_index_in_dim(kernel_bc, ctx // share, 2, False)
    kernel = jnp.concatenate([kernel_x, kernel_bc.reshape(taps + 1, 2 * N)], axis=1)
    conv_out = conv_silu(padded, kernel)
    conv_low = lax.optimization_barrier(conv_out.astype(BF16)).astype(F32)
    heads_mine = mine(head_params.reshape(3, nctx, heads).transpose(1, 0, 2))
    gain = mine(gate_gain.reshape(nctx, width))
    ssd, mixer_back = jax.vjp(mixer, conv_low[:, :width], conv_low[:, width:], raw_dt, heads_mine)

    sig = jax.nn.sigmoid(gate_pre)
    gate = gate_pre * sig
    gated = ssd * gate
    grad_gated = jnp.dot(cot_all, weight_out, preferred_element_type=F32)
    grad_scaled = grad_gated * gain
    sums = jnp.stack([jnp.sum(gated * gated, axis=1), jnp.sum(grad_scaled * gated, axis=1)])
    sums = (sums + partner(sums)) / group_width
    inverse = lax.rsqrt(sums[0] + EPS)[:, None]
    gated_norm = (gated * inverse * gain).astype(BF16)
    branch = sum_rows(dot_last(gated_norm, weight_out))
    part = length // ntp
    hidden_part = lax.dynamic_slice_in_dim(hidden, lax.axis_index("tp") * part, part, 0)
    mixed = lax.all_gather((hidden_part + branch).astype(BF16), "tp", axis=0, tiled=True)
    grad_out = return_grad(dot_first(cot_all, gated_norm), rows)

    gate_gain_grad = jnp.sum(grad_gated * gated * inverse, axis=0)
    grad_pre = inverse * grad_scaled - gated * (inverse * inverse * inverse * sums[1][:, None])
    grad_ssd = grad_pre * gate
    grad_gate = (grad_pre * ssd * (sig * (1.0 + gate_pre * (1.0 - sig)))).astype(BF16)
    grad_x, grad_maps, grad_dt, grad_heads = mixer_back(grad_ssd)

    odd = ctx % 2
    own_maps = lax.dynamic_slice_in_dim(grad_maps, odd * N, N, 1)
    send_maps = lax.dynamic_slice_in_dim(grad_maps, (1 - odd) * N, N, 1)
    own_maps = own_maps + partner(send_maps)
    own_padded = jnp.concatenate([padded[:, :width], lax.dynamic_slice_in_dim(padded, width + odd * N, N, 1)], axis=1)
    own_kernel = jnp.concatenate([kernel[:, :width], lax.dynamic_slice_in_dim(kernel, width + odd * N, N, 1)], axis=1)
    _, conv_back = jax.vjp(conv_silu, own_padded, own_kernel)
    grad_padded, grad_kernel = conv_back(jnp.concatenate([grad_x, own_maps], axis=1))
    grad_input = grad_padded[taps - 1 :].astype(BF16)
    grad_all = jnp.concatenate([grad_gate, grad_input, grad_dt.astype(BF16)], axis=1)
    own_weight = jnp.concatenate(
        [
            weight_in[:, : 2 * width],
            lax.dynamic_slice_in_dim(weight_in, 2 * width + odd * N, N, 1),
            weight_in[:, 2 * width + 2 * N :],
        ],
        axis=1,
    )
    normed_part = sum_rows(dot_last(grad_all, own_weight))
    grad_normed = lax.all_gather(normed_part.astype(BF16), "tp", axis=0, tiled=True).astype(F32)
    grad_in = return_grad(dot_first(normed_all, grad_all), rows)

    grad_hat = grad_normed * norm_gain
    norm_gain_grad = jnp.sum(grad_normed * hidden * rscale, axis=0)
    grad_hidden = rscale * grad_hat - hidden * (rscale * rscale * rscale) * jnp.mean(
        grad_hat * hidden, axis=1, keepdims=True
    )
    tokens_grad = cot.astype(F32) + grad_hidden

    zx_weight_grad = jnp.stack([grad_in[:, :, :width], grad_in[:, :, width : 2 * width]], axis=2)
    zx_weight_grad = zx_weight_grad.transpose(1, 2, 0, 3).reshape(rows, 2, inner)
    bc_weight_grad = grad_in[:, :, 2 * width : 2 * width + N].reshape(groups, 2, rows, N)
    bc_weight_grad = bc_weight_grad.transpose(2, 1, 0, 3).reshape(rows, 2, groups * N)
    dt_weight_grad = grad_in[:, :, 2 * width + N :].transpose(1, 0, 2).reshape(rows, nctx * heads)
    out_weight_grad = grad_out.transpose(1, 0, 2).reshape(rows, inner)

    small = jnp.concatenate([grad_kernel.reshape(-1), grad_heads.reshape(-1), gate_gain_grad])
    table = lax.dynamic_update_slice(jnp.zeros((nctx, small.shape[0]), F32), small[None], (ctx, 0))
    table, norm_gain_grad = lax.psum((table, norm_gain_grad), ("dp", "ctx"))
    kernel_end = (taps + 1) * (width + N)
    heads_end = kernel_end + 3 * heads
    kernels = table[:, :kernel_end].reshape(nctx, taps + 1, width + N)
    conv_x_grad = kernels[:, :, :width].transpose(1, 0, 2).reshape(taps + 1, inner)
    conv_bc_grad = kernels[:, :, width:].reshape(groups, 2, taps + 1, N).transpose(2, 1, 0, 3)
    conv_bc_grad = conv_bc_grad.reshape(taps + 1, 2, groups * N)
    head_grad = table[:, kernel_end:heads_end].reshape(nctx, 3, heads).transpose(1, 0, 2).reshape(3, nctx * heads)
    gate_gain_grad = table[:, heads_end:].reshape(inner)
    return (
        mixed.reshape(tokens.shape),
        tokens_grad.reshape(tokens.shape),
        norm_gain_grad,
        zx_weight_grad,
        bc_weight_grad,
        dt_weight_grad,
        conv_x_grad,
        conv_bc_grad,
        head_grad,
        gate_gain_grad,
        out_weight_grad,
    )


def solution(mesh):
    wide = P(("dp", "ctx"), None, "tp")
    flat = P(("dp", "ctx"), "tp")
    rows = P("dp", "ctx", None)
    return jax.shard_map(
        shards,
        mesh=mesh,
        in_specs=(rows, P(), wide, wide, flat, P(None, "tp"), P(None, None, "tp"), P(None, "tp"), P("tp"), flat, rows),
        out_specs=(rows, rows, P(), wide, wide, flat, P(None, "tp"), P(None, None, "tp"), P(None, "tp"), P("tp"), flat),
        check_vma=False,
    )
```

```python
import functools

import jax
import jax.numpy as jnp
from jax import lax
from jax.experimental import pallas as pl
from jax.experimental.pallas import tpu as pltpu
from jax.sharding import PartitionSpec as P

P_SIZE = 64
N = 128
BLOCK = 256
EDGE = 8
EPS = 1e-05
HIGH = lax.Precision.HIGHEST
F32 = jnp.float32
BF16 = jnp.bfloat16


def dot_on(left_side, right_side, left_dim, right_dim, precision=None):
    return lax.dot_general(
        left_side, right_side, (((left_dim,), (right_dim,)), ((), ())), precision=precision, preferred_element_type=F32
    )


def split(v):
    high = v.astype(BF16)
    return high, (v - high.astype(F32)).astype(BF16)


def dot_two(parts, other, part_dim, other_dim):
    return dot_on(parts[0], other, part_dim, other_dim) + dot_on(parts[1], other, part_dim, other_dim)


def dot_three(left_side, right_side, left_dim, right_dim):
    high = dot_two(left_side, right_side[0], left_dim, right_dim)
    return high + dot_on(left_side[0], right_side[1], left_dim, right_dim)


def softplus(v):
    return jnp.maximum(v, 0.0) + jnp.log1p(jnp.exp(-jnp.abs(v)))


def sigmoid(v):
    return 1.0 / (1.0 + jnp.exp(-v))


def order_mask(transposed):
    row = lax.broadcasted_iota(jnp.int32, (BLOCK, BLOCK), 0)
    col = lax.broadcasted_iota(jnp.int32, (BLOCK, BLOCK), 1)
    return row <= col if transposed else row >= col


def first_half(rows):
    return lax.broadcasted_iota(jnp.int32, (rows, 2 * P_SIZE), 1) < P_SIZE


def over_pair(value, pair):
    shape = (value.shape[0], P_SIZE * 2)
    left = jnp.broadcast_to(value[:, 2 * pair : 2 * pair + 1], shape)
    right = jnp.broadcast_to(value[:, 2 * pair + 1 : 2 * pair + 2], shape)
    return jnp.where(first_half(shape[0]), left, right)


def over_heads(value):
    return jnp.concatenate([over_pair(value, pair) for pair in range(value.shape[1] // 2)], axis=1)


def head_sums(value):
    columns = []
    for pair in range(value.shape[1] // (2 * P_SIZE)):
        part = value[:, pair * 2 * P_SIZE : (pair + 1) * 2 * P_SIZE]
        left = jnp.where(first_half(part.shape[0]), part, 0.0)
        columns += [jnp.sum(left, axis=1, keepdims=True), jnp.sum(part - left, axis=1, keepdims=True)]
    heads = len(columns)
    lane = lax.broadcasted_iota(jnp.int32, (value.shape[0], heads), 1)
    total = jnp.broadcast_to(columns[0], lane.shape)
    for head in range(1, heads):
        total = jnp.where(lane == head, columns[head], total)
    return total


def convolve(buffer, kernel_ref, start, width):
    taps = kernel_ref.shape[0] - 1
    total = kernel_ref[taps : taps + 1, start : start + width]
    for tap in range(taps):
        low = EDGE - taps + 1 + tap
        total = total + kernel_ref[tap : tap + 1, start : start + width] * buffer[low : low + BLOCK, start : start + width]
    return total


def block_steps(raw_ref, head_ref):
    dt = softplus(raw_ref[...] + head_ref[0:1, :])
    decay = -jnp.exp(head_ref[1:2, :])
    log_step = dt * decay
    lower = order_mask(False).astype(F32)
    total = dot_on(lower, log_step, 1, 0, HIGH)
    total_t = dot_on(log_step, lower, 0, 1, HIGH)
    return dt, decay, total, total_t


def forward_body(conv_ref, raw_ref, gate_ref, up_ref, kernel_ref, head_ref, gain_ref, low_ref, ssd_ref, state_ref, sums_ref, state, buffer):
    width = gate_ref.shape[1]
    first = pl.program_id(0) == 0

    @pl.when(first)
    def _():
        state[...] = jnp.zeros_like(state)
        buffer[0:EDGE, :] = jnp.zeros((EDGE, buffer.shape[1]), F32)

    @pl.when(jnp.logical_not(first))
    def _():
        buffer[0:EDGE, :] = buffer[BLOCK : BLOCK + EDGE, :]

    buffer[EDGE : EDGE + BLOCK, :] = conv_ref[...].astype(F32)
    before = convolve(buffer, kernel_ref, 0, buffer.shape[1])
    low_ref[...] = (before * sigmoid(before)).astype(BF16)
    dt, _, total, total_t = block_steps(raw_ref, head_ref)
    state_ref[0] = state[...]
    inject = low_ref[:, width : width + N]
    readout = low_ref[:, width + N : width + 2 * N]
    scores = dot_on(readout, inject, 1, 1)
    mask = order_mask(False)
    half = first_half(BLOCK)
    skip = over_heads(head_ref[2:3, :])
    squares = []
    for pair in range(width // (2 * P_SIZE)):
        cols = slice(pair * 2 * P_SIZE, (pair + 1) * 2 * P_SIZE)
        x = low_ref[:, cols].astype(F32)
        total_p = over_pair(total, pair)
        scaled = x * over_pair(dt, pair)
        scaled_two = split(scaled)
        local = []
        for head in (2 * pair, 2 * pair + 1):
            gap = total[:, head : head + 1] - total_t[head : head + 1, :]
            mixing = jnp.exp(jnp.where(mask, gap, -1e30)) * scores
            local.append(dot_three(split(mixing), scaled_two, 1, 0))
        held = state[:, cols]
        held_two = split(held)
        carried = jnp.exp(total_p) * (dot_on(readout, held_two[0], 1, 0) + dot_on(readout, held_two[1], 1, 0))
        ssd = jnp.where(half, local[0], local[1]) + carried + skip[:, cols] * x
        ssd_ref[:, cols] = ssd
        moved = split(scaled * jnp.exp(total_p[BLOCK - 1 : BLOCK, :] - total_p))
        state[:, cols] = held * jnp.exp(total_p[BLOCK - 1 : BLOCK, :]) + (
            dot_on(inject, moved[0], 0, 0) + dot_on(inject, moved[1], 0, 0)
        )
        gate_pre = gate_ref[:, cols]
        gated = ssd * (gate_pre * sigmoid(gate_pre))
        squares.append((gated * gated, gated * (up_ref[:, cols] * gain_ref[0:1, cols])))
    ones = jnp.ones((8, 2 * P_SIZE), F32)
    square = functools.reduce(jnp.add, [s[0] for s in squares])
    cross = functools.reduce(jnp.add, [s[1] for s in squares])
    sums_ref[0:1, :] = dot_on(ones, square, 1, 1, HIGH)[0:1, :]
    sums_ref[1:2, :] = dot_on(ones, cross, 1, 1, HIGH)[0:1, :]


def mixer_forward(conv_input, raw_dt, gate_pre, grad_gated, kernel, heads, gain):
    length, width = gate_pre.shape
    wide = conv_input.shape[1]
    count = length // BLOCK
    rows = lambda i: (i, 0)
    whole = lambda i: (0, 0)
    return pl.pallas_call(
        forward_body,
        grid=(count,),
        in_specs=[
            pl.BlockSpec((BLOCK, wide), rows),
            pl.BlockSpec((BLOCK, raw_dt.shape[1]), rows),
            pl.BlockSpec((BLOCK, width), rows),
            pl.BlockSpec((BLOCK, width), rows),
            pl.BlockSpec(kernel.shape, whole),
            pl.BlockSpec(heads.shape, whole),
            pl.BlockSpec(gain.shape, whole),
        ],
        out_specs=[
            pl.BlockSpec((BLOCK, wide), rows),
            pl.BlockSpec((BLOCK, width), rows),
            pl.BlockSpec((1, N, width), lambda i: (i, 0, 0)),
            pl.BlockSpec((2, BLOCK), lambda i: (0, i)),
        ],
        out_shape=[
            jax.ShapeDtypeStruct((length, wide), BF16),
            jax.ShapeDtypeStruct((length, width), F32),
            jax.ShapeDtypeStruct((count, N, width), F32),
            jax.ShapeDtypeStruct((2, length), F32),
        ],
        scratch_shapes=[pltpu.VMEM((N, width), F32), pltpu.VMEM((BLOCK + EDGE, wide), F32)],
        compiler_params=pltpu.CompilerParams(vmem_limit_bytes=48 << 20),
        name="mixer_forward",
    )(conv_input, raw_dt, gate_pre, grad_gated, kernel, heads, gain)


def backward_body(
    conv_ref, edge_ref, low_ref, raw_ref, gate_ref, up_ref, ssd_ref, state_ref, norm_ref, kernel_ref, head_ref, gain_ref,
    grad_gate_ref, grad_in_ref, grad_maps_ref, grad_dt_ref, grad_kernel_ref, grad_head_ref, grad_gain_ref,
    adjoint, buffer, grads, next_state,
):
    width = gate_ref.shape[1]
    taps = kernel_ref.shape[0] - 1
    count = pl.num_programs(0)
    step = pl.program_id(0)

    @pl.when(step == 0)
    def _():
        adjoint[...] = jnp.zeros_like(adjoint)
        next_state[...] = jnp.zeros_like(next_state)
        grads[BLOCK : BLOCK + EDGE, :] = jnp.zeros((EDGE, width), F32)
        grad_kernel_ref[...] = jnp.zeros_like(grad_kernel_ref)
        grad_head_ref[...] = jnp.zeros_like(grad_head_ref)
        grad_gain_ref[...] = jnp.zeros_like(grad_gain_ref)

    @pl.when(step > 0)
    def _():
        grads[BLOCK : BLOCK + EDGE, :] = grads[0:EDGE, :]

    edge = edge_ref[edge_ref.shape[0] - EDGE :, 0:width].astype(F32)
    buffer[0:EDGE, :] = jnp.where(step == count - 1, 0.0, edge)
    buffer[EDGE : EDGE + BLOCK, :] = conv_ref[:, 0:width].astype(F32)
    dt, decay, total, total_t = block_steps(raw_ref, head_ref)
    inject = low_ref[:, width : width + N]
    readout = low_ref[:, width + N : width + 2 * N]
    scores_t = dot_on(inject, readout, 1, 1)
    mask_t = order_mask(True)
    half = first_half(BLOCK)
    skip = over_heads(head_ref[2:3, :])
    inverse = norm_ref[:, 0:1]
    pull = norm_ref[:, 1:2]
    grad_scores_t = jnp.zeros((BLOCK, BLOCK), F32)
    grad_inject = jnp.zeros((BLOCK, N), F32)
    grad_readout = jnp.zeros((BLOCK, N), F32)
    decay_parts, step_parts, skip_parts, end_parts = [], [], [], []
    for pair in range(width // (2 * P_SIZE)):
        cols = slice(pair * 2 * P_SIZE, (pair + 1) * 2 * P_SIZE)
        x = low_ref[:, cols].astype(F32)
        gate_pre = gate_ref[:, cols]
        ssd = ssd_ref[:, cols]
        sig = sigmoid(gate_pre)
        gate = gate_pre * sig
        up = up_ref[:, cols]
        gated = ssd * gate
        grad_gain_ref[0:1, cols] += jnp.sum(up * gated * inverse, axis=0, keepdims=True)
        grad_pre = inverse * (up * gain_ref[0:1, cols]) - gated * pull
        grad_gate_ref[:, cols] = (grad_pre * ssd * (sig * (1.0 + gate_pre * (1.0 - sig)))).astype(BF16)
        grad_ssd = grad_pre * gate
        grad_two = split(grad_ssd)
        total_p = over_pair(total, pair)
        dt_p = over_pair(dt, pair)
        to_end = jnp.exp(total_p[BLOCK - 1 : BLOCK, :] - total_p)
        scaled = x * dt_p
        scaled_two = split(scaled)
        local = []
        for index, head in enumerate((2 * pair, 2 * pair + 1)):
            gap = total_t[head : head + 1, :] - total[:, head : head + 1]
            decays = jnp.exp(jnp.where(mask_t, gap, -1e30))
            own = half if index == 0 else jnp.logical_not(half)
            mine = [jnp.where(own, part, jnp.zeros_like(part)) for part in grad_two]
            grad_scores_t += decays * dot_three(scaled_two, mine, 1, 1)
            local.append(dot_three(split(decays * scores_t), grad_two, 1, 0))
        local = jnp.where(half, local[0], local[1])
        lam = adjoint[:, cols]
        lam_two = split(lam)
        held = state_ref[0, :, cols]
        far = dot_on(inject, lam_two[0], 1, 0) + dot_on(inject, lam_two[1], 1, 0)
        moved = scaled * to_end
        grad_inject += dot_three(split(moved), lam_two, 1, 1)
        rising = split(grad_ssd * jnp.exp(total_p))
        grad_readout += dot_three(rising, split(held), 1, 1)
        end_parts.append(jnp.sum(lam * next_state[:, cols], axis=0, keepdims=True))
        adjoint[:, cols] = lam * jnp.exp(total_p[BLOCK - 1 : BLOCK, :]) + (
            dot_on(readout, rising[0], 0, 0) + dot_on(readout, rising[1], 0, 0)
        )
        next_state[:, cols] = held
        pure = ssd - skip[:, cols] * x
        decay_parts.append(grad_ssd * pure - scaled * local - moved * far)
        grad_scaled = local + to_end * far
        step_parts.append(x * grad_scaled)
        skip_parts.append(jnp.sum(grad_ssd * x, axis=0, keepdims=True))
        grad_x = dt_p * grad_scaled + skip[:, cols] * grad_ssd
        before = convolve(buffer, kernel_ref, pair * 2 * P_SIZE, 2 * P_SIZE)
        sig = sigmoid(before)
        grads[0:BLOCK, cols] = grad_x * (sig * (1.0 + before * (1.0 - sig)))
    row_grads = head_sums(jnp.concatenate(decay_parts, axis=1))
    upper = order_mask(True).astype(F32)
    ends = head_sums(jnp.concatenate(end_parts, axis=1))
    grad_log = dot_on(upper, row_grads, 1, 0, HIGH) + ends
    grad_dt = head_sums(jnp.concatenate(step_parts, axis=1)) + decay * grad_log
    grad_raw = grad_dt * sigmoid(raw_ref[...] + head_ref[0:1, :])
    grad_dt_ref[...] = grad_raw
    grad_head_ref[0:1, :] += jnp.sum(grad_raw, axis=0, keepdims=True)
    grad_head_ref[1:2, :] += decay * jnp.sum(dt * grad_log, axis=0, keepdims=True)
    grad_head_ref[2:3, :] += head_sums(jnp.concatenate(skip_parts, axis=1))
    scores_two = split(grad_scores_t)
    grad_maps_ref[:, 0:N] = grad_inject + dot_two(scores_two, readout, 1, 0)
    grad_maps_ref[:, N : 2 * N] = grad_readout + dot_two(scores_two, inject, 0, 0)
    here = grads[0:BLOCK, :]
    grad_kernel_ref[taps : taps + 1, :] += jnp.sum(here, axis=0, keepdims=True)
    total_in = jnp.zeros((BLOCK, width), F32)
    for tap in range(taps):
        low = EDGE - taps + 1 + tap
        grad_kernel_ref[tap : tap + 1, :] += jnp.sum(here * buffer[low : low + BLOCK, :], axis=0, keepdims=True)
        ahead = taps - 1 - tap
        total_in = total_in + kernel_ref[tap : tap + 1, 0:width] * grads[ahead : ahead + BLOCK, :]
    grad_in_ref[...] = total_in.astype(BF16)


def mixer_backward(conv_input, low, raw_dt, gate_pre, grad_gated, ssd, states, norms, kernel, heads, gain):
    length, width = gate_pre.shape
    wide = conv_input.shape[1]
    count = length // BLOCK
    edge = 16
    back = lambda i: (count - 1 - i, 0)
    whole = lambda i: (0, 0)
    return pl.pallas_call(
        backward_body,
        grid=(count,),
        in_specs=[
            pl.BlockSpec((BLOCK, wide), back),
            pl.BlockSpec((edge, wide), lambda i: (jnp.maximum((count - 1 - i) * (BLOCK // edge) - 1, 0), 0)),
            pl.BlockSpec((BLOCK, wide), back),
            pl.BlockSpec((BLOCK, raw_dt.shape[1]), back),
            pl.BlockSpec((BLOCK, width), back),
            pl.BlockSpec((BLOCK, width), back),
            pl.BlockSpec((BLOCK, width), back),
            pl.BlockSpec((1, N, width), lambda i: (count - 1 - i, 0, 0)),
            pl.BlockSpec((BLOCK, norms.shape[1]), back),
            pl.BlockSpec(kernel.shape, whole),
            pl.BlockSpec(heads.shape, whole),
            pl.BlockSpec(gain.shape, whole),
        ],
        out_specs=[
            pl.BlockSpec((BLOCK, width), back),
            pl.BlockSpec((BLOCK, width), back),
            pl.BlockSpec((BLOCK, 2 * N), back),
            pl.BlockSpec((BLOCK, raw_dt.shape[1]), back),
            pl.BlockSpec((kernel.shape[0], width), whole),
            pl.BlockSpec(heads.shape, whole),
            pl.BlockSpec(gain.shape, whole),
        ],
        out_shape=[
            jax.ShapeDtypeStruct((length, width), BF16),
            jax.ShapeDtypeStruct((length, width), BF16),
            jax.ShapeDtypeStruct((length, 2 * N), F32),
            jax.ShapeDtypeStruct(raw_dt.shape, F32),
            jax.ShapeDtypeStruct((kernel.shape[0], width), F32),
            jax.ShapeDtypeStruct(heads.shape, F32),
            jax.ShapeDtypeStruct(gain.shape, F32),
        ],
        scratch_shapes=[
            pltpu.VMEM((N, width), F32),
            pltpu.VMEM((BLOCK + EDGE, width), F32),
            pltpu.VMEM((BLOCK + EDGE, width), F32),
            pltpu.VMEM((N, width), F32),
        ],
        compiler_params=pltpu.CompilerParams(vmem_limit_bytes=56 << 20),
        name="mixer_backward",
    )(conv_input, conv_input, low, raw_dt, gate_pre, grad_gated, ssd, states, norms, kernel, heads, gain)


def dot_last(left_side, right_side):
    return lax.dot_general(left_side, right_side, (((1,), (1,)), ((), ())), preferred_element_type=F32)


def dot_first(left_side, right_side):
    return lax.dot_general(left_side, right_side, (((0,), (0,)), ((), ())), preferred_element_type=F32)


def conv_silu(padded, kernel):
    tap_count = kernel.shape[0] - 1
    length = padded.shape[0] - tap_count + 1
    running = kernel[tap_count] + kernel[0] * padded[0:length]
    for offset in range(1, tap_count):
        running = running + kernel[offset] * padded[offset : offset + length]
    return jax.nn.silu(running)


def spread_rows(value):
    part = value.shape[0] // lax.axis_size("tp")
    mine = lax.dynamic_slice_in_dim(value, lax.axis_index("tp") * part, part, 0)
    along = lax.all_gather(mine, "ctx", axis=0)
    return lax.all_gather(along, "tp", axis=1).reshape(-1, value.shape[1])


def fetch_weight(packed):
    mine = lax.all_to_all(packed, "ctx", 0, 0, tiled=True)
    return lax.all_gather(mine.reshape(-1, packed.shape[2]), "dp", axis=0, tiled=True)


def return_grad(grad, rows):
    ndp, nctx = lax.axis_size("dp"), lax.axis_size("ctx")
    parts = grad.astype(BF16).reshape(ndp, nctx * rows, grad.shape[1])
    summed = jnp.sum(lax.all_to_all(parts, "dp", 0, 0, tiled=True).astype(F32), axis=0)
    back = lax.all_to_all(summed.astype(BF16).reshape(nctx, rows, grad.shape[1]), "ctx", 0, 0, tiled=True)
    return back.astype(F32)


def sum_rows(partial):
    return lax.psum_scatter(partial.astype(BF16), ("ctx", "tp"), scatter_dimension=0, tiled=True).astype(F32)


def shards(tokens, norm_gain, zx_weight, bc_weight, dt_weight, conv_x, conv_bc, head_params, gate_gain, out_weight, cotangent):
    seq_count, length, model_width = tokens.shape
    assert seq_count == 1
    nctx, ntp, ndp = lax.axis_size("ctx"), lax.axis_size("tp"), lax.axis_size("dp")
    ctx = lax.axis_index("ctx")
    rows = dt_weight.shape[0]
    inner = conv_x.shape[1]
    groups = bc_weight.shape[2] // N
    share = nctx // groups
    assert share == 2 and groups * share == nctx
    width = inner // nctx
    heads = dt_weight.shape[1] // nctx
    taps = conv_x.shape[0] - 1
    group_width = inner // groups

    def mine(value):
        return lax.dynamic_index_in_dim(value, ctx, 0, False)

    def partner(value):
        return lax.ppermute(value, "ctx", [(i, i ^ 1) for i in range(nctx)])

    hidden = tokens.astype(F32).reshape(length, model_width)
    cot = cotangent.reshape(length, model_width)
    rscale = lax.rsqrt(jnp.mean(hidden * hidden, axis=-1, keepdims=True) + EPS)
    normed = (hidden * rscale * norm_gain).astype(BF16)

    zx = zx_weight.reshape(rows, 2, nctx, width)
    bc = jnp.repeat(bc_weight.reshape(rows, 2, groups, N), share, axis=2)
    packed = jnp.concatenate(
        [zx[:, 0], zx[:, 1], bc[:, 0], bc[:, 1], dt_weight.reshape(rows, nctx, heads)], axis=2
    ).transpose(1, 0, 2)
    weight_in = fetch_weight(packed)
    weight_out = fetch_weight(out_weight.reshape(rows, nctx, width).transpose(1, 0, 2))
    normed_all = spread_rows(normed)
    cot_all = spread_rows(cot)

    conv_width = width + 2 * N
    grad_gated = jnp.dot(cot_all, weight_out, preferred_element_type=F32)
    gate_pre = jnp.dot(normed_all, weight_in[:, :width], preferred_element_type=F32)
    conv_input = jnp.dot(normed_all, weight_in[:, width : width + conv_width], preferred_element_type=F32).astype(BF16)
    raw_dt = jnp.dot(normed_all, weight_in[:, width + conv_width :], preferred_element_type=F32)
    kernel_x = mine(conv_x.reshape(taps + 1, nctx, width).transpose(1, 0, 2))
    kernel_bc = conv_bc.reshape(taps + 1, 2, groups, N)
    kernel_bc = lax.dynamic_index_in_dim(kernel_bc, ctx // share, 2, False)
    kernel = jnp.concatenate([kernel_x, kernel_bc.reshape(taps + 1, 2 * N)], axis=1)
    heads_mine = mine(head_params.reshape(3, nctx, heads).transpose(1, 0, 2))
    gain = mine(gate_gain.reshape(nctx, 1, width))
    low, ssd, states, sums = mixer_forward(conv_input, raw_dt, gate_pre, grad_gated, kernel, heads_mine, gain)
    sums = (sums + partner(sums)) / group_width
    inverse = lax.rsqrt(sums[0] + EPS)
    norms = jnp.stack([inverse, inverse * inverse * inverse * sums[1]], axis=1)
    gated_norm = (ssd * (gate_pre * jax.nn.sigmoid(gate_pre)) * norms[:, 0:1] * gain).astype(BF16)
    branch = sum_rows(dot_last(gated_norm, weight_out))
    part = length // ntp
    hidden_part = lax.dynamic_slice_in_dim(hidden, lax.axis_index("tp") * part, part, 0)
    mixed = lax.all_gather((hidden_part + branch).astype(BF16), "tp", axis=0, tiled=True)
    grad_out = return_grad(dot_first(cot_all, gated_norm), rows)
    grad_gate, grad_x, grad_maps, grad_dt, grad_kernel_x, grad_heads, gate_gain_grad = mixer_backward(
        conv_input, low, raw_dt, gate_pre, grad_gated, ssd, states, norms, kernel, heads_mine, gain
    )

    odd = ctx % 2
    own_maps = lax.dynamic_slice_in_dim(grad_maps, odd * N, N, 1)
    send_maps = lax.dynamic_slice_in_dim(grad_maps, (1 - odd) * N, N, 1)
    own_maps = own_maps + partner(send_maps)
    own_input = lax.dynamic_slice_in_dim(conv_input, width + odd * N, N, 1)
    own_padded = jnp.concatenate([jnp.zeros((taps - 1, N), BF16), own_input], axis=0).astype(F32)
    own_kernel = lax.dynamic_slice_in_dim(kernel, width + odd * N, N, 1)
    _, conv_back = jax.vjp(conv_silu, own_padded, own_kernel)
    grad_padded, grad_kernel_bc = conv_back(own_maps)
    grad_kernel = jnp.concatenate([grad_kernel_x, grad_kernel_bc], axis=1)
    grad_bc = grad_padded[taps - 1 :].astype(BF16)
    grad_all = jnp.concatenate([grad_gate, grad_x, grad_bc, grad_dt.astype(BF16)], axis=1)
    own_weight = jnp.concatenate(
        [
            weight_in[:, : 2 * width],
            lax.dynamic_slice_in_dim(weight_in, 2 * width + odd * N, N, 1),
            weight_in[:, 2 * width + 2 * N :],
        ],
        axis=1,
    )
    normed_part = sum_rows(dot_last(grad_all, own_weight))
    grad_normed = lax.all_gather(normed_part.astype(BF16), "tp", axis=0, tiled=True).astype(F32)
    grad_in = return_grad(dot_first(normed_all, grad_all), rows)

    grad_hat = grad_normed * norm_gain
    norm_gain_grad = jnp.sum(grad_normed * hidden * rscale, axis=0)
    grad_hidden = rscale * grad_hat - hidden * (rscale * rscale * rscale) * jnp.mean(
        grad_hat * hidden, axis=1, keepdims=True
    )
    tokens_grad = cot.astype(F32) + grad_hidden

    zx_weight_grad = jnp.stack([grad_in[:, :, :width], grad_in[:, :, width : 2 * width]], axis=2)
    zx_weight_grad = zx_weight_grad.transpose(1, 2, 0, 3).reshape(rows, 2, inner)
    bc_weight_grad = grad_in[:, :, 2 * width : 2 * width + N].reshape(groups, 2, rows, N)
    bc_weight_grad = bc_weight_grad.transpose(2, 1, 0, 3).reshape(rows, 2, groups * N)
    dt_weight_grad = grad_in[:, :, 2 * width + N :].transpose(1, 0, 2).reshape(rows, nctx * heads)
    out_weight_grad = grad_out.transpose(1, 0, 2).reshape(rows, inner)

    small = jnp.concatenate([grad_kernel.reshape(-1), grad_heads.reshape(-1), gate_gain_grad.reshape(-1)])
    table = lax.dynamic_update_slice(jnp.zeros((nctx, small.shape[0]), F32), small[None], (ctx, 0))
    table, norm_gain_grad = lax.psum((table, norm_gain_grad), ("dp", "ctx"))
    kernel_end = (taps + 1) * (width + N)
    heads_end = kernel_end + 3 * heads
    kernels = table[:, :kernel_end].reshape(nctx, taps + 1, width + N)
    conv_x_grad = kernels[:, :, :width].transpose(1, 0, 2).reshape(taps + 1, inner)
    conv_bc_grad = kernels[:, :, width:].reshape(groups, 2, taps + 1, N).transpose(2, 1, 0, 3)
    conv_bc_grad = conv_bc_grad.reshape(taps + 1, 2, groups * N)
    head_grad = table[:, kernel_end:heads_end].reshape(nctx, 3, heads).transpose(1, 0, 2).reshape(3, nctx * heads)
    gate_gain_grad = table[:, heads_end:].reshape(inner)
    return (
        mixed.reshape(tokens.shape),
        tokens_grad.reshape(tokens.shape),
        norm_gain_grad,
        zx_weight_grad,
        bc_weight_grad,
        dt_weight_grad,
        conv_x_grad,
        conv_bc_grad,
        head_grad,
        gate_gain_grad,
        out_weight_grad,
    )


def solution(mesh):
    wide = P(("dp", "ctx"), None, "tp")
    flat = P(("dp", "ctx"), "tp")
    rows = P("dp", "ctx", None)
    return jax.shard_map(
        shards,
        mesh=mesh,
        in_specs=(rows, P(), wide, wide, flat, P(None, "tp"), P(None, None, "tp"), P(None, "tp"), P("tp"), flat, rows),
        out_specs=(rows, rows, P(), wide, wide, flat, P(None, "tp"), P(None, None, "tp"), P(None, "tp"), P("tp"), flat),
        check_vma=False,
    )
```

```python
import functools

import jax
import jax.numpy as jnp
from jax import lax
from jax.experimental import pallas as pl
from jax.experimental.pallas import tpu as pltpu
from jax.sharding import PartitionSpec as P

P_SIZE = 64
N = 128
BLOCK = 256
EDGE = 8
DEPTH = 3
MESH = pl.DeviceIdType.MESH
EPS = 1e-05
HIGH = lax.Precision.HIGHEST
F32 = jnp.float32
BF16 = jnp.bfloat16


def dot_on(left_side, right_side, left_dim, right_dim, precision=None):
    return lax.dot_general(
        left_side, right_side, (((left_dim,), (right_dim,)), ((), ())), precision=precision, preferred_element_type=F32
    )


def split(v):
    high = v.astype(BF16)
    return high, (v - high.astype(F32)).astype(BF16)


def dot_two(parts, other, part_dim, other_dim):
    return dot_on(parts[0], other, part_dim, other_dim) + dot_on(parts[1], other, part_dim, other_dim)


def dot_three(left_side, right_side, left_dim, right_dim):
    high = dot_two(left_side, right_side[0], left_dim, right_dim)
    return high + dot_on(left_side[0], right_side[1], left_dim, right_dim)


def softplus(v):
    return jnp.maximum(v, 0.0) + jnp.log1p(jnp.exp(-jnp.abs(v)))


def sigmoid(v):
    return 1.0 / (1.0 + jnp.exp(-v))


def order_mask(transposed):
    row = lax.broadcasted_iota(jnp.int32, (BLOCK, BLOCK), 0)
    col = lax.broadcasted_iota(jnp.int32, (BLOCK, BLOCK), 1)
    return row <= col if transposed else row >= col


def first_half(rows):
    return lax.broadcasted_iota(jnp.int32, (rows, 2 * P_SIZE), 1) < P_SIZE


def over_pair(value, pair):
    shape = (value.shape[0], P_SIZE * 2)
    left = jnp.broadcast_to(value[:, 2 * pair : 2 * pair + 1], shape)
    right = jnp.broadcast_to(value[:, 2 * pair + 1 : 2 * pair + 2], shape)
    return jnp.where(first_half(shape[0]), left, right)


def over_heads(value):
    return jnp.concatenate([over_pair(value, pair) for pair in range(value.shape[1] // 2)], axis=1)


def head_sums(value):
    columns = []
    for pair in range(value.shape[1] // (2 * P_SIZE)):
        part = value[:, pair * 2 * P_SIZE : (pair + 1) * 2 * P_SIZE]
        left = jnp.where(first_half(part.shape[0]), part, 0.0)
        columns += [jnp.sum(left, axis=1, keepdims=True), jnp.sum(part - left, axis=1, keepdims=True)]
    heads = len(columns)
    lane = lax.broadcasted_iota(jnp.int32, (value.shape[0], heads), 1)
    total = jnp.broadcast_to(columns[0], lane.shape)
    for head in range(1, heads):
        total = jnp.where(lane == head, columns[head], total)
    return total


def convolve(buffer, kernel_ref, start, width):
    taps = kernel_ref.shape[0] - 1
    total = kernel_ref[taps : taps + 1, start : start + width]
    for tap in range(taps):
        low = EDGE - taps + 1 + tap
        total = total + kernel_ref[tap : tap + 1, start : start + width] * buffer[low : low + BLOCK, start : start + width]
    return total


def block_steps(raw, head_ref):
    dt = softplus(raw + head_ref[0:1, :])
    decay = -jnp.exp(head_ref[1:2, :])
    log_step = dt * decay
    lower = order_mask(False).astype(F32)
    total = dot_on(lower, log_step, 1, 0, HIGH)
    total_t = dot_on(log_step, lower, 0, 1, HIGH)
    return dt, decay, total, total_t


def forward_body(
    odd_ref, gate_ref, x_ref, own_ref, step_ref, other_ref, up_ref, kernel_ref, head_ref, gain_ref,
    low_ref, ssd_ref, state_ref, sums_ref, state, buffer,
):
    width = gate_ref.shape[1]
    raw = step_ref[:, 0 : head_ref.shape[1]]
    first = pl.program_id(0) == 0

    @pl.when(first)
    def _():
        state[...] = jnp.zeros_like(state)
        buffer[0:EDGE, :] = jnp.zeros((EDGE, buffer.shape[1]), F32)

    @pl.when(jnp.logical_not(first))
    def _():
        buffer[0:EDGE, :] = buffer[BLOCK : BLOCK + EDGE, :]

    buffer[EDGE : EDGE + BLOCK, 0:width] = x_ref[...].astype(BF16).astype(F32)
    buffer[EDGE : EDGE + BLOCK, width : width + N] = own_ref[...].astype(BF16).astype(F32)
    buffer[EDGE : EDGE + BLOCK, width + N :] = other_ref[...].astype(BF16).astype(F32)
    before = convolve(buffer, kernel_ref, 0, buffer.shape[1])
    low_ref[...] = (before * sigmoid(before)).astype(BF16)
    dt, _, total, total_t = block_steps(raw, head_ref)
    state_ref[0] = state[...]
    odd = odd_ref[0, 0] == 1
    own, other = low_ref[:, width : width + N], low_ref[:, width + N : width + 2 * N]
    inject, readout = jnp.where(odd, other, own), jnp.where(odd, own, other)
    scores = dot_on(readout, inject, 1, 1)
    mask = order_mask(False)
    half = first_half(BLOCK)
    skip = over_heads(head_ref[2:3, :])
    squares = []
    for pair in range(width // (2 * P_SIZE)):
        cols = slice(pair * 2 * P_SIZE, (pair + 1) * 2 * P_SIZE)
        x = low_ref[:, cols].astype(F32)
        total_p = over_pair(total, pair)
        scaled = x * over_pair(dt, pair)
        scaled_two = split(scaled)
        local = []
        for head in (2 * pair, 2 * pair + 1):
            gap = total[:, head : head + 1] - total_t[head : head + 1, :]
            mixing = jnp.exp(jnp.where(mask, gap, -1e30)) * scores
            local.append(dot_three(split(mixing), scaled_two, 1, 0))
        held = state[:, cols]
        held_two = split(held)
        carried = jnp.exp(total_p) * (dot_on(readout, held_two[0], 1, 0) + dot_on(readout, held_two[1], 1, 0))
        ssd = jnp.where(half, local[0], local[1]) + carried + skip[:, cols] * x
        ssd_ref[:, cols] = ssd
        moved = split(scaled * jnp.exp(total_p[BLOCK - 1 : BLOCK, :] - total_p))
        state[:, cols] = held * jnp.exp(total_p[BLOCK - 1 : BLOCK, :]) + (
            dot_on(inject, moved[0], 0, 0) + dot_on(inject, moved[1], 0, 0)
        )
        gate_pre = gate_ref[:, cols]
        gated = ssd * (gate_pre * sigmoid(gate_pre))
        squares.append((gated * gated, gated * (up_ref[:, cols] * gain_ref[0:1, cols])))
    ones = jnp.ones((8, 2 * P_SIZE), F32)
    square = functools.reduce(jnp.add, [s[0] for s in squares])
    cross = functools.reduce(jnp.add, [s[1] for s in squares])
    sums_ref[0:1, :] = dot_on(ones, square, 1, 1, HIGH)[0:1, :]
    sums_ref[1:2, :] = dot_on(ones, cross, 1, 1, HIGH)[0:1, :]


def proj_specs(width, index):
    narrow = lambda place: pl.BlockSpec((BLOCK, N), lambda i: (index(i), 2 * width // N + place))
    return [
        pl.BlockSpec(memory_space=pltpu.SMEM),
        pl.BlockSpec((BLOCK, width), lambda i: (index(i), 0)),
        pl.BlockSpec((BLOCK, width), lambda i: (index(i), 1)),
        narrow(0),
        narrow(1),
        narrow(2),
    ]


def mixer_forward(odd, proj, grad_gated, kernel, heads, gain):
    length, width = grad_gated.shape
    wide = width + 2 * N
    count = length // BLOCK
    rows = lambda i: (i, 0)
    whole = lambda i: (0, 0)
    return pl.pallas_call(
        forward_body,
        grid=(count,),
        in_specs=proj_specs(width, lambda i: i)
        + [
            pl.BlockSpec((BLOCK, width), rows),
            pl.BlockSpec(kernel.shape, whole),
            pl.BlockSpec(heads.shape, whole),
            pl.BlockSpec(gain.shape, whole),
        ],
        out_specs=[
            pl.BlockSpec((BLOCK, wide), rows),
            pl.BlockSpec((BLOCK, width), rows),
            pl.BlockSpec((1, N, width), lambda i: (i, 0, 0)),
            pl.BlockSpec((2, BLOCK), lambda i: (0, i)),
        ],
        out_shape=[
            jax.ShapeDtypeStruct((length, wide), BF16),
            jax.ShapeDtypeStruct((length, width), F32),
            jax.ShapeDtypeStruct((count, N, width), F32),
            jax.ShapeDtypeStruct((2, length), F32),
        ],
        scratch_shapes=[pltpu.VMEM((N, width), F32), pltpu.VMEM((BLOCK + EDGE, wide), F32)],
        compiler_params=pltpu.CompilerParams(vmem_limit_bytes=48 << 20),
        name="mixer_forward",
    )(odd, proj, proj, proj, proj, proj, grad_gated, kernel, heads, gain)


def backward_body(
    odd_ref, gate_ref, x_ref, step_ref, edge_ref, low_ref, up_ref, ssd_ref, state_ref, norm_ref, kernel_ref, head_ref, gain_ref,
    grad_ref, grad_step_ref, grad_own_ref, grad_other_ref, grad_kernel_ref, grad_head_ref, grad_gain_ref,
    adjoint, buffer, grads, next_state,
):
    width = gate_ref.shape[1]
    raw = step_ref[:, 0 : head_ref.shape[1]]
    taps = kernel_ref.shape[0] - 1
    count = pl.num_programs(0)
    step = pl.program_id(0)

    @pl.when(step == 0)
    def _():
        adjoint[...] = jnp.zeros_like(adjoint)
        next_state[...] = jnp.zeros_like(next_state)
        grads[BLOCK : BLOCK + EDGE, :] = jnp.zeros((EDGE, width), F32)
        grad_kernel_ref[...] = jnp.zeros_like(grad_kernel_ref)
        grad_head_ref[...] = jnp.zeros_like(grad_head_ref)
        grad_gain_ref[...] = jnp.zeros_like(grad_gain_ref)

    @pl.when(step > 0)
    def _():
        grads[BLOCK : BLOCK + EDGE, :] = grads[0:EDGE, :]

    last = step == count - 1
    buffer[0:EDGE, :] = jnp.where(last, 0.0, edge_ref[...].astype(BF16).astype(F32))
    buffer[EDGE : EDGE + BLOCK, :] = x_ref[...].astype(BF16).astype(F32)
    dt, decay, total, total_t = block_steps(raw, head_ref)
    odd = odd_ref[0, 0] == 1
    own, other = low_ref[:, width : width + N], low_ref[:, width + N : width + 2 * N]
    inject, readout = jnp.where(odd, other, own), jnp.where(odd, own, other)
    scores_t = dot_on(inject, readout, 1, 1)
    mask_t = order_mask(True)
    half = first_half(BLOCK)
    skip = over_heads(head_ref[2:3, :])
    inverse = norm_ref[:, 0:1]
    pull = norm_ref[:, 1:2]
    grad_scores_t = jnp.zeros((BLOCK, BLOCK), F32)
    grad_inject = jnp.zeros((BLOCK, N), F32)
    grad_readout = jnp.zeros((BLOCK, N), F32)
    decay_parts, step_parts, skip_parts, end_parts = [], [], [], []
    for pair in range(width // (2 * P_SIZE)):
        cols = slice(pair * 2 * P_SIZE, (pair + 1) * 2 * P_SIZE)
        x = low_ref[:, cols].astype(F32)
        gate_pre = gate_ref[:, cols]
        ssd = ssd_ref[:, cols]
        sig = sigmoid(gate_pre)
        gate = gate_pre * sig
        up = up_ref[:, cols]
        gated = ssd * gate
        grad_gain_ref[0:1, cols] += jnp.sum(up * gated * inverse, axis=0, keepdims=True)
        grad_pre = inverse * (up * gain_ref[0:1, cols]) - gated * pull
        grad_ref[:, cols] = (grad_pre * ssd * (sig * (1.0 + gate_pre * (1.0 - sig)))).astype(BF16)
        grad_ssd = grad_pre * gate
        grad_two = split(grad_ssd)
        total_p = over_pair(total, pair)
        dt_p = over_pair(dt, pair)
        to_end = jnp.exp(total_p[BLOCK - 1 : BLOCK, :] - total_p)
        scaled = x * dt_p
        scaled_two = split(scaled)
        local = []
        for index, head in enumerate((2 * pair, 2 * pair + 1)):
            gap = total_t[head : head + 1, :] - total[:, head : head + 1]
            decays = jnp.exp(jnp.where(mask_t, gap, -1e30))
            own = half if index == 0 else jnp.logical_not(half)
            mine = [jnp.where(own, part, jnp.zeros_like(part)) for part in grad_two]
            grad_scores_t += decays * dot_three(scaled_two, mine, 1, 1)
            local.append(dot_three(split(decays * scores_t), grad_two, 1, 0))
        local = jnp.where(half, local[0], local[1])
        lam = adjoint[:, cols]
        lam_two = split(lam)
        held = state_ref[0, :, cols]
        far = dot_on(inject, lam_two[0], 1, 0) + dot_on(inject, lam_two[1], 1, 0)
        moved = scaled * to_end
        grad_inject += dot_three(split(moved), lam_two, 1, 1)
        rising = split(grad_ssd * jnp.exp(total_p))
        grad_readout += dot_three(rising, split(held), 1, 1)
        end_parts.append(jnp.sum(lam * next_state[:, cols], axis=0, keepdims=True))
        adjoint[:, cols] = lam * jnp.exp(total_p[BLOCK - 1 : BLOCK, :]) + (
            dot_on(readout, rising[0], 0, 0) + dot_on(readout, rising[1], 0, 0)
        )
        next_state[:, cols] = held
        pure = ssd - skip[:, cols] * x
        decay_parts.append(grad_ssd * pure - scaled * local - moved * far)
        grad_scaled = local + to_end * far
        step_parts.append(x * grad_scaled)
        skip_parts.append(jnp.sum(grad_ssd * x, axis=0, keepdims=True))
        grad_x = dt_p * grad_scaled + skip[:, cols] * grad_ssd
        before = convolve(buffer, kernel_ref, pair * 2 * P_SIZE, 2 * P_SIZE)
        sig = sigmoid(before)
        grads[0:BLOCK, cols] = grad_x * (sig * (1.0 + before * (1.0 - sig)))
    row_grads = head_sums(jnp.concatenate(decay_parts, axis=1))
    upper = order_mask(True).astype(F32)
    ends = head_sums(jnp.concatenate(end_parts, axis=1))
    grad_log = dot_on(upper, row_grads, 1, 0, HIGH) + ends
    grad_dt = head_sums(jnp.concatenate(step_parts, axis=1)) + decay * grad_log
    grad_raw = grad_dt * sigmoid(raw + head_ref[0:1, :])
    grad_step_ref[...] = jnp.zeros((BLOCK, N), BF16)
    grad_step_ref[:, 0 : grad_raw.shape[1]] = grad_raw.astype(BF16)
    grad_head_ref[0:1, :] += jnp.sum(grad_raw, axis=0, keepdims=True)
    grad_head_ref[1:2, :] += decay * jnp.sum(dt * grad_log, axis=0, keepdims=True)
    grad_head_ref[2:3, :] += head_sums(jnp.concatenate(skip_parts, axis=1))
    scores_two = split(grad_scores_t)
    grad_inject = grad_inject + dot_two(scores_two, readout, 1, 0)
    grad_readout = grad_readout + dot_two(scores_two, inject, 0, 0)
    grad_own_ref[...] = jnp.where(odd, grad_readout, grad_inject)
    grad_other_ref[...] = jnp.where(odd, grad_inject, grad_readout)
    grad_ref[:, width : 2 * width] = convolve_back(buffer, grads, kernel_ref, grad_kernel_ref)


def convolve_back(buffer, grads, kernel_ref, grad_kernel_ref):
    taps = kernel_ref.shape[0] - 1
    width = grads.shape[1]
    here = grads[0:BLOCK, :]
    grad_kernel_ref[taps : taps + 1, :] += jnp.sum(here, axis=0, keepdims=True)
    total = jnp.zeros((BLOCK, width), F32)
    for tap in range(taps):
        low = EDGE - taps + 1 + tap
        grad_kernel_ref[tap : tap + 1, :] += jnp.sum(here * buffer[low : low + BLOCK, :], axis=0, keepdims=True)
        ahead = taps - 1 - tap
        total = total + kernel_ref[tap : tap + 1, 0:width] * grads[ahead : ahead + BLOCK, :]
    return total.astype(BF16)


def mixer_backward(odd, proj, low, grad_gated, ssd, states, norms, kernel, heads, gain):
    length, width = grad_gated.shape
    wide = width + 2 * N
    count = length // BLOCK
    place = lambda i: count - 1 - i
    back = lambda i: (place(i), 0)
    edge = lambda i: jnp.maximum(place(i) * (BLOCK // EDGE) - 1, 0)
    whole = lambda i: (0, 0)
    specs = proj_specs(width, place)
    return pl.pallas_call(
        backward_body,
        grid=(count,),
        in_specs=specs[:3]
        + [
            specs[4],
            pl.BlockSpec((EDGE, width), lambda i: (edge(i), 1)),
            pl.BlockSpec((BLOCK, wide), back),
            pl.BlockSpec((BLOCK, width), back),
            pl.BlockSpec((BLOCK, width), back),
            pl.BlockSpec((1, N, width), lambda i: (place(i), 0, 0)),
            pl.BlockSpec((BLOCK, norms.shape[1]), back),
            pl.BlockSpec(kernel.shape, whole),
            pl.BlockSpec(heads.shape, whole),
            pl.BlockSpec(gain.shape, whole),
        ],
        out_specs=[
            pl.BlockSpec((BLOCK, 2 * width), back),
            pl.BlockSpec((BLOCK, N), back),
            pl.BlockSpec((BLOCK, N), back),
            pl.BlockSpec((BLOCK, N), back),
            pl.BlockSpec((kernel.shape[0], width), whole),
            pl.BlockSpec(heads.shape, whole),
            pl.BlockSpec(gain.shape, whole),
        ],
        out_shape=[
            jax.ShapeDtypeStruct((length, 2 * width), BF16),
            jax.ShapeDtypeStruct((length, N), BF16),
            jax.ShapeDtypeStruct((length, N), F32),
            jax.ShapeDtypeStruct((length, N), F32),
            jax.ShapeDtypeStruct((kernel.shape[0], width), F32),
            jax.ShapeDtypeStruct(heads.shape, F32),
            jax.ShapeDtypeStruct(gain.shape, F32),
        ],
        scratch_shapes=[
            pltpu.VMEM((N, width), F32),
            pltpu.VMEM((BLOCK + EDGE, width), F32),
            pltpu.VMEM((BLOCK + EDGE, width), F32),
            pltpu.VMEM((N, width), F32),
        ],
        compiler_params=pltpu.CompilerParams(vmem_limit_bytes=56 << 20),
        name="mixer_backward",
    )(odd, proj, proj, proj, proj, low, grad_gated, ssd, states, norms, kernel, heads, gain)


def map_backward_body(own_ref, edge_ref, mine_ref, theirs_ref, step_ref, kernel_ref, grad_ref, grad_kernel_ref, buffer, grads):
    step = pl.program_id(0)

    @pl.when(step == 0)
    def _():
        grads[BLOCK : BLOCK + EDGE, :] = jnp.zeros((EDGE, N), F32)
        grad_kernel_ref[...] = jnp.zeros_like(grad_kernel_ref)

    @pl.when(step > 0)
    def _():
        grads[BLOCK : BLOCK + EDGE, :] = grads[0:EDGE, :]

    last = step == pl.num_programs(0) - 1
    buffer[0:EDGE, :] = jnp.where(last, 0.0, edge_ref[...].astype(BF16).astype(F32))
    buffer[EDGE : EDGE + BLOCK, :] = own_ref[...].astype(BF16).astype(F32)
    before = convolve(buffer, kernel_ref, 0, N)
    sig = sigmoid(before)
    grads[0:BLOCK, :] = (mine_ref[...] + theirs_ref[...]) * (sig * (1.0 + before * (1.0 - sig)))
    grad_ref[:, 0:N] = convolve_back(buffer, grads, kernel_ref, grad_kernel_ref)
    grad_ref[:, N : 2 * N] = step_ref[...]


def map_backward(proj, mine, theirs, steps, kernel, column):
    length = mine.shape[0]
    count = length // BLOCK
    place = lambda i: count - 1 - i
    edge = lambda i: jnp.maximum(place(i) * (BLOCK // EDGE) - 1, 0)
    back = lambda i: (place(i), 0)
    whole = lambda i: (0, 0)
    narrow = pl.BlockSpec((BLOCK, N), back)
    return pl.pallas_call(
        map_backward_body,
        grid=(count,),
        in_specs=[
            pl.BlockSpec((BLOCK, N), lambda i: (place(i), column // N)),
            pl.BlockSpec((EDGE, N), lambda i: (edge(i), column // N)),
            narrow,
            narrow,
            narrow,
            pl.BlockSpec(kernel.shape, whole),
        ],
        out_specs=[pl.BlockSpec((BLOCK, 2 * N), back), pl.BlockSpec(kernel.shape, whole)],
        out_shape=[jax.ShapeDtypeStruct((length, 2 * N), BF16), jax.ShapeDtypeStruct(kernel.shape, F32)],
        scratch_shapes=[pltpu.VMEM((BLOCK + EDGE, N), F32), pltpu.VMEM((BLOCK + EDGE, N), F32)],
        name="map_backward",
    )(proj, proj, mine, theirs, steps, kernel)


def remote(src, dst, send, recv, device):
    return pltpu.make_async_remote_copy(
        src_ref=src, dst_ref=dst, send_sem=send, recv_sem=recv, device_id=device, device_id_type=MESH
    )


def gather_body(order, sizes, *refs):
    nctx, ndp, ntp = sizes
    ntok, nw = 2, (len(refs) - 9) // 2 - 2
    toks, weights = refs[:ntok], refs[ntok : ntok + nw]
    tok_outs = refs[ntok + nw : 2 * ntok + nw]
    weight_outs = refs[2 * ntok + nw : 2 * ntok + 2 * nw]
    z_send, z_recv, t_send, t_recv, w_send, w_recv, x_send, x_recv, own = refs[2 * ntok + 2 * nw :]
    c, d, t = lax.axis_index("ctx"), lax.axis_index("dp"), lax.axis_index("tp")
    near = t + 1 - 2 * lax.rem(t, 2)
    far = lax.rem(t + 2, ntp)
    length = toks[0].shape[0]
    part = length // ntp

    barrier = pltpu.get_barrier_semaphore()
    peers = [{"ctx": lax.rem(c + s, nctx)} for s in range(1, nctx)]
    peers += [{"dp": lax.rem(d + s, ndp)} for s in range(1, ndp)]
    peers += [{"tp": near}, {"tp": far}]
    for peer in peers:
        pl.semaphore_signal(barrier, inc=1, device_id=peer, device_id_type=MESH)
    pl.semaphore_wait(barrier, len(peers))

    def rows(a, block, quarter):
        return tok_outs[a].at[pl.ds(pl.multiple_of(block * length + quarter * part, 16), part), :]

    def hop(a, j, side):
        block = c - j if side == 0 else c + j
        to = c + 1 if side == 0 else c - 1
        valid = (block >= 0) & (to < nctx) if side == 0 else (block < nctx) & (to >= 0)
        safe = jnp.clip(block, 0, nctx - 1)
        source = toks[a].at[pl.ds(pl.multiple_of(t * part, 16), part), :] if j == 0 else rows(a, safe, t)
        copy = remote(source, rows(a, safe, t), z_send.at[a, j, side], z_recv.at[a, safe], {"ctx": jnp.clip(to, 0, nctx - 1)})
        return valid, copy

    def arrival(j, side):
        block = c - 1 - j if side == 0 else c + 1 + j
        valid = block >= 0 if side == 0 else block < nctx
        return valid, jnp.clip(block, 0, nctx - 1)

    def tp_copy(a, block, kind):
        quarter = t if kind < 2 else far
        view = rows(a, block, quarter)
        return remote(view, view, t_send.at[a, block, kind], t_recv.at[a, block, kind], {"tp": far if kind == 0 else near})

    def tp_arrival(a, block, kind):
        quarter = far if kind == 0 else (near if kind == 1 else lax.rem(near + 2, ntp))
        view = rows(a, block, quarter)
        return remote(view, view, t_send.at[a, block, kind], t_recv.at[a, block, kind], {"tp": near})

    def w_copy(a, s):
        to = lax.rem(c + s, nctx)
        return remote(weights[a].at[to], weight_outs[a].at[d, c], w_send.at[a, s], w_recv.at[a, s], {"ctx": to})

    def w_arrival(a, s):
        view = weight_outs[a].at[d, lax.rem(c - s + nctx, nctx)]
        return remote(view, view, w_send.at[a, s], w_recv.at[a, s], {"ctx": c})

    def x_copy(a, s, e):
        block = lax.rem(c - s + nctx, nctx)
        source = weights[a].at[c] if s == 0 else weight_outs[a].at[d, block]
        return remote(source, weight_outs[a].at[d, block], x_send.at[a, s, e], x_recv.at[a, s, e], {"dp": lax.rem(d + e, ndp)})

    def x_arrival(a, s, e):
        view = weight_outs[a].at[lax.rem(d - e + ndp, ndp), lax.rem(c - s + nctx, nctx)]
        return remote(view, view, x_send.at[a, s, e], x_recv.at[a, s, e], {"dp": d})

    def own_tok(a):
        return pltpu.make_async_copy(toks[a], tok_outs[a].at[pl.ds(pl.multiple_of(c * length, 16), length), :], own.at[a])

    def own_weight(a):
        return pltpu.make_async_copy(weights[a].at[c], weight_outs[a].at[d, c], own.at[ntok + a])

    def launch(step):
        kind, a, j = step
        if kind == "tok":
            for side in (0, 1):
                valid, copy = hop(a, j, side)

                @pl.when(valid)
                def _():
                    copy.start()
        else:
            w_copy(a, j).start()

    def settle(step):
        kind, a, j = step
        if kind == "tok":
            for side in (0, 1):
                valid, block = arrival(j, side)

                @pl.when(valid)
                def _():
                    view = rows(a, block, t)
                    remote(view, view, z_send.at[a, j, side], z_recv.at[a, block], {"ctx": c}).wait_recv()
                    tp_copy(a, block, 0).start()
                    tp_copy(a, block, 1).start()
        else:
            w_arrival(a, j).wait_recv()
            for e in range(1, ndp):
                x_copy(a, j, e).start()

    def settle_far(step):
        kind, a, j = step
        if kind == "tok":
            for side in (0, 1):
                valid, block = arrival(j, side)

                @pl.when(valid)
                def _():
                    tp_arrival(a, block, 0).wait_recv()
                    tp_copy(a, block, 2).start()

    for step in order[:DEPTH]:
        launch(step)
    for a in range(nw):
        own_weight(a).start()
        for e in range(1, ndp):
            x_copy(a, 0, e).start()
    for a in range(ntok):
        own_tok(a).start()
    for index, step in enumerate(order):
        settle(step)
        if index + DEPTH < len(order):
            launch(order[index + DEPTH])
        if index >= 2:
            settle_far(order[index - 2])
    for step in order[-2:]:
        settle_far(step)
    for kind, a, j in order:
        if kind == "tok":
            for side in (0, 1):
                valid, copy = hop(a, j, side)
                here, block = arrival(j, side)

                @pl.when(valid)
                def _():
                    copy.wait_send()

                @pl.when(here)
                def _():
                    for part_kind in range(3):
                        tp_copy(a, block, part_kind).wait_send()
                    tp_arrival(a, block, 1).wait_recv()
                    tp_arrival(a, block, 2).wait_recv()
        else:
            w_copy(a, j).wait_send()
            for e in range(1, ndp):
                x_copy(a, j, e).wait_send()
                x_arrival(a, j, e).wait_recv()
    for a in range(nw):
        own_weight(a).wait()
        for e in range(1, ndp):
            x_copy(a, 0, e).wait_send()
            x_arrival(a, 0, e).wait_recv()
    for a in range(ntok):
        own_tok(a).wait()


def gather_all(toks, weights, sizes):
    nctx, ndp, ntp = sizes
    turns = range(1, nctx)
    nw = len(weights)
    tok = lambda a, j: [("tok", a, j)] if j < nctx - 1 else []
    per = lambda a: [("w", a, s) for s in turns]
    order = tok(0, 0) + tok(1, 0) + per(0) + tok(0, 1) + tok(1, 1) + per(1)[:1] + tok(0, 2) + tok(1, 2) + per(1)[1:]
    any_space = pl.BlockSpec(memory_space=pl.ANY)
    length, model = toks[0].shape
    out_shape = [jax.ShapeDtypeStruct((nctx * length, model), BF16) for _ in toks]
    out_shape += [jax.ShapeDtypeStruct((ndp,) + w.shape, BF16) for w in weights]
    dma = pltpu.SemaphoreType.DMA
    return pl.pallas_call(
        functools.partial(gather_body, order, sizes),
        out_shape=out_shape,
        in_specs=[any_space] * (len(toks) + nw),
        out_specs=[any_space] * len(out_shape),
        scratch_shapes=[
            dma((2, nctx, 2)), dma((2, nctx)), dma((2, nctx, 3)), dma((2, nctx, 3)),
            dma((nw, nctx)), dma((nw, nctx)), dma((nw, nctx, ndp)), dma((nw, nctx, ndp)), dma((2 + nw,)),
        ],
        compiler_params=pltpu.CompilerParams(collective_id=1, has_side_effects=True),
        name="gather_inputs",
    )(*toks, *weights)


def add_rows(target, sources, rows, step):
    def some(index, _):
        here = pl.ds(pl.multiple_of(index * step, step), step)
        total = sources[0][here, :].astype(F32)
        for source in sources[1:]:
            total = total + source[here, :].astype(F32)
        target[here, :] = total.astype(target.dtype)
        return 0

    lax.fori_loop(0, rows // step, some, 0)


def output_body(order, sizes, *refs):
    nctx, ndp, ntp = sizes
    nw = (len(refs) - 23) // 4
    partial, grads = refs[0], refs[1 : 1 + nw]
    sum_out, grad_outs = refs[1 + nw], refs[2 + nw : 2 + 2 * nw]
    (near_in, far_out, far_in, z_out, z_in, held, acc, done) = refs[2 + 2 * nw : 10 + 2 * nw]
    x_ins = refs[10 + 2 * nw : 10 + 3 * nw]
    x_sums = refs[10 + 3 * nw : 10 + 4 * nw]
    (near_s, near_r, far_s, far_r, z_s, z_r, x_s, x_r, w_s, w_r, fin_s, fin_r, local) = refs[10 + 4 * nw :]
    c, d, t = lax.axis_index("ctx"), lax.axis_index("dp"), lax.axis_index("tp")
    near = t + 1 - 2 * lax.rem(t, 2)
    far = lax.rem(t + 2, ntp)
    far_near = lax.rem(near + 2, ntp)
    length = sum_out.shape[0]
    part = length // ntp
    wrap = lambda i: lax.rem(i + nctx, nctx)

    barrier = pltpu.get_barrier_semaphore()
    peers = [{"ctx": lax.rem(c + s, nctx)} for s in range(1, nctx)]
    peers += [{"dp": lax.rem(d + e, ndp)} for e in range(1, ndp)]
    peers += [{"tp": near}, {"tp": far}]
    for peer in peers:
        pl.semaphore_signal(barrier, inc=1, device_id=peer, device_id_type=MESH)
    pl.semaphore_wait(barrier, len(peers))

    def rows(s, quarter):
        return partial.at[pl.ds(pl.multiple_of(wrap(c + s) * length + quarter * part, 16), part), :]

    def near_copy(s, slot):
        return remote(rows(s, near if slot == 0 else far_near), near_in.at[s, slot], near_s.at[s, slot], near_r.at[s, slot], {"tp": near})

    def far_copy(s):
        return remote(far_out.at[s], far_in.at[s], far_s.at[s], far_r.at[s], {"tp": far})

    def z_copy(s):
        return remote(z_out.at[s], z_in.at[s], z_s.at[s], z_r.at[s], {"ctx": wrap(c + s)})

    def x_copy(a, s, e):
        to = lax.rem(d + e, ndp)
        return remote(grads[a].at[to, wrap(c + s)], x_ins[a].at[s, e - 1], x_s.at[a, s, e], x_r.at[a, s, e], {"dp": to})

    def w_copy(a, s):
        return remote(x_sums[a].at[s], grad_outs[a].at[c], w_s.at[a, s], w_r.at[a, s], {"ctx": wrap(c + s)})

    def w_arrival(a, s):
        view = grad_outs[a].at[wrap(c - s)]
        return remote(view, view, w_s.at[a, s], w_r.at[a, s], {"ctx": c})

    def load(s, quarter, slot):
        return pltpu.make_async_copy(rows(s, quarter), held.at[slot], local.at[slot])

    def load_grad(a, s):
        return pltpu.make_async_copy(grads[a].at[d, wrap(c + s)], x_sums[a].at[s], local.at[2 + a * nctx + s])

    def start_x(s):
        for a in range(nw):
            for e in range(1, ndp):
                x_copy(a, s, e).start()

    def near_sum(s):
        load(s, far, 0).start()
        near_copy(s, 1).wait_recv()
        load(s, far, 0).wait()
        add_rows(far_out.at[s], [held.at[0], near_in.at[s, 1]], part, 16)
        far_copy(s).start()

    def far_sum(s):
        load(s, t, 1).start()
        near_copy(s, 0).wait_recv()
        far_copy(s).wait_recv()
        load(s, t, 1).wait()
        add_rows(acc if s == 0 else z_out.at[s], [held.at[1], near_in.at[s, 0], far_in.at[s]], part, 16)
        if s > 0:
            z_copy(s).start()

    def grad_sum(s):
        for a in range(nw):
            load_grad(a, s).wait()
            for e in range(1, ndp):
                x_copy(a, s, e).wait_recv()
            add_rows(x_sums[a].at[s], [x_sums[a].at[s]] + [x_ins[a].at[s, e - 1] for e in range(1, ndp)], x_sums[a].shape[1], 16)
            if s > 0:
                w_copy(a, s).start()
            else:
                pltpu.make_async_copy(x_sums[a].at[0], grad_outs[a].at[c], local.at[2 + nw * nctx + a]).start()

    for s in order:
        for slot in (1, 0):
            near_copy(s, slot).start()
        for a in range(nw):
            load_grad(a, s).start()
    ahead = 2
    for s in order[:ahead]:
        start_x(s)
    for s in order[:ahead]:
        near_sum(s)
    for index, s in enumerate(order):
        far_sum(s)
        if index + ahead < nctx:
            near_sum(order[index + ahead])
        grad_sum(s)
        if index + ahead < nctx:
            start_x(order[index + ahead])
    for s in range(1, nctx):
        z_copy(s).wait_recv()
    add_rows(done, [acc] + [z_in.at[s] for s in range(1, nctx)], part, 16)

    def mine(quarter):
        return sum_out.at[pl.ds(pl.multiple_of(quarter * part, 16), part), :]

    finals = [
        remote(done, mine(t), fin_s.at[0], fin_r.at[0], {"tp": far}),
        remote(done, mine(t), fin_s.at[1], fin_r.at[1], {"tp": near}),
        remote(mine(far), mine(far), fin_s.at[2], fin_r.at[2], {"tp": near}),
    ]
    keep = pltpu.make_async_copy(done, mine(t), local.at[0])
    finals[0].start()
    finals[1].start()
    keep.start()
    remote(mine(far), mine(far), fin_s.at[0], fin_r.at[0], {"tp": far}).wait_recv()
    finals[2].start()
    remote(mine(near), mine(near), fin_s.at[1], fin_r.at[1], {"tp": near}).wait_recv()
    remote(mine(far_near), mine(far_near), fin_s.at[2], fin_r.at[2], {"tp": near}).wait_recv()
    keep.wait()
    for copy in finals:
        copy.wait_send()
    for s in order:
        for slot in (1, 0):
            near_copy(s, slot).wait_send()
        far_copy(s).wait_send()
        for a in range(nw):
            for e in range(1, ndp):
                x_copy(a, s, e).wait_send()
            if s > 0:
                w_copy(a, s).wait_send()
                w_arrival(a, s).wait_recv()
            else:
                pltpu.make_async_copy(x_sums[a].at[0], grad_outs[a].at[c], local.at[2 + nw * nctx + a]).wait()
        if s > 0:
            z_copy(s).wait_send()


def return_all(partial, grads, sizes):
    nctx, ndp, ntp = sizes
    length = partial.shape[0] // nctx
    part, model = length // ntp, partial.shape[1]
    nw = len(grads)
    order = [nctx // 2] + [s for s in range(1, nctx) if s != nctx // 2] + [0]
    any_space = pl.BlockSpec(memory_space=pl.ANY)
    dma = pltpu.SemaphoreType.DMA
    vmem = pltpu.VMEM
    strip = lambda *lead: vmem(lead + (part, model), BF16)
    return pl.pallas_call(
        functools.partial(output_body, order, sizes),
        out_shape=[jax.ShapeDtypeStruct((length, model), BF16)] + [jax.ShapeDtypeStruct(g.shape[1:], BF16) for g in grads],
        in_specs=[any_space] * (1 + nw),
        out_specs=[any_space] * (1 + nw),
        scratch_shapes=[
            strip(nctx, 2), strip(nctx), strip(nctx), strip(nctx), strip(nctx), strip(2), vmem((part, model), F32), strip(),
        ]
        + [vmem((nctx, max(ndp - 1, 1)) + g.shape[2:], BF16) for g in grads]
        + [vmem((nctx,) + g.shape[2:], BF16) for g in grads]
        + [
            dma((nctx, 2)), dma((nctx, 2)), dma((nctx,)), dma((nctx,)), dma((nctx,)), dma((nctx,)),
            dma((nw, nctx, ndp)), dma((nw, nctx, ndp)), dma((nw, nctx)), dma((nw, nctx)), dma((3,)), dma((3,)),
            dma((2 + nw * nctx + nw,)),
        ],
        compiler_params=pltpu.CompilerParams(collective_id=2, has_side_effects=True, vmem_limit_bytes=60 << 20),
        name="return_outputs",
    )(partial, *grads)


def small_body(sizes, value, gathered, send, recv, own):
    nctx, ndp = sizes
    c, d = lax.axis_index("ctx"), lax.axis_index("dp")
    others = [(e, s) for e in range(ndp) for s in range(nctx) if e or s]
    place = lambda e, s: {"dp": lax.rem(d + e, ndp), "ctx": lax.rem(c + s, nctx)}
    barrier = pltpu.get_barrier_semaphore()
    for e, s in others:
        pl.semaphore_signal(barrier, inc=1, device_id=place(e, s), device_id_type=MESH)
    pl.semaphore_wait(barrier, len(others))
    keep = pltpu.make_async_copy(value, gathered.at[d, c], own)
    keep.start()
    for e, s in others:
        remote(value, gathered.at[d, c], send.at[e, s], recv.at[e, s], place(e, s)).start()
    for e, s in others:
        view = gathered.at[lax.rem(d - e + ndp, ndp), lax.rem(c - s + nctx, nctx)]
        remote(view, view, send.at[e, s], recv.at[e, s], place(e, s)).wait_recv()
        remote(value, gathered.at[d, c], send.at[e, s], recv.at[e, s], place(e, s)).wait_send()
    keep.wait()


def gather_small(value, sizes):
    nctx, ndp = sizes
    vmem = pl.BlockSpec(memory_space=pltpu.VMEM)
    dma = pltpu.SemaphoreType.DMA
    return pl.pallas_call(
        functools.partial(small_body, sizes),
        out_shape=jax.ShapeDtypeStruct((ndp, nctx) + value.shape, F32),
        in_specs=[vmem],
        out_specs=vmem,
        scratch_shapes=[dma((ndp, nctx)), dma((ndp, nctx)), dma],
        compiler_params=pltpu.CompilerParams(collective_id=3, has_side_effects=True),
        name="gather_small",
    )(value)


def dot_last(left_side, right_side):
    return lax.dot_general(left_side, right_side, (((1,), (1,)), ((), ())), preferred_element_type=F32)


def dot_first(left_side, right_side):
    return lax.dot_general(left_side, right_side, (((0,), (0,)), ((), ())), preferred_element_type=F32)


def sum_rows(partial):
    return lax.psum_scatter(partial.astype(BF16), ("ctx", "tp"), scatter_dimension=0, tiled=True).astype(F32)


def shards(tokens, norm_gain, zx_weight, bc_weight, dt_weight, conv_x, conv_bc, head_params, gate_gain, out_weight, cotangent):
    seq_count, length, model_width = tokens.shape
    assert seq_count == 1
    nctx, ntp, ndp = lax.axis_size("ctx"), lax.axis_size("tp"), lax.axis_size("dp")
    ctx = lax.axis_index("ctx")
    rows = dt_weight.shape[0]
    inner = conv_x.shape[1]
    groups = bc_weight.shape[2] // N
    share = nctx // groups
    assert share == 2 and groups * share == nctx
    width = inner // nctx
    heads = dt_weight.shape[1] // nctx
    taps = conv_x.shape[0] - 1
    group_width = inner // groups

    def mine(value):
        return lax.dynamic_index_in_dim(value, ctx, 0, False)

    def partner(value):
        return lax.ppermute(value, "ctx", [(i, i ^ 1) for i in range(nctx)])

    hidden = tokens.astype(F32).reshape(length, model_width)
    cot = cotangent.reshape(length, model_width)
    rscale = lax.rsqrt(jnp.mean(hidden * hidden, axis=-1, keepdims=True) + EPS)
    normed = (hidden * rscale * norm_gain).astype(BF16)

    zx = zx_weight.reshape(rows, 2, nctx, width)
    maps = bc_weight.reshape(rows, 2, groups, N).transpose(0, 2, 1, 3)
    own = maps.reshape(rows, nctx, N)
    other = maps[:, :, ::-1].reshape(rows, nctx, N)
    steps = jnp.pad(dt_weight.reshape(rows, nctx, heads), ((0, 0), (0, 0), (0, N - heads)))
    packed_in = jnp.concatenate([zx[:, 0], zx[:, 1], own, steps, other], axis=2).transpose(1, 0, 2)
    packed_out = out_weight.reshape(rows, nctx, width).transpose(1, 0, 2)
    normed_all, cot_all, weight_in, weight_out = gather_all((normed, cot), (packed_in, packed_out), (nctx, ndp, ntp))
    weight_in = weight_in.reshape(model_width, -1)
    weight_out = weight_out.reshape(model_width, width)

    grad_gated = jnp.dot(cot_all, weight_out, preferred_element_type=F32)
    proj = jnp.dot(normed_all, weight_in, preferred_element_type=F32)
    odd = lax.rem(ctx, 2)
    kernel_x = mine(conv_x.reshape(taps + 1, nctx, width).transpose(1, 0, 2))
    kernel_maps = conv_bc.reshape(taps + 1, 2, groups, N).transpose(2, 1, 0, 3).reshape(nctx, taps + 1, N)
    kernel_own = mine(kernel_maps)
    kernel_other = lax.dynamic_index_in_dim(kernel_maps, ctx + 1 - 2 * odd, 0, False)
    kernel = jnp.concatenate([kernel_x, kernel_own, kernel_other], axis=1)
    odd = odd.astype(jnp.int32).reshape(1, 1)
    heads_mine = mine(head_params.reshape(3, nctx, heads).transpose(1, 0, 2))
    gain = mine(gate_gain.reshape(nctx, 1, width))
    low, ssd, states, sums = mixer_forward(odd, proj, grad_gated, kernel, heads_mine, gain)
    sums = (sums + partner(sums)) / group_width
    inverse = lax.rsqrt(sums[0] + EPS)
    norms = jnp.stack([inverse, inverse * inverse * inverse * sums[1]], axis=1)
    gate_pre = proj[:, :width]
    gated_norm = (ssd * (gate_pre * jax.nn.sigmoid(gate_pre)) * norms[:, 0:1] * gain).astype(BF16)
    branch = sum_rows(dot_last(gated_norm, weight_out))
    part = length // ntp
    hidden_part = lax.dynamic_slice_in_dim(hidden, lax.axis_index("tp") * part, part, 0)
    mixed = lax.all_gather((hidden_part + branch).astype(BF16), "tp", axis=0, tiled=True)
    grad_zx, grad_steps, grad_own, grad_other, grad_kernel_x, grad_heads, gate_gain_grad = mixer_backward(
        odd, proj, low, grad_gated, ssd, states, norms, kernel, heads_mine, gain
    )
    theirs = partner(grad_other)
    grad_rest, grad_kernel_own = map_backward(proj, grad_own, theirs, grad_steps, kernel_own, 2 * width)
    grad_all = jnp.concatenate([grad_zx, grad_rest], axis=1)
    blocks = lambda grad: grad.astype(BF16).reshape(ndp, nctx, rows, -1)
    weight_grads = (
        blocks(dot_first(normed_all, grad_zx)),
        blocks(dot_first(normed_all, grad_rest)),
        blocks(dot_first(cot_all, gated_norm)),
    )
    partial = dot_last(grad_all, weight_in[:, : grad_all.shape[1]]).astype(BF16)
    grad_normed, back_zx, back_rest, back_out = return_all(partial, weight_grads, (nctx, ndp, ntp))
    grad_normed = grad_normed.astype(F32)

    grad_hat = grad_normed * norm_gain
    norm_gain_grad = jnp.sum(grad_normed * hidden * rscale, axis=0)
    grad_hidden = rscale * grad_hat - hidden * (rscale * rscale * rscale) * jnp.mean(
        grad_hat * hidden, axis=1, keepdims=True
    )
    tokens_grad = cot.astype(F32) + grad_hidden

    zx_weight_grad = back_zx.astype(F32).reshape(nctx, rows, 2, width).transpose(1, 2, 0, 3).reshape(rows, 2, inner)
    back_rest = back_rest.astype(F32)
    bc_weight_grad = back_rest[:, :, :N].reshape(groups, 2, rows, N).transpose(2, 1, 0, 3).reshape(rows, 2, groups * N)
    dt_weight_grad = back_rest[:, :, N : N + heads].transpose(1, 0, 2).reshape(rows, nctx * heads)
    out_weight_grad = back_out.astype(F32).transpose(1, 0, 2).reshape(rows, inner)

    pieces = (grad_kernel_x, grad_kernel_own, grad_heads, gate_gain_grad, norm_gain_grad)
    small = jnp.concatenate([piece.reshape(-1) for piece in pieces])
    lines = -(-small.shape[0] // (8 * N)) * 8
    small = jnp.pad(small, (0, lines * N - small.shape[0])).reshape(lines, N)
    table = jnp.sum(gather_small(small, (nctx, ndp)), axis=0).reshape(nctx, lines * N)
    ends = [0]
    for piece in pieces:
        ends.append(ends[-1] + piece.size)
    kernel_x, kernel_own, head_grad, gain_grad, norm_grad = [table[:, a:b] for a, b in zip(ends[:-1], ends[1:])]
    conv_x_grad = kernel_x.reshape(nctx, taps + 1, width).transpose(1, 0, 2).reshape(taps + 1, inner)
    conv_bc_grad = kernel_own.reshape(groups, 2, taps + 1, N).transpose(2, 1, 0, 3).reshape(taps + 1, 2, groups * N)
    head_grad = head_grad.reshape(nctx, 3, heads).transpose(1, 0, 2).reshape(3, nctx * heads)
    gate_gain_grad = gain_grad.reshape(inner)
    norm_gain_grad = jnp.sum(norm_grad, axis=0)
    return (
        mixed.reshape(tokens.shape),
        tokens_grad.reshape(tokens.shape),
        norm_gain_grad,
        zx_weight_grad,
        bc_weight_grad,
        dt_weight_grad,
        conv_x_grad,
        conv_bc_grad,
        head_grad,
        gate_gain_grad,
        out_weight_grad,
    )


def solution(mesh):
    wide = P(("dp", "ctx"), None, "tp")
    flat = P(("dp", "ctx"), "tp")
    rows = P("dp", "ctx", None)
    return jax.shard_map(
        shards,
        mesh=mesh,
        in_specs=(rows, P(), wide, wide, flat, P(None, "tp"), P(None, None, "tp"), P(None, "tp"), P("tp"), flat, rows),
        out_specs=(rows, rows, P(), wide, wide, flat, P(None, "tp"), P(None, None, "tp"), P(None, "tp"), P("tp"), flat),
        check_vma=False,
    )
```

```python
import functools

import jax
import jax.numpy as jnp
from jax import lax
from jax.experimental import pallas as pl
from jax.experimental.pallas import tpu as pltpu
from jax.sharding import PartitionSpec as P

P_SIZE = 64
N = 128
BLOCK = 256
EDGE = 8
DEPTH = 3
MESH = pl.DeviceIdType.MESH
EPS = 1e-05
HIGH = lax.Precision.HIGHEST
F32 = jnp.float32
BF16 = jnp.bfloat16


def dot_on(left_side, right_side, left_dim, right_dim, precision=None):
    return lax.dot_general(
        left_side, right_side, (((left_dim,), (right_dim,)), ((), ())), precision=precision, preferred_element_type=F32
    )


def split(v):
    high = v.astype(BF16)
    return high, (v - high.astype(F32)).astype(BF16)


def dot_two(parts, other, part_dim, other_dim):
    return dot_on(parts[0], other, part_dim, other_dim) + dot_on(parts[1], other, part_dim, other_dim)


def dot_three(left_side, right_side, left_dim, right_dim):
    high = dot_two(left_side, right_side[0], left_dim, right_dim)
    return high + dot_on(left_side[0], right_side[1], left_dim, right_dim)


def softplus(v):
    return jnp.maximum(v, 0.0) + jnp.log1p(jnp.exp(-jnp.abs(v)))


def sigmoid(v):
    return 1.0 / (1.0 + jnp.exp(-v))


def order_mask(transposed):
    row = lax.broadcasted_iota(jnp.int32, (BLOCK, BLOCK), 0)
    col = lax.broadcasted_iota(jnp.int32, (BLOCK, BLOCK), 1)
    return row <= col if transposed else row >= col


def first_half(rows):
    return lax.broadcasted_iota(jnp.int32, (rows, 2 * P_SIZE), 1) < P_SIZE


def over_pair(value, pair):
    shape = (value.shape[0], P_SIZE * 2)
    left = jnp.broadcast_to(value[:, 2 * pair : 2 * pair + 1], shape)
    right = jnp.broadcast_to(value[:, 2 * pair + 1 : 2 * pair + 2], shape)
    return jnp.where(first_half(shape[0]), left, right)


def over_heads(value):
    return jnp.concatenate([over_pair(value, pair) for pair in range(value.shape[1] // 2)], axis=1)


def head_sums(value):
    columns = []
    for pair in range(value.shape[1] // (2 * P_SIZE)):
        part = value[:, pair * 2 * P_SIZE : (pair + 1) * 2 * P_SIZE]
        left = jnp.where(first_half(part.shape[0]), part, 0.0)
        columns += [jnp.sum(left, axis=1, keepdims=True), jnp.sum(part - left, axis=1, keepdims=True)]
    heads = len(columns)
    lane = lax.broadcasted_iota(jnp.int32, (value.shape[0], heads), 1)
    total = jnp.broadcast_to(columns[0], lane.shape)
    for head in range(1, heads):
        total = jnp.where(lane == head, columns[head], total)
    return total


def convolve(buffer, kernel_ref, start, width):
    taps = kernel_ref.shape[0] - 1
    total = kernel_ref[taps : taps + 1, start : start + width]
    for tap in range(taps):
        low = EDGE - taps + 1 + tap
        total = total + kernel_ref[tap : tap + 1, start : start + width] * buffer[low : low + BLOCK, start : start + width]
    return total


def block_steps(raw, head_ref):
    dt = softplus(raw + head_ref[0:1, :])
    decay = -jnp.exp(head_ref[1:2, :])
    log_step = dt * decay
    lower = order_mask(False).astype(F32)
    total = dot_on(lower, log_step, 1, 0, HIGH)
    total_t = dot_on(log_step, lower, 0, 1, HIGH)
    return dt, decay, total, total_t


def forward_body(
    odd_ref, gate_ref, x_ref, own_ref, step_ref, other_ref, up_ref, kernel_ref, head_ref, gain_ref,
    low_ref, ssd_ref, state_ref, sums_ref, state, buffer,
):
    width = gate_ref.shape[1]
    raw = step_ref[:, 0 : head_ref.shape[1]]
    first = pl.program_id(0) == 0

    @pl.when(first)
    def _():
        state[...] = jnp.zeros_like(state)
        buffer[0:EDGE, :] = jnp.zeros((EDGE, buffer.shape[1]), F32)

    @pl.when(jnp.logical_not(first))
    def _():
        buffer[0:EDGE, :] = buffer[BLOCK : BLOCK + EDGE, :]

    buffer[EDGE : EDGE + BLOCK, 0:width] = x_ref[...].astype(BF16).astype(F32)
    buffer[EDGE : EDGE + BLOCK, width : width + N] = own_ref[...].astype(BF16).astype(F32)
    buffer[EDGE : EDGE + BLOCK, width + N :] = other_ref[...].astype(BF16).astype(F32)
    before = convolve(buffer, kernel_ref, 0, buffer.shape[1])
    low_ref[...] = (before * sigmoid(before)).astype(BF16)
    dt, _, total, total_t = block_steps(raw, head_ref)
    state_ref[0] = state[...]
    odd = odd_ref[0, 0] == 1
    own, other = low_ref[:, width : width + N], low_ref[:, width + N : width + 2 * N]
    inject, readout = jnp.where(odd, other, own), jnp.where(odd, own, other)
    scores = dot_on(readout, inject, 1, 1)
    mask = order_mask(False)
    half = first_half(BLOCK)
    skip = over_heads(head_ref[2:3, :])
    squares = []
    for pair in range(width // (2 * P_SIZE)):
        cols = slice(pair * 2 * P_SIZE, (pair + 1) * 2 * P_SIZE)
        x = low_ref[:, cols].astype(F32)
        total_p = over_pair(total, pair)
        scaled = x * over_pair(dt, pair)
        scaled_two = split(scaled)
        local = []
        for head in (2 * pair, 2 * pair + 1):
            gap = total[:, head : head + 1] - total_t[head : head + 1, :]
            mixing = jnp.exp(jnp.where(mask, gap, -1e30)) * scores
            local.append(dot_three(split(mixing), scaled_two, 1, 0))
        held = state[:, cols]
        held_two = split(held)
        carried = jnp.exp(total_p) * (dot_on(readout, held_two[0], 1, 0) + dot_on(readout, held_two[1], 1, 0))
        ssd = jnp.where(half, local[0], local[1]) + carried + skip[:, cols] * x
        ssd_ref[:, cols] = ssd
        moved = split(scaled * jnp.exp(total_p[BLOCK - 1 : BLOCK, :] - total_p))
        state[:, cols] = held * jnp.exp(total_p[BLOCK - 1 : BLOCK, :]) + (
            dot_on(inject, moved[0], 0, 0) + dot_on(inject, moved[1], 0, 0)
        )
        gate_pre = gate_ref[:, cols]
        gated = ssd * (gate_pre * sigmoid(gate_pre))
        squares.append((gated * gated, gated * (up_ref[:, cols] * gain_ref[0:1, cols])))
    ones = jnp.ones((8, 2 * P_SIZE), F32)
    square = functools.reduce(jnp.add, [s[0] for s in squares])
    cross = functools.reduce(jnp.add, [s[1] for s in squares])
    sums_ref[0:1, :] = dot_on(ones, square, 1, 1, HIGH)[0:1, :]
    sums_ref[1:2, :] = dot_on(ones, cross, 1, 1, HIGH)[0:1, :]


def proj_specs(width, index):
    narrow = lambda place: pl.BlockSpec((BLOCK, N), lambda i: (index(i), 2 * width // N + place))
    return [
        pl.BlockSpec(memory_space=pltpu.SMEM),
        pl.BlockSpec((BLOCK, width), lambda i: (index(i), 0)),
        pl.BlockSpec((BLOCK, width), lambda i: (index(i), 1)),
        narrow(0),
        narrow(1),
        narrow(2),
    ]


def mixer_forward(odd, proj, grad_gated, kernel, heads, gain):
    length, width = grad_gated.shape
    wide = width + 2 * N
    count = length // BLOCK
    rows = lambda i: (i, 0)
    whole = lambda i: (0, 0)
    return pl.pallas_call(
        forward_body,
        grid=(count,),
        in_specs=proj_specs(width, lambda i: i)
        + [
            pl.BlockSpec((BLOCK, width), rows),
            pl.BlockSpec(kernel.shape, whole),
            pl.BlockSpec(heads.shape, whole),
            pl.BlockSpec(gain.shape, whole),
        ],
        out_specs=[
            pl.BlockSpec((BLOCK, wide), rows),
            pl.BlockSpec((BLOCK, width), rows),
            pl.BlockSpec((1, N, width), lambda i: (i, 0, 0)),
            pl.BlockSpec((2, BLOCK), lambda i: (0, i)),
        ],
        out_shape=[
            jax.ShapeDtypeStruct((length, wide), BF16),
            jax.ShapeDtypeStruct((length, width), F32),
            jax.ShapeDtypeStruct((count, N, width), F32),
            jax.ShapeDtypeStruct((2, length), F32),
        ],
        scratch_shapes=[pltpu.VMEM((N, width), F32), pltpu.VMEM((BLOCK + EDGE, wide), F32)],
        compiler_params=pltpu.CompilerParams(vmem_limit_bytes=48 << 20),
        name="mixer_forward",
    )(odd, proj, proj, proj, proj, proj, grad_gated, kernel, heads, gain)


def backward_body(
    odd_ref, gate_ref, x_ref, step_ref, edge_ref, low_ref, up_ref, ssd_ref, state_ref, norm_ref, kernel_ref, head_ref, gain_ref,
    grad_ref, grad_step_ref, grad_own_ref, grad_other_ref, grad_kernel_ref, grad_head_ref, grad_gain_ref,
    adjoint, buffer, grads, next_state,
):
    width = gate_ref.shape[1]
    raw = step_ref[:, 0 : head_ref.shape[1]]
    taps = kernel_ref.shape[0] - 1
    count = pl.num_programs(0)
    step = pl.program_id(0)

    @pl.when(step == 0)
    def _():
        adjoint[...] = jnp.zeros_like(adjoint)
        next_state[...] = jnp.zeros_like(next_state)
        grads[BLOCK : BLOCK + EDGE, :] = jnp.zeros((EDGE, width), F32)
        grad_kernel_ref[...] = jnp.zeros_like(grad_kernel_ref)
        grad_head_ref[...] = jnp.zeros_like(grad_head_ref)
        grad_gain_ref[...] = jnp.zeros_like(grad_gain_ref)

    @pl.when(step > 0)
    def _():
        grads[BLOCK : BLOCK + EDGE, :] = grads[0:EDGE, :]

    last = step == count - 1
    buffer[0:EDGE, :] = jnp.where(last, 0.0, edge_ref[...].astype(BF16).astype(F32))
    buffer[EDGE : EDGE + BLOCK, :] = x_ref[...].astype(BF16).astype(F32)
    dt, decay, total, total_t = block_steps(raw, head_ref)
    odd = odd_ref[0, 0] == 1
    own, other = low_ref[:, width : width + N], low_ref[:, width + N : width + 2 * N]
    inject, readout = jnp.where(odd, other, own), jnp.where(odd, own, other)
    scores_t = dot_on(inject, readout, 1, 1)
    mask_t = order_mask(True)
    half = first_half(BLOCK)
    skip = over_heads(head_ref[2:3, :])
    inverse = norm_ref[:, 0:1]
    pull = norm_ref[:, 1:2]
    grad_scores_t = jnp.zeros((BLOCK, BLOCK), F32)
    grad_inject = jnp.zeros((BLOCK, N), F32)
    grad_readout = jnp.zeros((BLOCK, N), F32)
    decay_parts, step_parts, skip_parts, end_parts = [], [], [], []
    for pair in range(width // (2 * P_SIZE)):
        cols = slice(pair * 2 * P_SIZE, (pair + 1) * 2 * P_SIZE)
        x = low_ref[:, cols].astype(F32)
        gate_pre = gate_ref[:, cols]
        ssd = ssd_ref[:, cols]
        sig = sigmoid(gate_pre)
        gate = gate_pre * sig
        up = up_ref[:, cols]
        gated = ssd * gate
        grad_gain_ref[0:1, cols] += jnp.sum(up * gated * inverse, axis=0, keepdims=True)
        grad_pre = inverse * (up * gain_ref[0:1, cols]) - gated * pull
        grad_ref[:, cols] = (grad_pre * ssd * (sig * (1.0 + gate_pre * (1.0 - sig)))).astype(BF16)
        grad_ssd = grad_pre * gate
        grad_two = split(grad_ssd)
        total_p = over_pair(total, pair)
        dt_p = over_pair(dt, pair)
        to_end = jnp.exp(total_p[BLOCK - 1 : BLOCK, :] - total_p)
        scaled = x * dt_p
        scaled_two = split(scaled)
        local = []
        for index, head in enumerate((2 * pair, 2 * pair + 1)):
            gap = total_t[head : head + 1, :] - total[:, head : head + 1]
            decays = jnp.exp(jnp.where(mask_t, gap, -1e30))
            own = half if index == 0 else jnp.logical_not(half)
            mine = [jnp.where(own, part, jnp.zeros_like(part)) for part in grad_two]
            grad_scores_t += decays * dot_three(scaled_two, mine, 1, 1)
            local.append(dot_three(split(decays * scores_t), grad_two, 1, 0))
        local = jnp.where(half, local[0], local[1])
        lam = adjoint[:, cols]
        lam_two = split(lam)
        held = state_ref[0, :, cols]
        far = dot_on(inject, lam_two[0], 1, 0) + dot_on(inject, lam_two[1], 1, 0)
        moved = scaled * to_end
        grad_inject += dot_three(split(moved), lam_two, 1, 1)
        rising = split(grad_ssd * jnp.exp(total_p))
        grad_readout += dot_three(rising, split(held), 1, 1)
        end_parts.append(jnp.sum(lam * next_state[:, cols], axis=0, keepdims=True))
        adjoint[:, cols] = lam * jnp.exp(total_p[BLOCK - 1 : BLOCK, :]) + (
            dot_on(readout, rising[0], 0, 0) + dot_on(readout, rising[1], 0, 0)
        )
        next_state[:, cols] = held
        pure = ssd - skip[:, cols] * x
        decay_parts.append(grad_ssd * pure - scaled * local - moved * far)
        grad_scaled = local + to_end * far
        step_parts.append(x * grad_scaled)
        skip_parts.append(jnp.sum(grad_ssd * x, axis=0, keepdims=True))
        grad_x = dt_p * grad_scaled + skip[:, cols] * grad_ssd
        before = convolve(buffer, kernel_ref, pair * 2 * P_SIZE, 2 * P_SIZE)
        sig = sigmoid(before)
        grads[0:BLOCK, cols] = grad_x * (sig * (1.0 + before * (1.0 - sig)))
    row_grads = head_sums(jnp.concatenate(decay_parts, axis=1))
    upper = order_mask(True).astype(F32)
    ends = head_sums(jnp.concatenate(end_parts, axis=1))
    grad_log = dot_on(upper, row_grads, 1, 0, HIGH) + ends
    grad_dt = head_sums(jnp.concatenate(step_parts, axis=1)) + decay * grad_log
    grad_raw = grad_dt * sigmoid(raw + head_ref[0:1, :])
    grad_step_ref[...] = jnp.zeros((BLOCK, N), BF16)
    grad_step_ref[:, 0 : grad_raw.shape[1]] = grad_raw.astype(BF16)
    grad_head_ref[0:1, :] += jnp.sum(grad_raw, axis=0, keepdims=True)
    grad_head_ref[1:2, :] += decay * jnp.sum(dt * grad_log, axis=0, keepdims=True)
    grad_head_ref[2:3, :] += head_sums(jnp.concatenate(skip_parts, axis=1))
    scores_two = split(grad_scores_t)
    grad_inject = grad_inject + dot_two(scores_two, readout, 1, 0)
    grad_readout = grad_readout + dot_two(scores_two, inject, 0, 0)
    grad_own_ref[...] = jnp.where(odd, grad_readout, grad_inject)
    grad_other_ref[...] = jnp.where(odd, grad_inject, grad_readout)
    grad_ref[:, width : 2 * width] = convolve_back(buffer, grads, kernel_ref, grad_kernel_ref)


def convolve_back(buffer, grads, kernel_ref, grad_kernel_ref):
    taps = kernel_ref.shape[0] - 1
    width = grads.shape[1]
    here = grads[0:BLOCK, :]
    grad_kernel_ref[taps : taps + 1, :] += jnp.sum(here, axis=0, keepdims=True)
    total = jnp.zeros((BLOCK, width), F32)
    for tap in range(taps):
        low = EDGE - taps + 1 + tap
        grad_kernel_ref[tap : tap + 1, :] += jnp.sum(here * buffer[low : low + BLOCK, :], axis=0, keepdims=True)
        ahead = taps - 1 - tap
        total = total + kernel_ref[tap : tap + 1, 0:width] * grads[ahead : ahead + BLOCK, :]
    return total.astype(BF16)


def mixer_backward(odd, proj, low, grad_gated, ssd, states, norms, kernel, heads, gain):
    length, width = grad_gated.shape
    wide = width + 2 * N
    count = length // BLOCK
    place = lambda i: count - 1 - i
    back = lambda i: (place(i), 0)
    edge = lambda i: jnp.maximum(place(i) * (BLOCK // EDGE) - 1, 0)
    whole = lambda i: (0, 0)
    specs = proj_specs(width, place)
    return pl.pallas_call(
        backward_body,
        grid=(count,),
        in_specs=specs[:3]
        + [
            specs[4],
            pl.BlockSpec((EDGE, width), lambda i: (edge(i), 1)),
            pl.BlockSpec((BLOCK, wide), back),
            pl.BlockSpec((BLOCK, width), back),
            pl.BlockSpec((BLOCK, width), back),
            pl.BlockSpec((1, N, width), lambda i: (place(i), 0, 0)),
            pl.BlockSpec((BLOCK, norms.shape[1]), back),
            pl.BlockSpec(kernel.shape, whole),
            pl.BlockSpec(heads.shape, whole),
            pl.BlockSpec(gain.shape, whole),
        ],
        out_specs=[
            pl.BlockSpec((BLOCK, 2 * width), back),
            pl.BlockSpec((BLOCK, N), back),
            pl.BlockSpec((BLOCK, N), back),
            pl.BlockSpec((BLOCK, N), back),
            pl.BlockSpec((kernel.shape[0], width), whole),
            pl.BlockSpec(heads.shape, whole),
            pl.BlockSpec(gain.shape, whole),
        ],
        out_shape=[
            jax.ShapeDtypeStruct((length, 2 * width), BF16),
            jax.ShapeDtypeStruct((length, N), BF16),
            jax.ShapeDtypeStruct((length, N), F32),
            jax.ShapeDtypeStruct((length, N), F32),
            jax.ShapeDtypeStruct((kernel.shape[0], width), F32),
            jax.ShapeDtypeStruct(heads.shape, F32),
            jax.ShapeDtypeStruct(gain.shape, F32),
        ],
        scratch_shapes=[
            pltpu.VMEM((N, width), F32),
            pltpu.VMEM((BLOCK + EDGE, width), F32),
            pltpu.VMEM((BLOCK + EDGE, width), F32),
            pltpu.VMEM((N, width), F32),
        ],
        compiler_params=pltpu.CompilerParams(vmem_limit_bytes=56 << 20),
        name="mixer_backward",
    )(odd, proj, proj, proj, proj, low, grad_gated, ssd, states, norms, kernel, heads, gain)


def map_backward_body(own_ref, edge_ref, mine_ref, theirs_ref, step_ref, kernel_ref, grad_ref, grad_kernel_ref, buffer, grads):
    step = pl.program_id(0)

    @pl.when(step == 0)
    def _():
        grads[BLOCK : BLOCK + EDGE, :] = jnp.zeros((EDGE, N), F32)
        grad_kernel_ref[...] = jnp.zeros_like(grad_kernel_ref)

    @pl.when(step > 0)
    def _():
        grads[BLOCK : BLOCK + EDGE, :] = grads[0:EDGE, :]

    last = step == pl.num_programs(0) - 1
    buffer[0:EDGE, :] = jnp.where(last, 0.0, edge_ref[...].astype(BF16).astype(F32))
    buffer[EDGE : EDGE + BLOCK, :] = own_ref[...].astype(BF16).astype(F32)
    before = convolve(buffer, kernel_ref, 0, N)
    sig = sigmoid(before)
    grads[0:BLOCK, :] = (mine_ref[...] + theirs_ref[...]) * (sig * (1.0 + before * (1.0 - sig)))
    grad_ref[:, 0:N] = convolve_back(buffer, grads, kernel_ref, grad_kernel_ref)
    grad_ref[:, N : 2 * N] = step_ref[...]


def map_backward(proj, mine, theirs, steps, kernel, column):
    length = mine.shape[0]
    count = length // BLOCK
    place = lambda i: count - 1 - i
    edge = lambda i: jnp.maximum(place(i) * (BLOCK // EDGE) - 1, 0)
    back = lambda i: (place(i), 0)
    whole = lambda i: (0, 0)
    narrow = pl.BlockSpec((BLOCK, N), back)
    return pl.pallas_call(
        map_backward_body,
        grid=(count,),
        in_specs=[
            pl.BlockSpec((BLOCK, N), lambda i: (place(i), column // N)),
            pl.BlockSpec((EDGE, N), lambda i: (edge(i), column // N)),
            narrow,
            narrow,
            narrow,
            pl.BlockSpec(kernel.shape, whole),
        ],
        out_specs=[pl.BlockSpec((BLOCK, 2 * N), back), pl.BlockSpec(kernel.shape, whole)],
        out_shape=[jax.ShapeDtypeStruct((length, 2 * N), BF16), jax.ShapeDtypeStruct(kernel.shape, F32)],
        scratch_shapes=[pltpu.VMEM((BLOCK + EDGE, N), F32), pltpu.VMEM((BLOCK + EDGE, N), F32)],
        name="map_backward",
    )(proj, proj, mine, theirs, steps, kernel)


def remote(src, dst, send, recv, device):
    return pltpu.make_async_remote_copy(
        src_ref=src, dst_ref=dst, send_sem=send, recv_sem=recv, device_id=device, device_id_type=MESH
    )


def gather_body(order, sizes, parts, *refs):
    nctx, ndp, ntp = sizes
    ntok, nin, nw = 2, parts[-1][0] + 1, parts[-1][2] + 1
    toks, weights = refs[:ntok], refs[ntok : ntok + nin]
    tok_outs = refs[ntok + nin : 2 * ntok + nin]
    weight_outs = refs[2 * ntok + nin : 2 * ntok + nin + nw]
    z_send, z_recv, t_send, t_recv, w_send, w_recv, x_send, x_recv, own = refs[2 * ntok + nin + nw :]
    c, d, t = lax.axis_index("ctx"), lax.axis_index("dp"), lax.axis_index("tp")
    near = t + 1 - 2 * lax.rem(t, 2)
    far = lax.rem(t + 2, ntp)
    length = toks[0].shape[0]
    part = length // ntp

    barrier = pltpu.get_barrier_semaphore()
    peers = [{"ctx": lax.rem(c + s, nctx)} for s in range(1, nctx)]
    peers += [{"dp": lax.rem(d + s, ndp)} for s in range(1, ndp)]
    peers += [{"tp": near}, {"tp": far}]
    for peer in peers:
        pl.semaphore_signal(barrier, inc=1, device_id=peer, device_id_type=MESH)
    pl.semaphore_wait(barrier, len(peers))

    def piece(p, to):
        array, column, _, _, width = parts[p]
        return weights[array].at[:, pl.ds(pl.multiple_of(column(to), N), width)]

    def landing(p, block):
        _, _, out, start, width = parts[p]
        return weight_outs[out].at[d, block, :, start : start + width]

    def of(out):
        return [p for p in range(len(parts)) if parts[p][2] == out]

    def rows(a, block, quarter):
        return tok_outs[a].at[pl.ds(pl.multiple_of(block * length + quarter * part, 16), part), :]

    def hop(a, j, side):
        block = c - j if side == 0 else c + j
        to = c + 1 if side == 0 else c - 1
        valid = (block >= 0) & (to < nctx) if side == 0 else (block < nctx) & (to >= 0)
        safe = jnp.clip(block, 0, nctx - 1)
        source = toks[a].at[pl.ds(pl.multiple_of(t * part, 16), part), :] if j == 0 else rows(a, safe, t)
        copy = remote(source, rows(a, safe, t), z_send.at[a, j, side], z_recv.at[a, safe], {"ctx": jnp.clip(to, 0, nctx - 1)})
        return valid, copy

    def arrival(j, side):
        block = c - 1 - j if side == 0 else c + 1 + j
        valid = block >= 0 if side == 0 else block < nctx
        return valid, jnp.clip(block, 0, nctx - 1)

    def tp_copy(a, block, kind):
        quarter = t if kind < 2 else far
        view = rows(a, block, quarter)
        return remote(view, view, t_send.at[a, block, kind], t_recv.at[a, block, kind], {"tp": far if kind == 0 else near})

    def tp_arrival(a, block, kind):
        quarter = far if kind == 0 else (near if kind == 1 else lax.rem(near + 2, ntp))
        view = rows(a, block, quarter)
        return remote(view, view, t_send.at[a, block, kind], t_recv.at[a, block, kind], {"tp": near})

    def w_copy(p, s):
        to = lax.rem(c + s, nctx)
        return remote(piece(p, to), landing(p, c), w_send.at[p, s], w_recv.at[p, s], {"ctx": to})

    def w_arrival(p, s):
        view = landing(p, lax.rem(c - s + nctx, nctx))
        return remote(view, view, w_send.at[p, s], w_recv.at[p, s], {"ctx": c})

    def x_copy(a, s, e):
        view = weight_outs[a].at[d, lax.rem(c - s + nctx, nctx)]
        return remote(view, view, x_send.at[a, s, e], x_recv.at[a, s, e], {"dp": lax.rem(d + e, ndp)})

    def x_arrival(a, s, e):
        view = weight_outs[a].at[lax.rem(d - e + ndp, ndp), lax.rem(c - s + nctx, nctx)]
        return remote(view, view, x_send.at[a, s, e], x_recv.at[a, s, e], {"dp": d})

    def own_tok(a):
        return pltpu.make_async_copy(toks[a], tok_outs[a].at[pl.ds(pl.multiple_of(c * length, 16), length), :], own.at[a])

    def own_piece(p):
        return pltpu.make_async_copy(piece(p, c), landing(p, c), own.at[ntok + p])

    def launch(step):
        kind, a, j = step
        if kind == "tok":
            for side in (0, 1):
                valid, copy = hop(a, j, side)

                @pl.when(valid)
                def _():
                    copy.start()
        else:
            for p in of(a):
                w_copy(p, j).start()

    def settle(step):
        kind, a, j = step
        if kind == "tok":
            for side in (0, 1):
                valid, block = arrival(j, side)

                @pl.when(valid)
                def _():
                    view = rows(a, block, t)
                    remote(view, view, z_send.at[a, j, side], z_recv.at[a, block], {"ctx": c}).wait_recv()
                    tp_copy(a, block, 0).start()
                    tp_copy(a, block, 1).start()
        else:
            for p in of(a):
                w_arrival(p, j).wait_recv()
            for e in range(1, ndp):
                x_copy(a, j, e).start()

    def settle_far(step):
        kind, a, j = step
        if kind == "tok":
            for side in (0, 1):
                valid, block = arrival(j, side)

                @pl.when(valid)
                def _():
                    tp_arrival(a, block, 0).wait_recv()
                    tp_copy(a, block, 2).start()

    for step in order[:DEPTH]:
        launch(step)
    for p in range(len(parts)):
        own_piece(p).start()
    for p in range(len(parts)):
        own_piece(p).wait()
    for a in range(nw):
        for e in range(1, ndp):
            x_copy(a, 0, e).start()
    for a in range(ntok):
        own_tok(a).start()
    for index, step in enumerate(order):
        settle(step)
        if index + DEPTH < len(order):
            launch(order[index + DEPTH])
        if index >= 2:
            settle_far(order[index - 2])
    for step in order[-2:]:
        settle_far(step)
    for kind, a, j in order:
        if kind == "tok":
            for side in (0, 1):
                valid, copy = hop(a, j, side)
                here, block = arrival(j, side)

                @pl.when(valid)
                def _():
                    copy.wait_send()

                @pl.when(here)
                def _():
                    for part_kind in range(3):
                        tp_copy(a, block, part_kind).wait_send()
                    tp_arrival(a, block, 1).wait_recv()
                    tp_arrival(a, block, 2).wait_recv()
        else:
            for p in of(a):
                w_copy(p, j).wait_send()
            for e in range(1, ndp):
                x_copy(a, j, e).wait_send()
                x_arrival(a, j, e).wait_recv()
    for a in range(nw):
        for e in range(1, ndp):
            x_copy(a, 0, e).wait_send()
            x_arrival(a, 0, e).wait_recv()
    for a in range(ntok):
        own_tok(a).wait()


def gather_all(toks, weights, parts, sizes):
    nctx, ndp, ntp = sizes
    turns = range(1, nctx)
    nw = parts[-1][2] + 1
    widths = [sum(p[4] for p in parts if p[2] == out) for out in range(nw)]
    shard_rows = weights[0].shape[0]
    tok = lambda a, j: [("tok", a, j)] if j < nctx - 1 else []
    per = lambda a: [("w", a, s) for s in turns]
    order = tok(0, 0) + tok(1, 0) + per(0) + tok(0, 1) + tok(1, 1) + per(1)[:1] + tok(0, 2) + tok(1, 2) + per(1)[1:]
    any_space = pl.BlockSpec(memory_space=pl.ANY)
    length, model = toks[0].shape
    out_shape = [jax.ShapeDtypeStruct((nctx * length, model), BF16) for _ in toks]
    out_shape += [jax.ShapeDtypeStruct((ndp, nctx, shard_rows, width), BF16) for width in widths]
    dma = pltpu.SemaphoreType.DMA
    return pl.pallas_call(
        functools.partial(gather_body, order, sizes, parts),
        out_shape=out_shape,
        in_specs=[any_space] * (len(toks) + len(weights)),
        out_specs=[any_space] * len(out_shape),
        scratch_shapes=[
            dma((2, nctx, 2)), dma((2, nctx)), dma((2, nctx, 3)), dma((2, nctx, 3)),
            dma((len(parts), nctx)), dma((len(parts), nctx)), dma((nw, nctx, ndp)), dma((nw, nctx, ndp)), dma((2 + len(parts),)),
        ],
        compiler_params=pltpu.CompilerParams(collective_id=1, has_side_effects=True),
        name="gather_inputs",
    )(*toks, *weights)


def add_rows(target, sources, rows, step):
    def some(index, _):
        here = pl.ds(pl.multiple_of(index * step, step), step)
        total = sources[0][here, :].astype(F32)
        for source in sources[1:]:
            total = total + source[here, :].astype(F32)
        target[here, :] = total.astype(target.dtype)
        return 0

    lax.fori_loop(0, rows // step, some, 0)


def output_body(order, sizes, nw, parts, *refs):
    nctx, ndp, ntp = sizes
    nout = len(parts)
    partial, small, grads = refs[0], refs[1], refs[2 : 2 + nw]
    sum_out, small_out, grad_outs = refs[2 + nw], refs[3 + nw], refs[4 + nw : 4 + nw + nout]
    rest = refs[4 + nw + nout :]
    (near_in, far_out, far_in, z_out, z_in, held, acc, done) = rest[:8]
    x_ins, x_sums = rest[8 : 8 + nw], rest[8 + nw : 8 + 2 * nw]
    (near_s, near_r, far_s, far_r, z_s, z_r, x_s, x_r, w_s, w_r, fin_s, fin_r, local, small_s, small_r) = rest[8 + 2 * nw :]
    c, d, t = lax.axis_index("ctx"), lax.axis_index("dp"), lax.axis_index("tp")
    near = t + 1 - 2 * lax.rem(t, 2)
    far = lax.rem(t + 2, ntp)
    far_near = lax.rem(near + 2, ntp)
    length = sum_out.shape[0]
    part = length // ntp
    wrap = lambda i: lax.rem(i + nctx, nctx)

    barrier = pltpu.get_barrier_semaphore()
    others = [(e, s) for e in range(ndp) for s in range(nctx) if e or s]
    place = lambda e, s: {"dp": lax.rem(d + e, ndp), "ctx": lax.rem(c + s, nctx)}
    peers = [place(e, s) for e, s in others] + [{"tp": near}, {"tp": far}]
    for peer in peers:
        pl.semaphore_signal(barrier, inc=1, device_id=peer, device_id_type=MESH)
    pl.semaphore_wait(barrier, len(peers))

    def small_copy(e, s):
        return remote(small, small_out.at[d, c], small_s.at[e, s], small_r.at[e, s], place(e, s))

    def small_arrival(e, s):
        view = small_out.at[lax.rem(d - e + ndp, ndp), wrap(c - s)]
        return remote(view, view, small_s.at[e, s], small_r.at[e, s], place(e, s))

    def rows(s, quarter):
        return partial.at[pl.ds(pl.multiple_of(wrap(c + s) * length + quarter * part, 16), part), :]

    def near_copy(s, slot):
        return remote(rows(s, near if slot == 0 else far_near), near_in.at[s, slot], near_s.at[s, slot], near_r.at[s, slot], {"tp": near})

    def far_copy(s):
        return remote(far_out.at[s], far_in.at[s], far_s.at[s], far_r.at[s], {"tp": far})

    def z_copy(s):
        return remote(z_out.at[s], z_in.at[s], z_s.at[s], z_r.at[s], {"ctx": wrap(c + s)})

    def x_copy(a, s, e):
        to = lax.rem(d + e, ndp)
        return remote(grads[a].at[to, wrap(c + s)], x_ins[a].at[s, e - 1], x_s.at[a, s, e], x_r.at[a, s, e], {"dp": to})

    def piece(p, s):
        a, start, width, _, _ = parts[p]
        return x_sums[a].at[s, :, start : start + width]

    def landing(p, block):
        _, _, width, out, split_columns = parts[p]
        if split_columns:
            return grad_outs[out].at[:, pl.ds(pl.multiple_of(block * width, N), width)]
        return grad_outs[out].at[block]

    def w_copy(p, s):
        return remote(piece(p, s), landing(p, c), w_s.at[p, s], w_r.at[p, s], {"ctx": wrap(c + s)})

    def w_arrival(p, s):
        view = landing(p, wrap(c - s))
        return remote(view, view, w_s.at[p, s], w_r.at[p, s], {"ctx": c})

    def w_own(p):
        return pltpu.make_async_copy(piece(p, 0), landing(p, c), local.at[2 + nw * nctx + p])

    def load(s, quarter, slot):
        return pltpu.make_async_copy(rows(s, quarter), held.at[slot], local.at[slot])

    def load_grad(a, s):
        return pltpu.make_async_copy(grads[a].at[d, wrap(c + s)], x_sums[a].at[s], local.at[2 + a * nctx + s])

    def start_x(s):
        for a in range(nw):
            for e in range(1, ndp):
                x_copy(a, s, e).start()

    def near_sum(s):
        load(s, far, 0).start()
        near_copy(s, 1).wait_recv()
        load(s, far, 0).wait()
        add_rows(far_out.at[s], [held.at[0], near_in.at[s, 1]], part, 16)
        far_copy(s).start()

    def far_sum(s):
        load(s, t, 1).start()
        near_copy(s, 0).wait_recv()
        far_copy(s).wait_recv()
        load(s, t, 1).wait()
        add_rows(acc if s == 0 else z_out.at[s], [held.at[1], near_in.at[s, 0], far_in.at[s]], part, 16)
        if s > 0:
            z_copy(s).start()

    def grad_sum(s):
        for a in range(nw):
            load_grad(a, s).wait()
            for e in range(1, ndp):
                x_copy(a, s, e).wait_recv()
            add_rows(x_sums[a].at[s], [x_sums[a].at[s]] + [x_ins[a].at[s, e - 1] for e in range(1, ndp)], x_sums[a].shape[1], 16)
        for p in range(nout):
            if s > 0:
                w_copy(p, s).start()
            else:
                w_own(p).start()

    for s in order:
        for slot in (1, 0):
            near_copy(s, slot).start()
        for a in range(nw):
            load_grad(a, s).start()
    ahead = 2
    for s in order[:ahead]:
        start_x(s)
    for e, s in others:
        small_copy(e, s).start()
    small_own = pltpu.make_async_copy(small, small_out.at[d, c], local.at[2 + nw * nctx + nout])
    small_own.start()
    for s in order[:ahead]:
        near_sum(s)
    for index, s in enumerate(order):
        far_sum(s)
        if index + ahead < nctx:
            near_sum(order[index + ahead])
        grad_sum(s)
        if index + ahead < nctx:
            start_x(order[index + ahead])
    for s in range(1, nctx):
        z_copy(s).wait_recv()
    add_rows(done, [acc] + [z_in.at[s] for s in range(1, nctx)], part, 16)

    def mine(quarter):
        return sum_out.at[pl.ds(pl.multiple_of(quarter * part, 16), part), :]

    finals = [
        remote(done, mine(t), fin_s.at[0], fin_r.at[0], {"tp": far}),
        remote(done, mine(t), fin_s.at[1], fin_r.at[1], {"tp": near}),
        remote(mine(far), mine(far), fin_s.at[2], fin_r.at[2], {"tp": near}),
    ]
    keep = pltpu.make_async_copy(done, mine(t), local.at[0])
    finals[0].start()
    finals[1].start()
    keep.start()
    remote(mine(far), mine(far), fin_s.at[0], fin_r.at[0], {"tp": far}).wait_recv()
    finals[2].start()
    remote(mine(near), mine(near), fin_s.at[1], fin_r.at[1], {"tp": near}).wait_recv()
    remote(mine(far_near), mine(far_near), fin_s.at[2], fin_r.at[2], {"tp": near}).wait_recv()
    keep.wait()
    for copy in finals:
        copy.wait_send()
    for s in order:
        for slot in (1, 0):
            near_copy(s, slot).wait_send()
        far_copy(s).wait_send()
        for a in range(nw):
            for e in range(1, ndp):
                x_copy(a, s, e).wait_send()
        for p in range(nout):
            if s > 0:
                w_copy(p, s).wait_send()
                w_arrival(p, s).wait_recv()
            else:
                w_own(p).wait()
        if s > 0:
            z_copy(s).wait_send()
    for e, s in others:
        small_copy(e, s).wait_send()
        small_arrival(e, s).wait_recv()
    small_own.wait()


def return_all(partial, small, grads, parts, sizes):
    nctx, ndp, ntp = sizes
    length = partial.shape[0] // nctx
    part, model = length // ntp, partial.shape[1]
    nw, nout = len(grads), len(parts)
    outs = [(nctx,) + grads[p[0]].shape[2:] if not p[4] else (grads[0].shape[2], nctx * p[2]) for p in parts]
    order = [nctx // 2] + [s for s in range(1, nctx) if s != nctx // 2] + [0]
    any_space = pl.BlockSpec(memory_space=pl.ANY)
    dma = pltpu.SemaphoreType.DMA
    vmem = pltpu.VMEM
    strip = lambda *lead: vmem(lead + (part, model), BF16)
    return pl.pallas_call(
        functools.partial(output_body, order, sizes, nw, parts),
        out_shape=[jax.ShapeDtypeStruct((length, model), BF16), jax.ShapeDtypeStruct((ndp, nctx) + small.shape, F32)]
        + [jax.ShapeDtypeStruct(out, BF16) for out in outs],
        in_specs=[any_space] * (2 + nw),
        out_specs=[any_space] * (2 + nout),
        scratch_shapes=[
            strip(nctx, 2), strip(nctx), strip(nctx), strip(nctx), strip(nctx), strip(2), vmem((part, model), F32), strip(),
        ]
        + [vmem((nctx, max(ndp - 1, 1)) + g.shape[2:], BF16) for g in grads]
        + [vmem((nctx,) + g.shape[2:], BF16) for g in grads]
        + [
            dma((nctx, 2)), dma((nctx, 2)), dma((nctx,)), dma((nctx,)), dma((nctx,)), dma((nctx,)),
            dma((nw, nctx, ndp)), dma((nw, nctx, ndp)), dma((nout, nctx)), dma((nout, nctx)), dma((3,)), dma((3,)),
            dma((2 + nw * nctx + nout + 1,)), dma((ndp, nctx)), dma((ndp, nctx)),
        ],
        compiler_params=pltpu.CompilerParams(collective_id=2, has_side_effects=True, vmem_limit_bytes=60 << 20),
        name="return_outputs",
    )(partial, small, *grads)


def small_body(sizes, value, gathered, send, recv, own):
    nctx, ndp = sizes
    c, d = lax.axis_index("ctx"), lax.axis_index("dp")
    others = [(e, s) for e in range(ndp) for s in range(nctx) if e or s]
    place = lambda e, s: {"dp": lax.rem(d + e, ndp), "ctx": lax.rem(c + s, nctx)}
    barrier = pltpu.get_barrier_semaphore()
    for e, s in others:
        pl.semaphore_signal(barrier, inc=1, device_id=place(e, s), device_id_type=MESH)
    pl.semaphore_wait(barrier, len(others))
    keep = pltpu.make_async_copy(value, gathered.at[d, c], own)
    keep.start()
    for e, s in others:
        remote(value, gathered.at[d, c], send.at[e, s], recv.at[e, s], place(e, s)).start()
    for e, s in others:
        view = gathered.at[lax.rem(d - e + ndp, ndp), lax.rem(c - s + nctx, nctx)]
        remote(view, view, send.at[e, s], recv.at[e, s], place(e, s)).wait_recv()
        remote(value, gathered.at[d, c], send.at[e, s], recv.at[e, s], place(e, s)).wait_send()
    keep.wait()


def gather_small(value, sizes):
    nctx, ndp = sizes
    vmem = pl.BlockSpec(memory_space=pltpu.VMEM)
    dma = pltpu.SemaphoreType.DMA
    return pl.pallas_call(
        functools.partial(small_body, sizes),
        out_shape=jax.ShapeDtypeStruct((ndp, nctx) + value.shape, F32),
        in_specs=[vmem],
        out_specs=vmem,
        scratch_shapes=[dma((ndp, nctx)), dma((ndp, nctx)), dma],
        compiler_params=pltpu.CompilerParams(collective_id=3, has_side_effects=True),
        name="gather_small",
    )(value)


def dot_last(left_side, right_side):
    return lax.dot_general(left_side, right_side, (((1,), (1,)), ((), ())), preferred_element_type=F32)


def dot_first(left_side, right_side):
    return lax.dot_general(left_side, right_side, (((0,), (0,)), ((), ())), preferred_element_type=F32)


def sum_rows(partial):
    return lax.psum_scatter(partial.astype(BF16), ("ctx", "tp"), scatter_dimension=0, tiled=True).astype(F32)


def shards(tokens, norm_gain, zx_weight, bc_weight, dt_weight, conv_x, conv_bc, head_params, gate_gain, out_weight, cotangent):
    seq_count, length, model_width = tokens.shape
    assert seq_count == 1
    nctx, ntp, ndp = lax.axis_size("ctx"), lax.axis_size("tp"), lax.axis_size("dp")
    ctx = lax.axis_index("ctx")
    rows = dt_weight.shape[0]
    inner = conv_x.shape[1]
    pair_width = bc_weight.shape[2]
    groups = pair_width // N
    share = nctx // groups
    assert share == 2 and groups * share == nctx
    width = inner // nctx
    heads = dt_weight.shape[1] // nctx
    taps = conv_x.shape[0] - 1
    group_width = inner // groups

    def mine(value):
        return lax.dynamic_index_in_dim(value, ctx, 0, False)

    def partner(value):
        return lax.ppermute(value, "ctx", [(i, i ^ 1) for i in range(nctx)])

    hidden = tokens.astype(F32).reshape(length, model_width)
    cot = cotangent.reshape(length, model_width)
    rscale = lax.rsqrt(jnp.mean(hidden * hidden, axis=-1, keepdims=True) + EPS)
    normed = (hidden * rscale * norm_gain).astype(BF16)

    steps = jnp.pad(dt_weight.reshape(rows, nctx, heads), ((0, 0), (0, 0), (0, N - heads))).reshape(rows, nctx * N)
    map_at = lambda which: lambda to: (lax.rem(to + which, 2) * groups + to // share) * N
    parts = (
        (0, lambda to: to * width, 0, 0, width),
        (0, lambda to: inner + to * width, 0, width, width),
        (1, map_at(0), 0, 2 * width, N),
        (2, lambda to: to * N, 0, 2 * width + N, N),
        (1, map_at(1), 0, 2 * width + 2 * N, N),
        (3, lambda to: to * width, 1, 0, width),
    )
    sources = (zx_weight.reshape(rows, 2 * inner), bc_weight.reshape(rows, 2 * pair_width), steps, out_weight)
    normed_all, cot_all, weight_in, weight_out = gather_all((normed, cot), sources, parts, (nctx, ndp, ntp))
    weight_in = weight_in.reshape(model_width, -1)
    weight_out = weight_out.reshape(model_width, width)

    grad_gated = jnp.dot(cot_all, weight_out, preferred_element_type=F32)
    proj = jnp.dot(normed_all, weight_in, preferred_element_type=F32)
    odd = lax.rem(ctx, 2)
    kernel_x = mine(conv_x.reshape(taps + 1, nctx, width).transpose(1, 0, 2))
    kernel_maps = conv_bc.reshape(taps + 1, 2, groups, N).transpose(2, 1, 0, 3).reshape(nctx, taps + 1, N)
    kernel_own = mine(kernel_maps)
    kernel_other = lax.dynamic_index_in_dim(kernel_maps, ctx + 1 - 2 * odd, 0, False)
    kernel = jnp.concatenate([kernel_x, kernel_own, kernel_other], axis=1)
    odd = odd.astype(jnp.int32).reshape(1, 1)
    heads_mine = mine(head_params.reshape(3, nctx, heads).transpose(1, 0, 2))
    gain = mine(gate_gain.reshape(nctx, 1, width))
    low, ssd, states, sums = mixer_forward(odd, proj, grad_gated, kernel, heads_mine, gain)
    sums = (sums + partner(sums)) / group_width
    inverse = lax.rsqrt(sums[0] + EPS)
    norms = jnp.stack([inverse, inverse * inverse * inverse * sums[1]], axis=1)
    gate_pre = proj[:, :width]
    gated_norm = (ssd * (gate_pre * jax.nn.sigmoid(gate_pre)) * norms[:, 0:1] * gain).astype(BF16)
    branch = sum_rows(dot_last(gated_norm, weight_out))
    grad_zx, grad_steps, grad_own, grad_other, grad_kernel_x, grad_heads, gate_gain_grad = mixer_backward(
        odd, proj, low, grad_gated, ssd, states, norms, kernel, heads_mine, gain
    )
    theirs = partner(grad_other)
    grad_rest, grad_kernel_own = map_backward(proj, grad_own, theirs, grad_steps, kernel_own, 2 * width)
    grad_all = jnp.concatenate([grad_zx, grad_rest], axis=1)
    blocks = lambda grad: grad.astype(BF16).reshape(ndp, nctx, rows, -1)
    weight_grads = (
        blocks(dot_first(normed_all, grad_zx)),
        blocks(dot_first(normed_all, grad_rest)),
        blocks(dot_first(cot_all, gated_norm)),
    )
    partial = dot_last(grad_all, weight_in[:, : grad_all.shape[1]]).astype(BF16)
    pieces = (grad_kernel_x, grad_kernel_own, grad_heads, gate_gain_grad)
    small = jnp.concatenate([piece.reshape(-1) for piece in pieces])
    lines = -(-small.shape[0] // (8 * N)) * 8
    small = jnp.pad(small, (0, lines * N - small.shape[0])).reshape(lines, N)
    out_parts = (
        (0, 0, width, 0, True),
        (0, width, width, 1, True),
        (1, 0, 2 * N, 2, False),
        (2, 0, width, 3, True),
    )
    grad_normed, table, back_z, back_x, back_rest, back_out = return_all(
        partial, small, weight_grads, out_parts, (nctx, ndp, ntp)
    )
    grad_normed, branch = lax.optimization_barrier((grad_normed, branch))
    part = length // ntp
    hidden_part = lax.dynamic_slice_in_dim(hidden, lax.axis_index("tp") * part, part, 0)
    mixed = lax.all_gather((hidden_part + branch).astype(BF16), "tp", axis=0, tiled=True)
    grad_normed = grad_normed.astype(F32)

    grad_hat = grad_normed * norm_gain
    norm_gain_grad = jnp.sum(grad_normed * hidden * rscale, axis=0)
    grad_hidden = rscale * grad_hat - hidden * (rscale * rscale * rscale) * jnp.mean(
        grad_hat * hidden, axis=1, keepdims=True
    )
    tokens_grad = cot.astype(F32) + grad_hidden

    zx_weight_grad = jnp.stack([back_z, back_x], axis=1).astype(F32)
    back_rest = back_rest.astype(F32)
    bc_weight_grad = back_rest[:, :, :N].reshape(groups, 2, rows, N).transpose(2, 1, 0, 3).reshape(rows, 2, groups * N)
    dt_weight_grad = back_rest[:, :, N : N + heads].transpose(1, 0, 2).reshape(rows, nctx * heads)
    out_weight_grad = back_out.astype(F32)

    table = jnp.sum(table, axis=0).reshape(nctx, lines * N)
    ends = [0]
    for piece in pieces:
        ends.append(ends[-1] + piece.size)
    kernel_x, kernel_own, head_grad, gain_grad = [table[:, a:b] for a, b in zip(ends[:-1], ends[1:])]
    conv_x_grad = kernel_x.reshape(nctx, taps + 1, width).transpose(1, 0, 2).reshape(taps + 1, inner)
    conv_bc_grad = kernel_own.reshape(groups, 2, taps + 1, N).transpose(2, 1, 0, 3).reshape(taps + 1, 2, groups * N)
    head_grad = head_grad.reshape(nctx, 3, heads).transpose(1, 0, 2).reshape(3, nctx * heads)
    gate_gain_grad = gain_grad.reshape(inner)
    norm_gain_grad = jnp.sum(gather_small(norm_gain_grad.reshape(-1, N), (nctx, ndp)), axis=(0, 1)).reshape(model_width)
    return (
        mixed.reshape(tokens.shape),
        tokens_grad.reshape(tokens.shape),
        norm_gain_grad,
        zx_weight_grad,
        bc_weight_grad,
        dt_weight_grad,
        conv_x_grad,
        conv_bc_grad,
        head_grad,
        gate_gain_grad,
        out_weight_grad,
    )


def solution(mesh):
    wide = P(("dp", "ctx"), None, "tp")
    flat = P(("dp", "ctx"), "tp")
    rows = P("dp", "ctx", None)
    return jax.shard_map(
        shards,
        mesh=mesh,
        in_specs=(rows, P(), wide, wide, flat, P(None, "tp"), P(None, None, "tp"), P(None, "tp"), P("tp"), flat, rows),
        out_specs=(rows, rows, P(), wide, wide, flat, P(None, "tp"), P(None, None, "tp"), P(None, "tp"), P("tp"), flat),
        check_vma=False,
    )
```

```python
import functools

import jax
import jax.numpy as jnp
from jax import lax
from jax.experimental import pallas as pl
from jax.experimental.pallas import tpu as pltpu
from jax.sharding import PartitionSpec as P

P_SIZE = 64
N = 128
BLOCK = 256
EDGE = 8
DEPTH = 3
MESH = pl.DeviceIdType.MESH
EPS = 1e-05
HIGH = lax.Precision.HIGHEST
F32 = jnp.float32
BF16 = jnp.bfloat16


def dot_on(left_side, right_side, left_dim, right_dim, precision=None):
    return lax.dot_general(
        left_side, right_side, (((left_dim,), (right_dim,)), ((), ())), precision=precision, preferred_element_type=F32
    )


def split(v):
    high = v.astype(BF16)
    return high, (v - high.astype(F32)).astype(BF16)


def dot_two(parts, other, part_dim, other_dim):
    return dot_on(parts[0], other, part_dim, other_dim) + dot_on(parts[1], other, part_dim, other_dim)


def dot_three(left_side, right_side, left_dim, right_dim):
    high = dot_two(left_side, right_side[0], left_dim, right_dim)
    return high + dot_on(left_side[0], right_side[1], left_dim, right_dim)


def softplus(v):
    return jnp.maximum(v, 0.0) + jnp.log1p(jnp.exp(-jnp.abs(v)))


def sigmoid(v):
    return 1.0 / (1.0 + jnp.exp(-v))


def order_mask(transposed):
    row = lax.broadcasted_iota(jnp.int32, (BLOCK, BLOCK), 0)
    col = lax.broadcasted_iota(jnp.int32, (BLOCK, BLOCK), 1)
    return row <= col if transposed else row >= col


def first_half(rows):
    return lax.broadcasted_iota(jnp.int32, (rows, 2 * P_SIZE), 1) < P_SIZE


def over_pair(value, pair):
    shape = (value.shape[0], P_SIZE * 2)
    left = jnp.broadcast_to(value[:, 2 * pair : 2 * pair + 1], shape)
    right = jnp.broadcast_to(value[:, 2 * pair + 1 : 2 * pair + 2], shape)
    return jnp.where(first_half(shape[0]), left, right)


def over_heads(value):
    return jnp.concatenate([over_pair(value, pair) for pair in range(value.shape[1] // 2)], axis=1)


def head_sums(value):
    columns = []
    for pair in range(value.shape[1] // (2 * P_SIZE)):
        part = value[:, pair * 2 * P_SIZE : (pair + 1) * 2 * P_SIZE]
        left = jnp.where(first_half(part.shape[0]), part, 0.0)
        columns += [jnp.sum(left, axis=1, keepdims=True), jnp.sum(part - left, axis=1, keepdims=True)]
    heads = len(columns)
    lane = lax.broadcasted_iota(jnp.int32, (value.shape[0], heads), 1)
    total = jnp.broadcast_to(columns[0], lane.shape)
    for head in range(1, heads):
        total = jnp.where(lane == head, columns[head], total)
    return total


def convolve(buffer, kernel_ref, start, width):
    taps = kernel_ref.shape[0] - 1
    total = kernel_ref[taps : taps + 1, start : start + width]
    for tap in range(taps):
        low = EDGE - taps + 1 + tap
        total = total + kernel_ref[tap : tap + 1, start : start + width] * buffer[low : low + BLOCK, start : start + width]
    return total


def block_steps(raw, head_ref):
    dt = softplus(raw + head_ref[0:1, :])
    decay = -jnp.exp(head_ref[1:2, :])
    log_step = dt * decay
    lower = order_mask(False).astype(F32)
    total = dot_on(lower, log_step, 1, 0, HIGH)
    total_t = dot_on(log_step, lower, 0, 1, HIGH)
    return dt, decay, total, total_t


def forward_body(
    odd_ref, gate_ref, x_ref, own_ref, step_ref, other_ref, up_ref, kernel_ref, head_ref, gain_ref,
    low_ref, ssd_ref, state_ref, sums_ref, state, buffer,
):
    width = gate_ref.shape[1]
    raw = step_ref[:, 0 : head_ref.shape[1]]
    first = pl.program_id(0) == 0

    @pl.when(first)
    def _():
        state[...] = jnp.zeros_like(state)
        buffer[0:EDGE, :] = jnp.zeros((EDGE, buffer.shape[1]), F32)

    @pl.when(jnp.logical_not(first))
    def _():
        buffer[0:EDGE, :] = buffer[BLOCK : BLOCK + EDGE, :]

    buffer[EDGE : EDGE + BLOCK, 0:width] = x_ref[...].astype(BF16).astype(F32)
    buffer[EDGE : EDGE + BLOCK, width : width + N] = own_ref[...].astype(BF16).astype(F32)
    buffer[EDGE : EDGE + BLOCK, width + N :] = other_ref[...].astype(BF16).astype(F32)
    before = convolve(buffer, kernel_ref, 0, buffer.shape[1])
    low_ref[...] = (before * sigmoid(before)).astype(BF16)
    dt, _, total, total_t = block_steps(raw, head_ref)
    state_ref[0] = state[...]
    odd = odd_ref[0, 0] == 1
    own, other = low_ref[:, width : width + N], low_ref[:, width + N : width + 2 * N]
    inject, readout = jnp.where(odd, other, own), jnp.where(odd, own, other)
    scores = dot_on(readout, inject, 1, 1)
    mask = order_mask(False)
    half = first_half(BLOCK)
    skip = over_heads(head_ref[2:3, :])
    squares = []
    for pair in range(width // (2 * P_SIZE)):
        cols = slice(pair * 2 * P_SIZE, (pair + 1) * 2 * P_SIZE)
        x = low_ref[:, cols].astype(F32)
        total_p = over_pair(total, pair)
        scaled = x * over_pair(dt, pair)
        scaled_two = split(scaled)
        local = []
        for head in (2 * pair, 2 * pair + 1):
            gap = total[:, head : head + 1] - total_t[head : head + 1, :]
            mixing = jnp.exp(jnp.where(mask, gap, -1e30)) * scores
            local.append(dot_three(split(mixing), scaled_two, 1, 0))
        held = state[:, cols]
        held_two = split(held)
        carried = jnp.exp(total_p) * (dot_on(readout, held_two[0], 1, 0) + dot_on(readout, held_two[1], 1, 0))
        ssd = jnp.where(half, local[0], local[1]) + carried + skip[:, cols] * x
        ssd_ref[:, cols] = ssd
        moved = split(scaled * jnp.exp(total_p[BLOCK - 1 : BLOCK, :] - total_p))
        state[:, cols] = held * jnp.exp(total_p[BLOCK - 1 : BLOCK, :]) + (
            dot_on(inject, moved[0], 0, 0) + dot_on(inject, moved[1], 0, 0)
        )
        gate_pre = gate_ref[:, cols]
        gated = ssd * (gate_pre * sigmoid(gate_pre))
        squares.append((gated * gated, gated * (up_ref[:, cols] * gain_ref[0:1, cols])))
    ones = jnp.ones((8, 2 * P_SIZE), F32)
    square = functools.reduce(jnp.add, [s[0] for s in squares])
    cross = functools.reduce(jnp.add, [s[1] for s in squares])
    sums_ref[0:1, :] = dot_on(ones, square, 1, 1, HIGH)[0:1, :]
    sums_ref[1:2, :] = dot_on(ones, cross, 1, 1, HIGH)[0:1, :]


def proj_specs(width, index):
    narrow = lambda place: pl.BlockSpec((BLOCK, N), lambda i: (index(i), 2 * width // N + place))
    return [
        pl.BlockSpec(memory_space=pltpu.SMEM),
        pl.BlockSpec((BLOCK, width), lambda i: (index(i), 0)),
        pl.BlockSpec((BLOCK, width), lambda i: (index(i), 1)),
        narrow(0),
        narrow(1),
        narrow(2),
    ]


def mixer_forward(odd, proj, grad_gated, kernel, heads, gain):
    length, width = grad_gated.shape
    wide = width + 2 * N
    count = length // BLOCK
    rows = lambda i: (i, 0)
    whole = lambda i: (0, 0)
    return pl.pallas_call(
        forward_body,
        grid=(count,),
        in_specs=proj_specs(width, lambda i: i)
        + [
            pl.BlockSpec((BLOCK, width), rows),
            pl.BlockSpec(kernel.shape, whole),
            pl.BlockSpec(heads.shape, whole),
            pl.BlockSpec(gain.shape, whole),
        ],
        out_specs=[
            pl.BlockSpec((BLOCK, wide), rows),
            pl.BlockSpec((BLOCK, width), rows),
            pl.BlockSpec((1, N, width), lambda i: (i, 0, 0)),
            pl.BlockSpec((2, BLOCK), lambda i: (0, i)),
        ],
        out_shape=[
            jax.ShapeDtypeStruct((length, wide), BF16),
            jax.ShapeDtypeStruct((length, width), F32),
            jax.ShapeDtypeStruct((count, N, width), F32),
            jax.ShapeDtypeStruct((2, length), F32),
        ],
        scratch_shapes=[pltpu.VMEM((N, width), F32), pltpu.VMEM((BLOCK + EDGE, wide), F32)],
        compiler_params=pltpu.CompilerParams(vmem_limit_bytes=48 << 20),
        name="mixer_forward",
    )(odd, proj, proj, proj, proj, proj, grad_gated, kernel, heads, gain)


def backward_body(
    odd_ref, gate_ref, x_ref, step_ref, edge_ref, low_ref, up_ref, ssd_ref, state_ref, norm_ref, kernel_ref, head_ref, gain_ref,
    grad_ref, grad_step_ref, grad_own_ref, grad_other_ref, grad_kernel_ref, grad_head_ref, grad_gain_ref,
    adjoint, buffer, grads, next_state,
):
    width = gate_ref.shape[1]
    raw = step_ref[:, 0 : head_ref.shape[1]]
    taps = kernel_ref.shape[0] - 1
    count = pl.num_programs(0)
    step = pl.program_id(0)

    @pl.when(step == 0)
    def _():
        adjoint[...] = jnp.zeros_like(adjoint)
        next_state[...] = jnp.zeros_like(next_state)
        grads[BLOCK : BLOCK + EDGE, :] = jnp.zeros((EDGE, width), F32)
        grad_kernel_ref[...] = jnp.zeros_like(grad_kernel_ref)
        grad_head_ref[...] = jnp.zeros_like(grad_head_ref)
        grad_gain_ref[...] = jnp.zeros_like(grad_gain_ref)

    @pl.when(step > 0)
    def _():
        grads[BLOCK : BLOCK + EDGE, :] = grads[0:EDGE, :]

    last = step == count - 1
    buffer[0:EDGE, :] = jnp.where(last, 0.0, edge_ref[...].astype(BF16).astype(F32))
    buffer[EDGE : EDGE + BLOCK, :] = x_ref[...].astype(BF16).astype(F32)
    dt, decay, total, total_t = block_steps(raw, head_ref)
    odd = odd_ref[0, 0] == 1
    own, other = low_ref[:, width : width + N], low_ref[:, width + N : width + 2 * N]
    inject, readout = jnp.where(odd, other, own), jnp.where(odd, own, other)
    scores_t = dot_on(inject, readout, 1, 1)
    mask_t = order_mask(True)
    half = first_half(BLOCK)
    skip = over_heads(head_ref[2:3, :])
    inverse = norm_ref[:, 0:1]
    pull = norm_ref[:, 1:2]
    grad_scores_t = jnp.zeros((BLOCK, BLOCK), F32)
    grad_inject = jnp.zeros((BLOCK, N), F32)
    grad_readout = jnp.zeros((BLOCK, N), F32)
    decay_parts, step_parts, skip_parts, end_parts = [], [], [], []
    for pair in range(width // (2 * P_SIZE)):
        cols = slice(pair * 2 * P_SIZE, (pair + 1) * 2 * P_SIZE)
        x = low_ref[:, cols].astype(F32)
        gate_pre = gate_ref[:, cols]
        ssd = ssd_ref[:, cols]
        sig = sigmoid(gate_pre)
        gate = gate_pre * sig
        up = up_ref[:, cols]
        gated = ssd * gate
        grad_gain_ref[0:1, cols] += jnp.sum(up * gated * inverse, axis=0, keepdims=True)
        grad_pre = inverse * (up * gain_ref[0:1, cols]) - gated * pull
        grad_ref[:, cols] = (grad_pre * ssd * (sig * (1.0 + gate_pre * (1.0 - sig)))).astype(BF16)
        grad_ssd = grad_pre * gate
        grad_two = split(grad_ssd)
        total_p = over_pair(total, pair)
        dt_p = over_pair(dt, pair)
        to_end = jnp.exp(total_p[BLOCK - 1 : BLOCK, :] - total_p)
        scaled = x * dt_p
        scaled_two = split(scaled)
        local = []
        for index, head in enumerate((2 * pair, 2 * pair + 1)):
            gap = total_t[head : head + 1, :] - total[:, head : head + 1]
            decays = jnp.exp(jnp.where(mask_t, gap, -1e30))
            own = half if index == 0 else jnp.logical_not(half)
            mine = [jnp.where(own, part, jnp.zeros_like(part)) for part in grad_two]
            grad_scores_t += decays * dot_three(scaled_two, mine, 1, 1)
            local.append(dot_three(split(decays * scores_t), grad_two, 1, 0))
        local = jnp.where(half, local[0], local[1])
        lam = adjoint[:, cols]
        lam_two = split(lam)
        held = state_ref[0, :, cols]
        far = dot_on(inject, lam_two[0], 1, 0) + dot_on(inject, lam_two[1], 1, 0)
        moved = scaled * to_end
        grad_inject += dot_three(split(moved), lam_two, 1, 1)
        rising = split(grad_ssd * jnp.exp(total_p))
        grad_readout += dot_three(rising, split(held), 1, 1)
        end_parts.append(jnp.sum(lam * next_state[:, cols], axis=0, keepdims=True))
        adjoint[:, cols] = lam * jnp.exp(total_p[BLOCK - 1 : BLOCK, :]) + (
            dot_on(readout, rising[0], 0, 0) + dot_on(readout, rising[1], 0, 0)
        )
        next_state[:, cols] = held
        pure = ssd - skip[:, cols] * x
        decay_parts.append(grad_ssd * pure - scaled * local - moved * far)
        grad_scaled = local + to_end * far
        step_parts.append(x * grad_scaled)
        skip_parts.append(jnp.sum(grad_ssd * x, axis=0, keepdims=True))
        grad_x = dt_p * grad_scaled + skip[:, cols] * grad_ssd
        before = convolve(buffer, kernel_ref, pair * 2 * P_SIZE, 2 * P_SIZE)
        sig = sigmoid(before)
        grads[0:BLOCK, cols] = grad_x * (sig * (1.0 + before * (1.0 - sig)))
    row_grads = head_sums(jnp.concatenate(decay_parts, axis=1))
    upper = order_mask(True).astype(F32)
    ends = head_sums(jnp.concatenate(end_parts, axis=1))
    grad_log = dot_on(upper, row_grads, 1, 0, HIGH) + ends
    grad_dt = head_sums(jnp.concatenate(step_parts, axis=1)) + decay * grad_log
    grad_raw = grad_dt * sigmoid(raw + head_ref[0:1, :])
    grad_step_ref[...] = jnp.zeros((BLOCK, N), BF16)
    grad_step_ref[:, 0 : grad_raw.shape[1]] = grad_raw.astype(BF16)
    grad_head_ref[0:1, :] += jnp.sum(grad_raw, axis=0, keepdims=True)
    grad_head_ref[1:2, :] += decay * jnp.sum(dt * grad_log, axis=0, keepdims=True)
    grad_head_ref[2:3, :] += head_sums(jnp.concatenate(skip_parts, axis=1))
    scores_two = split(grad_scores_t)
    grad_inject = grad_inject + dot_two(scores_two, readout, 1, 0)
    grad_readout = grad_readout + dot_two(scores_two, inject, 0, 0)
    grad_own_ref[...] = jnp.where(odd, grad_readout, grad_inject)
    grad_other_ref[...] = jnp.where(odd, grad_inject, grad_readout)
    grad_ref[:, width : 2 * width] = convolve_back(buffer, grads, kernel_ref, grad_kernel_ref)


def convolve_back(buffer, grads, kernel_ref, grad_kernel_ref):
    taps = kernel_ref.shape[0] - 1
    width = grads.shape[1]
    here = grads[0:BLOCK, :]
    grad_kernel_ref[taps : taps + 1, :] += jnp.sum(here, axis=0, keepdims=True)
    total = jnp.zeros((BLOCK, width), F32)
    for tap in range(taps):
        low = EDGE - taps + 1 + tap
        grad_kernel_ref[tap : tap + 1, :] += jnp.sum(here * buffer[low : low + BLOCK, :], axis=0, keepdims=True)
        ahead = taps - 1 - tap
        total = total + kernel_ref[tap : tap + 1, 0:width] * grads[ahead : ahead + BLOCK, :]
    return total.astype(BF16)


def mixer_backward(odd, proj, low, grad_gated, ssd, states, norms, kernel, heads, gain):
    length, width = grad_gated.shape
    wide = width + 2 * N
    count = length // BLOCK
    place = lambda i: count - 1 - i
    back = lambda i: (place(i), 0)
    edge = lambda i: jnp.maximum(place(i) * (BLOCK // EDGE) - 1, 0)
    whole = lambda i: (0, 0)
    specs = proj_specs(width, place)
    return pl.pallas_call(
        backward_body,
        grid=(count,),
        in_specs=specs[:3]
        + [
            specs[4],
            pl.BlockSpec((EDGE, width), lambda i: (edge(i), 1)),
            pl.BlockSpec((BLOCK, wide), back),
            pl.BlockSpec((BLOCK, width), back),
            pl.BlockSpec((BLOCK, width), back),
            pl.BlockSpec((1, N, width), lambda i: (place(i), 0, 0)),
            pl.BlockSpec((BLOCK, norms.shape[1]), back),
            pl.BlockSpec(kernel.shape, whole),
            pl.BlockSpec(heads.shape, whole),
            pl.BlockSpec(gain.shape, whole),
        ],
        out_specs=[
            pl.BlockSpec((BLOCK, 2 * width), back),
            pl.BlockSpec((BLOCK, N), back),
            pl.BlockSpec((BLOCK, N), back),
            pl.BlockSpec((BLOCK, N), back),
            pl.BlockSpec((kernel.shape[0], width), whole),
            pl.BlockSpec(heads.shape, whole),
            pl.BlockSpec(gain.shape, whole),
        ],
        out_shape=[
            jax.ShapeDtypeStruct((length, 2 * width), BF16),
            jax.ShapeDtypeStruct((length, N), BF16),
            jax.ShapeDtypeStruct((length, N), F32),
            jax.ShapeDtypeStruct((length, N), F32),
            jax.ShapeDtypeStruct((kernel.shape[0], width), F32),
            jax.ShapeDtypeStruct(heads.shape, F32),
            jax.ShapeDtypeStruct(gain.shape, F32),
        ],
        scratch_shapes=[
            pltpu.VMEM((N, width), F32),
            pltpu.VMEM((BLOCK + EDGE, width), F32),
            pltpu.VMEM((BLOCK + EDGE, width), F32),
            pltpu.VMEM((N, width), F32),
        ],
        compiler_params=pltpu.CompilerParams(vmem_limit_bytes=56 << 20),
        name="mixer_backward",
    )(odd, proj, proj, proj, proj, low, grad_gated, ssd, states, norms, kernel, heads, gain)


def map_backward_body(own_ref, edge_ref, mine_ref, theirs_ref, step_ref, kernel_ref, grad_ref, grad_kernel_ref, buffer, grads):
    step = pl.program_id(0)

    @pl.when(step == 0)
    def _():
        grads[BLOCK : BLOCK + EDGE, :] = jnp.zeros((EDGE, N), F32)
        grad_kernel_ref[...] = jnp.zeros_like(grad_kernel_ref)

    @pl.when(step > 0)
    def _():
        grads[BLOCK : BLOCK + EDGE, :] = grads[0:EDGE, :]

    last = step == pl.num_programs(0) - 1
    buffer[0:EDGE, :] = jnp.where(last, 0.0, edge_ref[...].astype(BF16).astype(F32))
    buffer[EDGE : EDGE + BLOCK, :] = own_ref[...].astype(BF16).astype(F32)
    before = convolve(buffer, kernel_ref, 0, N)
    sig = sigmoid(before)
    grads[0:BLOCK, :] = (mine_ref[...] + theirs_ref[...]) * (sig * (1.0 + before * (1.0 - sig)))
    grad_ref[:, 0:N] = convolve_back(buffer, grads, kernel_ref, grad_kernel_ref)
    grad_ref[:, N : 2 * N] = step_ref[...]


def map_backward(proj, mine, theirs, steps, kernel, column):
    length = mine.shape[0]
    count = length // BLOCK
    place = lambda i: count - 1 - i
    edge = lambda i: jnp.maximum(place(i) * (BLOCK // EDGE) - 1, 0)
    back = lambda i: (place(i), 0)
    whole = lambda i: (0, 0)
    narrow = pl.BlockSpec((BLOCK, N), back)
    return pl.pallas_call(
        map_backward_body,
        grid=(count,),
        in_specs=[
            pl.BlockSpec((BLOCK, N), lambda i: (place(i), column // N)),
            pl.BlockSpec((EDGE, N), lambda i: (edge(i), column // N)),
            narrow,
            narrow,
            narrow,
            pl.BlockSpec(kernel.shape, whole),
        ],
        out_specs=[pl.BlockSpec((BLOCK, 2 * N), back), pl.BlockSpec(kernel.shape, whole)],
        out_shape=[jax.ShapeDtypeStruct((length, 2 * N), BF16), jax.ShapeDtypeStruct(kernel.shape, F32)],
        scratch_shapes=[pltpu.VMEM((BLOCK + EDGE, N), F32), pltpu.VMEM((BLOCK + EDGE, N), F32)],
        name="map_backward",
    )(proj, proj, mine, theirs, steps, kernel)


def remote(src, dst, send, recv, device):
    return pltpu.make_async_remote_copy(
        src_ref=src, dst_ref=dst, send_sem=send, recv_sem=recv, device_id=device, device_id_type=MESH
    )


def gather_body(order, sizes, parts, *refs):
    nctx, ndp, ntp = sizes
    ntok, nin, nw = 2, parts[-1][0] + 1, parts[-1][2] + 1
    toks, weights = refs[:ntok], refs[ntok : ntok + nin]
    tok_outs = refs[ntok + nin : 2 * ntok + nin]
    weight_outs = refs[2 * ntok + nin : 2 * ntok + nin + nw]
    z_send, z_recv, t_send, t_recv, w_send, w_recv, x_send, x_recv, own = refs[2 * ntok + nin + nw :]
    c, d, t = lax.axis_index("ctx"), lax.axis_index("dp"), lax.axis_index("tp")
    near = t + 1 - 2 * lax.rem(t, 2)
    far = lax.rem(t + 2, ntp)
    length = toks[0].shape[0]
    part = length // ntp

    barrier = pltpu.get_barrier_semaphore()
    peers = [{"ctx": lax.rem(c + s, nctx)} for s in range(1, nctx)]
    peers += [{"dp": lax.rem(d + s, ndp)} for s in range(1, ndp)]
    peers += [{"tp": near}, {"tp": far}]
    for peer in peers:
        pl.semaphore_signal(barrier, inc=1, device_id=peer, device_id_type=MESH)
    pl.semaphore_wait(barrier, len(peers))

    def piece(p, to):
        array, column, _, _, width = parts[p]
        return weights[array].at[:, pl.ds(pl.multiple_of(column(to), N), width)]

    def landing(p, block):
        _, _, out, start, width = parts[p]
        return weight_outs[out].at[d, block, :, start : start + width]

    def of(out):
        return [p for p in range(len(parts)) if parts[p][2] == out]

    def rows(a, block, quarter):
        return tok_outs[a].at[pl.ds(pl.multiple_of(block * length + quarter * part, 16), part), :]

    def hop(a, j, side):
        block = c - j if side == 0 else c + j
        to = c + 1 if side == 0 else c - 1
        valid = (block >= 0) & (to < nctx) if side == 0 else (block < nctx) & (to >= 0)
        safe = jnp.clip(block, 0, nctx - 1)
        source = toks[a].at[pl.ds(pl.multiple_of(t * part, 16), part), :] if j == 0 else rows(a, safe, t)
        copy = remote(source, rows(a, safe, t), z_send.at[a, j, side], z_recv.at[a, safe], {"ctx": jnp.clip(to, 0, nctx - 1)})
        return valid, copy

    def arrival(j, side):
        block = c - 1 - j if side == 0 else c + 1 + j
        valid = block >= 0 if side == 0 else block < nctx
        return valid, jnp.clip(block, 0, nctx - 1)

    def tp_copy(a, block, kind):
        quarter = t if kind < 2 else far
        view = rows(a, block, quarter)
        return remote(view, view, t_send.at[a, block, kind], t_recv.at[a, block, kind], {"tp": far if kind == 0 else near})

    def tp_arrival(a, block, kind):
        quarter = far if kind == 0 else (near if kind == 1 else lax.rem(near + 2, ntp))
        view = rows(a, block, quarter)
        return remote(view, view, t_send.at[a, block, kind], t_recv.at[a, block, kind], {"tp": near})

    def w_copy(p, s):
        to = lax.rem(c + s, nctx)
        return remote(piece(p, to), landing(p, c), w_send.at[p, s], w_recv.at[p, s], {"ctx": to})

    def w_arrival(p, s):
        view = landing(p, lax.rem(c - s + nctx, nctx))
        return remote(view, view, w_send.at[p, s], w_recv.at[p, s], {"ctx": c})

    def x_copy(a, s, e):
        view = weight_outs[a].at[d, lax.rem(c - s + nctx, nctx)]
        return remote(view, view, x_send.at[a, s, e], x_recv.at[a, s, e], {"dp": lax.rem(d + e, ndp)})

    def x_arrival(a, s, e):
        view = weight_outs[a].at[lax.rem(d - e + ndp, ndp), lax.rem(c - s + nctx, nctx)]
        return remote(view, view, x_send.at[a, s, e], x_recv.at[a, s, e], {"dp": d})

    def own_tok(a):
        return pltpu.make_async_copy(toks[a], tok_outs[a].at[pl.ds(pl.multiple_of(c * length, 16), length), :], own.at[a])

    def own_piece(p):
        return pltpu.make_async_copy(piece(p, c), landing(p, c), own.at[ntok + p])

    def launch(step):
        kind, a, j = step
        if kind == "tok":
            for side in (0, 1):
                valid, copy = hop(a, j, side)

                @pl.when(valid)
                def _():
                    copy.start()
        else:
            for p in of(a):
                w_copy(p, j).start()

    def settle(step):
        kind, a, j = step
        if kind == "tok":
            for side in (0, 1):
                valid, block = arrival(j, side)

                @pl.when(valid)
                def _():
                    view = rows(a, block, t)
                    remote(view, view, z_send.at[a, j, side], z_recv.at[a, block], {"ctx": c}).wait_recv()
                    tp_copy(a, block, 0).start()
                    tp_copy(a, block, 1).start()
        else:
            for p in of(a):
                w_arrival(p, j).wait_recv()
            for e in range(1, ndp):
                x_copy(a, j, e).start()

    def settle_far(step):
        kind, a, j = step
        if kind == "tok":
            for side in (0, 1):
                valid, block = arrival(j, side)

                @pl.when(valid)
                def _():
                    tp_arrival(a, block, 0).wait_recv()
                    tp_copy(a, block, 2).start()

    for step in order[:DEPTH]:
        launch(step)
    for p in range(len(parts)):
        own_piece(p).start()
    for p in range(len(parts)):
        own_piece(p).wait()
    for a in range(nw):
        for e in range(1, ndp):
            x_copy(a, 0, e).start()
    for a in range(ntok):
        own_tok(a).start()
    for index, step in enumerate(order):
        settle(step)
        if index + DEPTH < len(order):
            launch(order[index + DEPTH])
        if index >= 2:
            settle_far(order[index - 2])
    for step in order[-2:]:
        settle_far(step)
    for kind, a, j in order:
        if kind == "tok":
            for side in (0, 1):
                valid, copy = hop(a, j, side)
                here, block = arrival(j, side)

                @pl.when(valid)
                def _():
                    copy.wait_send()

                @pl.when(here)
                def _():
                    for part_kind in range(3):
                        tp_copy(a, block, part_kind).wait_send()
                    tp_arrival(a, block, 1).wait_recv()
                    tp_arrival(a, block, 2).wait_recv()
        else:
            for p in of(a):
                w_copy(p, j).wait_send()
            for e in range(1, ndp):
                x_copy(a, j, e).wait_send()
                x_arrival(a, j, e).wait_recv()
    for a in range(nw):
        for e in range(1, ndp):
            x_copy(a, 0, e).wait_send()
            x_arrival(a, 0, e).wait_recv()
    for a in range(ntok):
        own_tok(a).wait()


def gather_all(toks, weights, parts, sizes):
    nctx, ndp, ntp = sizes
    turns = range(1, nctx)
    nw = parts[-1][2] + 1
    widths = [sum(p[4] for p in parts if p[2] == out) for out in range(nw)]
    shard_rows = weights[0].shape[0]
    tok = lambda a, j: [("tok", a, j)] if j < nctx - 1 else []
    per = lambda a: [("w", a, s) for s in turns]
    order = tok(0, 0) + tok(1, 0) + per(0) + tok(0, 1) + tok(1, 1) + per(1)[:1] + tok(0, 2) + tok(1, 2) + per(1)[1:]
    any_space = pl.BlockSpec(memory_space=pl.ANY)
    length, model = toks[0].shape
    out_shape = [jax.ShapeDtypeStruct((nctx * length, model), BF16) for _ in toks]
    out_shape += [jax.ShapeDtypeStruct((ndp, nctx, shard_rows, width), BF16) for width in widths]
    dma = pltpu.SemaphoreType.DMA
    return pl.pallas_call(
        functools.partial(gather_body, order, sizes, parts),
        out_shape=out_shape,
        in_specs=[any_space] * (len(toks) + len(weights)),
        out_specs=[any_space] * len(out_shape),
        scratch_shapes=[
            dma((2, nctx, 2)), dma((2, nctx)), dma((2, nctx, 3)), dma((2, nctx, 3)),
            dma((len(parts), nctx)), dma((len(parts), nctx)), dma((nw, nctx, ndp)), dma((nw, nctx, ndp)), dma((2 + len(parts),)),
        ],
        compiler_params=pltpu.CompilerParams(collective_id=1, has_side_effects=True),
        name="gather_inputs",
    )(*toks, *weights)


def add_rows(target, sources, rows, step):
    def some(index, _):
        here = pl.ds(pl.multiple_of(index * step, step), step)
        total = sources[0][here, :].astype(F32)
        for source in sources[1:]:
            total = total + source[here, :].astype(F32)
        target[here, :] = total.astype(target.dtype)
        return 0

    lax.fori_loop(0, rows // step, some, 0)


def output_body(order, sizes, nw, parts, *refs):
    nctx, ndp, ntp = sizes
    nout = len(parts)
    partial, small, grads = refs[0], refs[1], refs[2 : 2 + nw]
    sum_out, small_out, grad_outs = refs[2 + nw], refs[3 + nw], refs[4 + nw : 4 + nw + nout]
    rest = refs[4 + nw + nout :]
    (near_in, far_out, far_in, z_out, z_in, held, acc, done) = rest[:8]
    x_ins, x_sums = rest[8 : 8 + nw], rest[8 + nw : 8 + 2 * nw]
    (near_s, near_r, far_s, far_r, z_s, z_r, x_s, x_r, w_s, w_r, fin_s, fin_r, local, small_s, small_r) = rest[8 + 2 * nw :]
    c, d, t = lax.axis_index("ctx"), lax.axis_index("dp"), lax.axis_index("tp")
    near = t + 1 - 2 * lax.rem(t, 2)
    far = lax.rem(t + 2, ntp)
    far_near = lax.rem(near + 2, ntp)
    length = sum_out.shape[0]
    part = length // ntp
    wrap = lambda i: lax.rem(i + nctx, nctx)

    barrier = pltpu.get_barrier_semaphore()
    others = [(e, s) for e in range(ndp) for s in range(nctx) if e or s]
    place = lambda e, s: {"dp": lax.rem(d + e, ndp), "ctx": lax.rem(c + s, nctx)}
    peers = [place(e, s) for e, s in others] + [{"tp": near}, {"tp": far}]
    for peer in peers:
        pl.semaphore_signal(barrier, inc=1, device_id=peer, device_id_type=MESH)
    pl.semaphore_wait(barrier, len(peers))

    def small_copy(e, s):
        return remote(small, small_out.at[d, c], small_s.at[e, s], small_r.at[e, s], place(e, s))

    def small_arrival(e, s):
        view = small_out.at[lax.rem(d - e + ndp, ndp), wrap(c - s)]
        return remote(view, view, small_s.at[e, s], small_r.at[e, s], place(e, s))

    def rows(s, quarter):
        return partial.at[pl.ds(pl.multiple_of(wrap(c + s) * length + quarter * part, 16), part), :]

    def near_copy(s, slot):
        return remote(rows(s, near if slot == 0 else far_near), near_in.at[s, slot], near_s.at[s, slot], near_r.at[s, slot], {"tp": near})

    def far_copy(s):
        return remote(far_out.at[s], far_in.at[s], far_s.at[s], far_r.at[s], {"tp": far})

    def z_copy(s):
        return remote(z_out.at[s], z_in.at[s], z_s.at[s], z_r.at[s], {"ctx": wrap(c + s)})

    def x_copy(a, s, e):
        to = lax.rem(d + e, ndp)
        return remote(grads[a].at[to, wrap(c + s)], x_ins[a].at[s, e - 1], x_s.at[a, s, e], x_r.at[a, s, e], {"dp": to})

    def piece(p, s):
        a, start, width, _, _ = parts[p]
        return x_sums[a].at[s, :, start : start + width]

    def landing(p, block):
        _, _, width, out, split_columns = parts[p]
        if split_columns:
            return grad_outs[out].at[:, pl.ds(pl.multiple_of(block * width, N), width)]
        return grad_outs[out].at[block]

    def w_copy(p, s):
        return remote(piece(p, s), landing(p, c), w_s.at[p, s], w_r.at[p, s], {"ctx": wrap(c + s)})

    def w_arrival(p, s):
        view = landing(p, wrap(c - s))
        return remote(view, view, w_s.at[p, s], w_r.at[p, s], {"ctx": c})

    def w_own(p):
        return pltpu.make_async_copy(piece(p, 0), landing(p, c), local.at[2 + nw * nctx + p])

    def load(s, quarter, slot):
        return pltpu.make_async_copy(rows(s, quarter), held.at[slot], local.at[slot])

    def load_grad(a, s):
        return pltpu.make_async_copy(grads[a].at[d, wrap(c + s)], x_sums[a].at[s], local.at[2 + a * nctx + s])

    def start_x(s):
        for a in range(nw):
            for e in range(1, ndp):
                x_copy(a, s, e).start()

    def near_sum(s):
        load(s, far, 0).start()
        near_copy(s, 1).wait_recv()
        load(s, far, 0).wait()
        add_rows(far_out.at[s], [held.at[0], near_in.at[s, 1]], part, 16)
        far_copy(s).start()

    def far_sum(s):
        load(s, t, 1).start()
        near_copy(s, 0).wait_recv()
        far_copy(s).wait_recv()
        load(s, t, 1).wait()
        add_rows(acc if s == 0 else z_out.at[s], [held.at[1], near_in.at[s, 0], far_in.at[s]], part, 16)
        if s > 0:
            z_copy(s).start()

    def grad_sum(s):
        for a in range(nw):
            load_grad(a, s).wait()
            for e in range(1, ndp):
                x_copy(a, s, e).wait_recv()
            add_rows(x_sums[a].at[s], [x_sums[a].at[s]] + [x_ins[a].at[s, e - 1] for e in range(1, ndp)], x_sums[a].shape[1], 16)
        for p in range(nout):
            if s > 0:
                w_copy(p, s).start()
            else:
                w_own(p).start()

    for s in order:
        for slot in (1, 0):
            near_copy(s, slot).start()
        for a in range(nw):
            load_grad(a, s).start()
    ahead = 2
    for s in order[:ahead]:
        start_x(s)
    for e, s in others:
        small_copy(e, s).start()
    small_own = pltpu.make_async_copy(small, small_out.at[d, c], local.at[2 + nw * nctx + nout])
    small_own.start()
    for s in order[:ahead]:
        near_sum(s)
    for index, s in enumerate(order):
        far_sum(s)
        if index + ahead < nctx:
            near_sum(order[index + ahead])
        grad_sum(s)
        if index + ahead < nctx:
            start_x(order[index + ahead])
    for s in range(1, nctx):
        z_copy(s).wait_recv()
    add_rows(done, [acc] + [z_in.at[s] for s in range(1, nctx)], part, 16)

    def mine(quarter):
        return sum_out.at[pl.ds(pl.multiple_of(quarter * part, 16), part), :]

    finals = [
        remote(done, mine(t), fin_s.at[0], fin_r.at[0], {"tp": far}),
        remote(done, mine(t), fin_s.at[1], fin_r.at[1], {"tp": near}),
        remote(mine(far), mine(far), fin_s.at[2], fin_r.at[2], {"tp": near}),
    ]
    keep = pltpu.make_async_copy(done, mine(t), local.at[0])
    finals[0].start()
    finals[1].start()
    keep.start()
    remote(mine(far), mine(far), fin_s.at[0], fin_r.at[0], {"tp": far}).wait_recv()
    finals[2].start()
    remote(mine(near), mine(near), fin_s.at[1], fin_r.at[1], {"tp": near}).wait_recv()
    remote(mine(far_near), mine(far_near), fin_s.at[2], fin_r.at[2], {"tp": near}).wait_recv()
    keep.wait()
    for copy in finals:
        copy.wait_send()
    for s in order:
        for slot in (1, 0):
            near_copy(s, slot).wait_send()
        far_copy(s).wait_send()
        for a in range(nw):
            for e in range(1, ndp):
                x_copy(a, s, e).wait_send()
        for p in range(nout):
            if s > 0:
                w_copy(p, s).wait_send()
                w_arrival(p, s).wait_recv()
            else:
                w_own(p).wait()
        if s > 0:
            z_copy(s).wait_send()
    for e, s in others:
        small_copy(e, s).wait_send()
        small_arrival(e, s).wait_recv()
    small_own.wait()


def return_all(partial, small, grads, parts, sizes):
    nctx, ndp, ntp = sizes
    length = partial.shape[0] // nctx
    part, model = length // ntp, partial.shape[1]
    nw, nout = len(grads), len(parts)
    outs = [(nctx,) + grads[p[0]].shape[2:] if not p[4] else (grads[0].shape[2], nctx * p[2]) for p in parts]
    order = [nctx // 2] + [s for s in range(1, nctx) if s != nctx // 2] + [0]
    any_space = pl.BlockSpec(memory_space=pl.ANY)
    dma = pltpu.SemaphoreType.DMA
    vmem = pltpu.VMEM
    strip = lambda *lead: vmem(lead + (part, model), BF16)
    return pl.pallas_call(
        functools.partial(output_body, order, sizes, nw, parts),
        out_shape=[jax.ShapeDtypeStruct((length, model), BF16), jax.ShapeDtypeStruct((ndp, nctx) + small.shape, F32)]
        + [jax.ShapeDtypeStruct(out, BF16) for out in outs],
        in_specs=[any_space] * (2 + nw),
        out_specs=[any_space] * (2 + nout),
        scratch_shapes=[
            strip(nctx, 2), strip(nctx), strip(nctx), strip(nctx), strip(nctx), strip(2), vmem((part, model), F32), strip(),
        ]
        + [vmem((nctx, max(ndp - 1, 1)) + g.shape[2:], BF16) for g in grads]
        + [vmem((nctx,) + g.shape[2:], BF16) for g in grads]
        + [
            dma((nctx, 2)), dma((nctx, 2)), dma((nctx,)), dma((nctx,)), dma((nctx,)), dma((nctx,)),
            dma((nw, nctx, ndp)), dma((nw, nctx, ndp)), dma((nout, nctx)), dma((nout, nctx)), dma((3,)), dma((3,)),
            dma((2 + nw * nctx + nout + 1,)), dma((ndp, nctx)), dma((ndp, nctx)),
        ],
        compiler_params=pltpu.CompilerParams(collective_id=2, has_side_effects=True, vmem_limit_bytes=60 << 20),
        name="return_outputs",
    )(partial, small, *grads)


def small_body(sizes, value, total, gathered, send, recv):
    nctx, ndp = sizes
    c, d = lax.axis_index("ctx"), lax.axis_index("dp")
    others = [(e, s) for e in range(ndp) for s in range(nctx) if e or s]
    place = lambda e, s: {"dp": lax.rem(d + e, ndp), "ctx": lax.rem(c + s, nctx)}
    barrier = pltpu.get_barrier_semaphore()
    for e, s in others:
        pl.semaphore_signal(barrier, inc=1, device_id=place(e, s), device_id_type=MESH)
    pl.semaphore_wait(barrier, len(others))
    gathered[d, c] = value[...]
    for e, s in others:
        remote(value, gathered.at[d, c], send.at[e, s], recv.at[e, s], place(e, s)).start()
    for e, s in others:
        view = gathered.at[lax.rem(d - e + ndp, ndp), lax.rem(c - s + nctx, nctx)]
        remote(view, view, send.at[e, s], recv.at[e, s], place(e, s)).wait_recv()
        remote(value, gathered.at[d, c], send.at[e, s], recv.at[e, s], place(e, s)).wait_send()
    running = jnp.zeros(value.shape, F32)
    for e in range(ndp):
        for s in range(nctx):
            running = running + gathered[e, s]
    total[...] = running


def sum_small(value, sizes):
    nctx, ndp = sizes
    vmem = pl.BlockSpec(memory_space=pltpu.VMEM)
    dma = pltpu.SemaphoreType.DMA
    return pl.pallas_call(
        functools.partial(small_body, sizes),
        out_shape=jax.ShapeDtypeStruct(value.shape, F32),
        in_specs=[vmem],
        out_specs=vmem,
        scratch_shapes=[pltpu.VMEM((ndp, nctx) + value.shape, F32), dma((ndp, nctx)), dma((ndp, nctx))],
        compiler_params=pltpu.CompilerParams(collective_id=3, has_side_effects=True),
        name="sum_small",
    )(value)


def dot_last(left_side, right_side):
    return lax.dot_general(left_side, right_side, (((1,), (1,)), ((), ())), preferred_element_type=F32)


def dot_first(left_side, right_side):
    return lax.dot_general(left_side, right_side, (((0,), (0,)), ((), ())), preferred_element_type=F32)


def sum_rows(partial):
    return lax.psum_scatter(partial.astype(BF16), ("ctx", "tp"), scatter_dimension=0, tiled=True).astype(F32)


def shards(tokens, norm_gain, zx_weight, bc_weight, dt_weight, conv_x, conv_bc, head_params, gate_gain, out_weight, cotangent):
    seq_count, length, model_width = tokens.shape
    assert seq_count == 1
    nctx, ntp, ndp = lax.axis_size("ctx"), lax.axis_size("tp"), lax.axis_size("dp")
    ctx = lax.axis_index("ctx")
    rows = dt_weight.shape[0]
    inner = conv_x.shape[1]
    pair_width = bc_weight.shape[2]
    groups = pair_width // N
    share = nctx // groups
    assert share == 2 and groups * share == nctx
    width = inner // nctx
    heads = dt_weight.shape[1] // nctx
    taps = conv_x.shape[0] - 1
    group_width = inner // groups

    def mine(value):
        return lax.dynamic_index_in_dim(value, ctx, 0, False)

    def partner(value):
        return lax.ppermute(value, "ctx", [(i, i ^ 1) for i in range(nctx)])

    hidden = tokens.astype(F32).reshape(length, model_width)
    cot = cotangent.reshape(length, model_width)
    rscale = lax.rsqrt(jnp.mean(hidden * hidden, axis=-1, keepdims=True) + EPS)
    normed = (hidden * rscale * norm_gain).astype(BF16)

    steps = jnp.pad(dt_weight.reshape(rows, nctx, heads), ((0, 0), (0, 0), (0, N - heads))).reshape(rows, nctx * N)
    map_at = lambda which: lambda to: (lax.rem(to + which, 2) * groups + to // share) * N
    parts = (
        (0, lambda to: to * width, 0, 0, width),
        (0, lambda to: inner + to * width, 0, width, width),
        (1, map_at(0), 0, 2 * width, N),
        (2, lambda to: to * N, 0, 2 * width + N, N),
        (1, map_at(1), 0, 2 * width + 2 * N, N),
        (3, lambda to: to * width, 1, 0, width),
    )
    sources = (zx_weight.reshape(rows, 2 * inner), bc_weight.reshape(rows, 2 * pair_width), steps, out_weight)
    normed_all, cot_all, weight_in, weight_out = gather_all((normed, cot), sources, parts, (nctx, ndp, ntp))
    weight_in = weight_in.reshape(model_width, -1)
    weight_out = weight_out.reshape(model_width, width)

    grad_gated = jnp.dot(cot_all, weight_out, preferred_element_type=F32)
    proj = jnp.dot(normed_all, weight_in, preferred_element_type=F32)
    odd = lax.rem(ctx, 2)
    kernel_x = mine(conv_x.reshape(taps + 1, nctx, width).transpose(1, 0, 2))
    kernel_maps = conv_bc.reshape(taps + 1, 2, groups, N).transpose(2, 1, 0, 3).reshape(nctx, taps + 1, N)
    kernel_own = mine(kernel_maps)
    kernel_other = lax.dynamic_index_in_dim(kernel_maps, ctx + 1 - 2 * odd, 0, False)
    kernel = jnp.concatenate([kernel_x, kernel_own, kernel_other], axis=1)
    odd = odd.astype(jnp.int32).reshape(1, 1)
    heads_mine = mine(head_params.reshape(3, nctx, heads).transpose(1, 0, 2))
    gain = mine(gate_gain.reshape(nctx, 1, width))
    low, ssd, states, sums = mixer_forward(odd, proj, grad_gated, kernel, heads_mine, gain)
    sums = (sums + partner(sums)) / group_width
    inverse = lax.rsqrt(sums[0] + EPS)
    norms = jnp.stack([inverse, inverse * inverse * inverse * sums[1]], axis=1)
    gate_pre = proj[:, :width]
    gated_norm = (ssd * (gate_pre * jax.nn.sigmoid(gate_pre)) * norms[:, 0:1] * gain).astype(BF16)
    branch = sum_rows(dot_last(gated_norm, weight_out))
    grad_zx, grad_steps, grad_own, grad_other, grad_kernel_x, grad_heads, gate_gain_grad = mixer_backward(
        odd, proj, low, grad_gated, ssd, states, norms, kernel, heads_mine, gain
    )
    theirs = partner(grad_other)
    grad_rest, grad_kernel_own = map_backward(proj, grad_own, theirs, grad_steps, kernel_own, 2 * width)
    grad_all = jnp.concatenate([grad_zx, grad_rest], axis=1)
    blocks = lambda grad: grad.astype(BF16).reshape(ndp, nctx, rows, -1)
    weight_grads = (
        blocks(dot_first(normed_all, grad_zx)),
        blocks(dot_first(normed_all, grad_rest)),
        blocks(dot_first(cot_all, gated_norm)),
    )
    partial = dot_last(grad_all, weight_in[:, : grad_all.shape[1]]).astype(BF16)
    pieces = (grad_kernel_x, grad_kernel_own, grad_heads, gate_gain_grad)
    small = jnp.concatenate([piece.reshape(-1) for piece in pieces])
    lines = -(-small.shape[0] // (8 * N)) * 8
    small = jnp.pad(small, (0, lines * N - small.shape[0])).reshape(lines, N)
    out_parts = (
        (0, 0, width, 0, True),
        (0, width, width, 1, True),
        (1, 0, 2 * N, 2, False),
        (2, 0, width, 3, True),
    )
    grad_normed, table, back_z, back_x, back_rest, back_out = return_all(
        partial, small, weight_grads, out_parts, (nctx, ndp, ntp)
    )
    grad_normed, branch = lax.optimization_barrier((grad_normed, branch))
    part = length // ntp
    token_part = lax.dynamic_slice_in_dim(tokens.reshape(length, model_width), lax.axis_index("tp") * part, part, 0)
    mixed = lax.all_gather((token_part.astype(F32) + branch).astype(BF16), "tp", axis=0, tiled=True)
    grad_normed = grad_normed.astype(F32)

    grad_hat = grad_normed * norm_gain
    norm_gain_grad = jnp.sum(grad_normed * hidden * rscale, axis=0)
    grad_hidden = rscale * grad_hat - hidden * (rscale * rscale * rscale) * jnp.mean(
        grad_hat * hidden, axis=1, keepdims=True
    )
    tokens_grad = cot.astype(F32) + grad_hidden

    zx_weight_grad = jnp.stack([back_z, back_x], axis=1).astype(F32)
    back_rest = back_rest.astype(F32)
    bc_weight_grad = back_rest[:, :, :N].reshape(groups, 2, rows, N).transpose(2, 1, 0, 3).reshape(rows, 2, groups * N)
    dt_weight_grad = back_rest[:, :, N : N + heads].transpose(1, 0, 2).reshape(rows, nctx * heads)
    out_weight_grad = back_out.astype(F32)

    table = jnp.sum(table, axis=0).reshape(nctx, lines * N)
    ends = [0]
    for piece in pieces:
        ends.append(ends[-1] + piece.size)
    kernel_x, kernel_own, head_grad, gain_grad = [table[:, a:b] for a, b in zip(ends[:-1], ends[1:])]
    conv_x_grad = kernel_x.reshape(nctx, taps + 1, width).transpose(1, 0, 2).reshape(taps + 1, inner)
    conv_bc_grad = kernel_own.reshape(groups, 2, taps + 1, N).transpose(2, 1, 0, 3).reshape(taps + 1, 2, groups * N)
    head_grad = head_grad.reshape(nctx, 3, heads).transpose(1, 0, 2).reshape(3, nctx * heads)
    gate_gain_grad = gain_grad.reshape(inner)
    norm_gain_grad = sum_small(norm_gain_grad.reshape(-1, N), (nctx, ndp)).reshape(model_width)
    return (
        mixed.reshape(tokens.shape),
        tokens_grad.reshape(tokens.shape),
        norm_gain_grad,
        zx_weight_grad,
        bc_weight_grad,
        dt_weight_grad,
        conv_x_grad,
        conv_bc_grad,
        head_grad,
        gate_gain_grad,
        out_weight_grad,
    )


def solution(mesh):
    wide = P(("dp", "ctx"), None, "tp")
    flat = P(("dp", "ctx"), "tp")
    rows = P("dp", "ctx", None)
    return jax.shard_map(
        shards,
        mesh=mesh,
        in_specs=(rows, P(), wide, wide, flat, P(None, "tp"), P(None, None, "tp"), P(None, "tp"), P("tp"), flat, rows),
        out_specs=(rows, rows, P(), wide, wide, flat, P(None, "tp"), P(None, None, "tp"), P(None, "tp"), P("tp"), flat),
        check_vma=False,
    )
```

```python
import functools

import jax
import jax.numpy as jnp
from jax import lax
from jax.experimental import pallas as pl
from jax.experimental.pallas import tpu as pltpu
from jax.sharding import PartitionSpec as P

P_SIZE = 64
N = 128
BLOCK = 256
EDGE = 8
DEPTH = 3
MESH = pl.DeviceIdType.MESH
EPS = 1e-05
HIGH = lax.Precision.HIGHEST
F32 = jnp.float32
BF16 = jnp.bfloat16


def dot_on(left_side, right_side, left_dim, right_dim, precision=None):
    return lax.dot_general(
        left_side, right_side, (((left_dim,), (right_dim,)), ((), ())), precision=precision, preferred_element_type=F32
    )


def split(v):
    high = v.astype(BF16)
    return high, (v - high.astype(F32)).astype(BF16)


def dot_two(parts, other, part_dim, other_dim):
    return dot_on(parts[0], other, part_dim, other_dim) + dot_on(parts[1], other, part_dim, other_dim)


def dot_three(left_side, right_side, left_dim, right_dim):
    high = dot_two(left_side, right_side[0], left_dim, right_dim)
    return high + dot_on(left_side[0], right_side[1], left_dim, right_dim)


def softplus(v):
    return jnp.maximum(v, 0.0) + jnp.log1p(jnp.exp(-jnp.abs(v)))


def sigmoid(v):
    return 1.0 / (1.0 + jnp.exp(-v))


def order_mask(transposed):
    row = lax.broadcasted_iota(jnp.int32, (BLOCK, BLOCK), 0)
    col = lax.broadcasted_iota(jnp.int32, (BLOCK, BLOCK), 1)
    return row <= col if transposed else row >= col


def first_half(rows):
    return lax.broadcasted_iota(jnp.int32, (rows, 2 * P_SIZE), 1) < P_SIZE


def over_pair(value, pair):
    shape = (value.shape[0], P_SIZE * 2)
    left = jnp.broadcast_to(value[:, 2 * pair : 2 * pair + 1], shape)
    right = jnp.broadcast_to(value[:, 2 * pair + 1 : 2 * pair + 2], shape)
    return jnp.where(first_half(shape[0]), left, right)


def over_heads(value):
    return jnp.concatenate([over_pair(value, pair) for pair in range(value.shape[1] // 2)], axis=1)


def head_sums(value):
    columns = []
    for pair in range(value.shape[1] // (2 * P_SIZE)):
        part = value[:, pair * 2 * P_SIZE : (pair + 1) * 2 * P_SIZE]
        left = jnp.where(first_half(part.shape[0]), part, 0.0)
        columns += [jnp.sum(left, axis=1, keepdims=True), jnp.sum(part - left, axis=1, keepdims=True)]
    heads = len(columns)
    lane = lax.broadcasted_iota(jnp.int32, (value.shape[0], heads), 1)
    total = jnp.broadcast_to(columns[0], lane.shape)
    for head in range(1, heads):
        total = jnp.where(lane == head, columns[head], total)
    return total


def convolve(buffer, kernel_ref, start, width):
    taps = kernel_ref.shape[0] - 1
    total = kernel_ref[taps : taps + 1, start : start + width]
    for tap in range(taps):
        low = EDGE - taps + 1 + tap
        total = total + kernel_ref[tap : tap + 1, start : start + width] * buffer[low : low + BLOCK, start : start + width]
    return total


def block_steps(raw, head_ref):
    dt = softplus(raw + head_ref[0:1, :])
    decay = -jnp.exp(head_ref[1:2, :])
    log_step = dt * decay
    lower = order_mask(False).astype(F32)
    total = dot_on(lower, log_step, 1, 0, HIGH)
    total_t = dot_on(log_step, lower, 0, 1, HIGH)
    return dt, decay, total, total_t


def forward_body(
    odd_ref, gate_ref, x_ref, own_ref, step_ref, other_ref, up_ref, kernel_ref, head_ref, gain_ref,
    low_ref, ssd_ref, state_ref, sums_ref, state, buffer,
):
    width = gate_ref.shape[1]
    raw = step_ref[:, 0 : head_ref.shape[1]]
    first = pl.program_id(0) == 0

    @pl.when(first)
    def _():
        state[...] = jnp.zeros_like(state)
        buffer[0:EDGE, :] = jnp.zeros((EDGE, buffer.shape[1]), F32)

    @pl.when(jnp.logical_not(first))
    def _():
        buffer[0:EDGE, :] = buffer[BLOCK : BLOCK + EDGE, :]

    buffer[EDGE : EDGE + BLOCK, 0:width] = x_ref[...].astype(BF16).astype(F32)
    buffer[EDGE : EDGE + BLOCK, width : width + N] = own_ref[...].astype(BF16).astype(F32)
    buffer[EDGE : EDGE + BLOCK, width + N :] = other_ref[...].astype(BF16).astype(F32)
    before = convolve(buffer, kernel_ref, 0, buffer.shape[1])
    low_ref[...] = (before * sigmoid(before)).astype(BF16)
    dt, _, total, total_t = block_steps(raw, head_ref)
    state_ref[0] = state[...]
    odd = odd_ref[0, 0] == 1
    own, other = low_ref[:, width : width + N], low_ref[:, width + N : width + 2 * N]
    inject, readout = jnp.where(odd, other, own), jnp.where(odd, own, other)
    scores = dot_on(readout, inject, 1, 1)
    mask = order_mask(False)
    half = first_half(BLOCK)
    skip = over_heads(head_ref[2:3, :])
    squares = []
    for pair in range(width // (2 * P_SIZE)):
        cols = slice(pair * 2 * P_SIZE, (pair + 1) * 2 * P_SIZE)
        x = low_ref[:, cols].astype(F32)
        total_p = over_pair(total, pair)
        scaled = x * over_pair(dt, pair)
        scaled_two = split(scaled)
        local = []
        for head in (2 * pair, 2 * pair + 1):
            gap = total[:, head : head + 1] - total_t[head : head + 1, :]
            mixing = jnp.exp(jnp.where(mask, gap, -1e30)) * scores
            local.append(dot_three(split(mixing), scaled_two, 1, 0))
        held = state[:, cols]
        held_two = split(held)
        carried = jnp.exp(total_p) * (dot_on(readout, held_two[0], 1, 0) + dot_on(readout, held_two[1], 1, 0))
        ssd = jnp.where(half, local[0], local[1]) + carried + skip[:, cols] * x
        ssd_ref[:, cols] = ssd
        moved = split(scaled * jnp.exp(total_p[BLOCK - 1 : BLOCK, :] - total_p))
        state[:, cols] = held * jnp.exp(total_p[BLOCK - 1 : BLOCK, :]) + (
            dot_on(inject, moved[0], 0, 0) + dot_on(inject, moved[1], 0, 0)
        )
        gate_pre = gate_ref[:, cols]
        gated = ssd * (gate_pre * sigmoid(gate_pre))
        squares.append((gated * gated, gated * (up_ref[:, cols] * gain_ref[0:1, cols])))
    ones = jnp.ones((8, 2 * P_SIZE), F32)
    square = functools.reduce(jnp.add, [s[0] for s in squares])
    cross = functools.reduce(jnp.add, [s[1] for s in squares])
    sums_ref[0:1, :] = dot_on(ones, square, 1, 1, HIGH)[0:1, :]
    sums_ref[1:2, :] = dot_on(ones, cross, 1, 1, HIGH)[0:1, :]


def proj_specs(width, index):
    narrow = lambda place: pl.BlockSpec((BLOCK, N), lambda i: (index(i), 2 * width // N + place))
    return [
        pl.BlockSpec(memory_space=pltpu.SMEM),
        pl.BlockSpec((BLOCK, width), lambda i: (index(i), 0)),
        pl.BlockSpec((BLOCK, width), lambda i: (index(i), 1)),
        narrow(0),
        narrow(1),
        narrow(2),
    ]


def mixer_forward(odd, proj, grad_gated, kernel, heads, gain):
    length, width = grad_gated.shape
    wide = width + 2 * N
    count = length // BLOCK
    rows = lambda i: (i, 0)
    whole = lambda i: (0, 0)
    return pl.pallas_call(
        forward_body,
        grid=(count,),
        in_specs=proj_specs(width, lambda i: i)
        + [
            pl.BlockSpec((BLOCK, width), rows),
            pl.BlockSpec(kernel.shape, whole),
            pl.BlockSpec(heads.shape, whole),
            pl.BlockSpec(gain.shape, whole),
        ],
        out_specs=[
            pl.BlockSpec((BLOCK, wide), rows),
            pl.BlockSpec((BLOCK, width), rows),
            pl.BlockSpec((1, N, width), lambda i: (i, 0, 0)),
            pl.BlockSpec((2, BLOCK), lambda i: (0, i)),
        ],
        out_shape=[
            jax.ShapeDtypeStruct((length, wide), BF16),
            jax.ShapeDtypeStruct((length, width), F32),
            jax.ShapeDtypeStruct((count, N, width), F32),
            jax.ShapeDtypeStruct((2, length), F32),
        ],
        scratch_shapes=[pltpu.VMEM((N, width), F32), pltpu.VMEM((BLOCK + EDGE, wide), F32)],
        compiler_params=pltpu.CompilerParams(vmem_limit_bytes=48 << 20),
        name="mixer_forward",
    )(odd, proj, proj, proj, proj, proj, grad_gated, kernel, heads, gain)


def backward_body(
    odd_ref, gate_ref, x_ref, step_ref, edge_ref, low_ref, up_ref, ssd_ref, state_ref, norm_ref, kernel_ref, head_ref, gain_ref,
    grad_ref, grad_step_ref, grad_own_ref, grad_other_ref, grad_kernel_ref, grad_head_ref, grad_gain_ref,
    adjoint, buffer, grads, next_state,
):
    width = gate_ref.shape[1]
    raw = step_ref[:, 0 : head_ref.shape[1]]
    taps = kernel_ref.shape[0] - 1
    count = pl.num_programs(0)
    step = pl.program_id(0)

    @pl.when(step == 0)
    def _():
        adjoint[...] = jnp.zeros_like(adjoint)
        next_state[...] = jnp.zeros_like(next_state)
        grads[BLOCK : BLOCK + EDGE, :] = jnp.zeros((EDGE, width), F32)
        grad_kernel_ref[...] = jnp.zeros_like(grad_kernel_ref)
        grad_head_ref[...] = jnp.zeros_like(grad_head_ref)
        grad_gain_ref[...] = jnp.zeros_like(grad_gain_ref)

    @pl.when(step > 0)
    def _():
        grads[BLOCK : BLOCK + EDGE, :] = grads[0:EDGE, :]

    last = step == count - 1
    buffer[0:EDGE, :] = jnp.where(last, 0.0, edge_ref[...].astype(BF16).astype(F32))
    buffer[EDGE : EDGE + BLOCK, :] = x_ref[...].astype(BF16).astype(F32)
    dt, decay, total, total_t = block_steps(raw, head_ref)
    odd = odd_ref[0, 0] == 1
    own, other = low_ref[:, width : width + N], low_ref[:, width + N : width + 2 * N]
    inject, readout = jnp.where(odd, other, own), jnp.where(odd, own, other)
    scores_t = dot_on(inject, readout, 1, 1)
    mask_t = order_mask(True)
    half = first_half(BLOCK)
    skip = over_heads(head_ref[2:3, :])
    inverse = norm_ref[:, 0:1]
    pull = norm_ref[:, 1:2]
    grad_scores_t = jnp.zeros((BLOCK, BLOCK), F32)
    grad_inject = jnp.zeros((BLOCK, N), F32)
    grad_readout = jnp.zeros((BLOCK, N), F32)
    decay_parts, step_parts, skip_parts, end_parts = [], [], [], []
    for pair in range(width // (2 * P_SIZE)):
        cols = slice(pair * 2 * P_SIZE, (pair + 1) * 2 * P_SIZE)
        x = low_ref[:, cols].astype(F32)
        gate_pre = gate_ref[:, cols]
        ssd = ssd_ref[:, cols]
        sig = sigmoid(gate_pre)
        gate = gate_pre * sig
        up = up_ref[:, cols]
        gated = ssd * gate
        grad_gain_ref[0:1, cols] += jnp.sum(up * gated * inverse, axis=0, keepdims=True)
        grad_pre = inverse * (up * gain_ref[0:1, cols]) - gated * pull
        grad_ref[:, cols] = (grad_pre * ssd * (sig * (1.0 + gate_pre * (1.0 - sig)))).astype(BF16)
        grad_ssd = grad_pre * gate
        grad_two = split(grad_ssd)
        total_p = over_pair(total, pair)
        dt_p = over_pair(dt, pair)
        to_end = jnp.exp(total_p[BLOCK - 1 : BLOCK, :] - total_p)
        scaled = x * dt_p
        scaled_two = split(scaled)
        local = []
        for index, head in enumerate((2 * pair, 2 * pair + 1)):
            gap = total_t[head : head + 1, :] - total[:, head : head + 1]
            decays = jnp.exp(jnp.where(mask_t, gap, -1e30))
            own = half if index == 0 else jnp.logical_not(half)
            mine = [jnp.where(own, part, jnp.zeros_like(part)) for part in grad_two]
            grad_scores_t += decays * dot_three(scaled_two, mine, 1, 1)
            local.append(dot_three(split(decays * scores_t), grad_two, 1, 0))
        local = jnp.where(half, local[0], local[1])
        lam = adjoint[:, cols]
        lam_two = split(lam)
        held = state_ref[0, :, cols]
        far = dot_on(inject, lam_two[0], 1, 0) + dot_on(inject, lam_two[1], 1, 0)
        moved = scaled * to_end
        grad_inject += dot_three(split(moved), lam_two, 1, 1)
        rising = split(grad_ssd * jnp.exp(total_p))
        grad_readout += dot_three(rising, split(held), 1, 1)
        end_parts.append(jnp.sum(lam * next_state[:, cols], axis=0, keepdims=True))
        adjoint[:, cols] = lam * jnp.exp(total_p[BLOCK - 1 : BLOCK, :]) + (
            dot_on(readout, rising[0], 0, 0) + dot_on(readout, rising[1], 0, 0)
        )
        next_state[:, cols] = held
        pure = ssd - skip[:, cols] * x
        decay_parts.append(grad_ssd * pure - scaled * local - moved * far)
        grad_scaled = local + to_end * far
        step_parts.append(x * grad_scaled)
        skip_parts.append(jnp.sum(grad_ssd * x, axis=0, keepdims=True))
        grad_x = dt_p * grad_scaled + skip[:, cols] * grad_ssd
        before = convolve(buffer, kernel_ref, pair * 2 * P_SIZE, 2 * P_SIZE)
        sig = sigmoid(before)
        grads[0:BLOCK, cols] = grad_x * (sig * (1.0 + before * (1.0 - sig)))
    row_grads = head_sums(jnp.concatenate(decay_parts, axis=1))
    upper = order_mask(True).astype(F32)
    ends = head_sums(jnp.concatenate(end_parts, axis=1))
    grad_log = dot_on(upper, row_grads, 1, 0, HIGH) + ends
    grad_dt = head_sums(jnp.concatenate(step_parts, axis=1)) + decay * grad_log
    grad_raw = grad_dt * sigmoid(raw + head_ref[0:1, :])
    grad_step_ref[...] = jnp.zeros((BLOCK, N), BF16)
    grad_step_ref[:, 0 : grad_raw.shape[1]] = grad_raw.astype(BF16)
    grad_head_ref[0:1, :] += jnp.sum(grad_raw, axis=0, keepdims=True)
    grad_head_ref[1:2, :] += decay * jnp.sum(dt * grad_log, axis=0, keepdims=True)
    grad_head_ref[2:3, :] += head_sums(jnp.concatenate(skip_parts, axis=1))
    scores_two = split(grad_scores_t)
    grad_inject = grad_inject + dot_two(scores_two, readout, 1, 0)
    grad_readout = grad_readout + dot_two(scores_two, inject, 0, 0)
    grad_own_ref[...] = jnp.where(odd, grad_readout, grad_inject)
    grad_other_ref[...] = jnp.where(odd, grad_inject, grad_readout)
    grad_ref[:, width : 2 * width] = convolve_back(buffer, grads, kernel_ref, grad_kernel_ref)


def convolve_back(buffer, grads, kernel_ref, grad_kernel_ref):
    taps = kernel_ref.shape[0] - 1
    width = grads.shape[1]
    here = grads[0:BLOCK, :]
    grad_kernel_ref[taps : taps + 1, :] += jnp.sum(here, axis=0, keepdims=True)
    total = jnp.zeros((BLOCK, width), F32)
    for tap in range(taps):
        low = EDGE - taps + 1 + tap
        grad_kernel_ref[tap : tap + 1, :] += jnp.sum(here * buffer[low : low + BLOCK, :], axis=0, keepdims=True)
        ahead = taps - 1 - tap
        total = total + kernel_ref[tap : tap + 1, 0:width] * grads[ahead : ahead + BLOCK, :]
    return total.astype(BF16)


def mixer_backward(odd, proj, low, grad_gated, ssd, states, norms, kernel, heads, gain):
    length, width = grad_gated.shape
    wide = width + 2 * N
    count = length // BLOCK
    place = lambda i: count - 1 - i
    back = lambda i: (place(i), 0)
    edge = lambda i: jnp.maximum(place(i) * (BLOCK // EDGE) - 1, 0)
    whole = lambda i: (0, 0)
    specs = proj_specs(width, place)
    return pl.pallas_call(
        backward_body,
        grid=(count,),
        in_specs=specs[:3]
        + [
            specs[4],
            pl.BlockSpec((EDGE, width), lambda i: (edge(i), 1)),
            pl.BlockSpec((BLOCK, wide), back),
            pl.BlockSpec((BLOCK, width), back),
            pl.BlockSpec((BLOCK, width), back),
            pl.BlockSpec((1, N, width), lambda i: (place(i), 0, 0)),
            pl.BlockSpec((BLOCK, norms.shape[1]), back),
            pl.BlockSpec(kernel.shape, whole),
            pl.BlockSpec(heads.shape, whole),
            pl.BlockSpec(gain.shape, whole),
        ],
        out_specs=[
            pl.BlockSpec((BLOCK, 2 * width), back),
            pl.BlockSpec((BLOCK, N), back),
            pl.BlockSpec((BLOCK, N), back),
            pl.BlockSpec((BLOCK, N), back),
            pl.BlockSpec((kernel.shape[0], width), whole),
            pl.BlockSpec(heads.shape, whole),
            pl.BlockSpec(gain.shape, whole),
        ],
        out_shape=[
            jax.ShapeDtypeStruct((length, 2 * width), BF16),
            jax.ShapeDtypeStruct((length, N), BF16),
            jax.ShapeDtypeStruct((length, N), F32),
            jax.ShapeDtypeStruct((length, N), F32),
            jax.ShapeDtypeStruct((kernel.shape[0], width), F32),
            jax.ShapeDtypeStruct(heads.shape, F32),
            jax.ShapeDtypeStruct(gain.shape, F32),
        ],
        scratch_shapes=[
            pltpu.VMEM((N, width), F32),
            pltpu.VMEM((BLOCK + EDGE, width), F32),
            pltpu.VMEM((BLOCK + EDGE, width), F32),
            pltpu.VMEM((N, width), F32),
        ],
        compiler_params=pltpu.CompilerParams(vmem_limit_bytes=56 << 20),
        name="mixer_backward",
    )(odd, proj, proj, proj, proj, low, grad_gated, ssd, states, norms, kernel, heads, gain)


def map_backward_body(own_ref, edge_ref, mine_ref, theirs_ref, step_ref, kernel_ref, grad_ref, grad_kernel_ref, buffer, grads):
    step = pl.program_id(0)

    @pl.when(step == 0)
    def _():
        grads[BLOCK : BLOCK + EDGE, :] = jnp.zeros((EDGE, N), F32)
        grad_kernel_ref[...] = jnp.zeros_like(grad_kernel_ref)

    @pl.when(step > 0)
    def _():
        grads[BLOCK : BLOCK + EDGE, :] = grads[0:EDGE, :]

    last = step == pl.num_programs(0) - 1
    buffer[0:EDGE, :] = jnp.where(last, 0.0, edge_ref[...].astype(BF16).astype(F32))
    buffer[EDGE : EDGE + BLOCK, :] = own_ref[...].astype(BF16).astype(F32)
    before = convolve(buffer, kernel_ref, 0, N)
    sig = sigmoid(before)
    grads[0:BLOCK, :] = (mine_ref[...] + theirs_ref[...]) * (sig * (1.0 + before * (1.0 - sig)))
    grad_ref[:, 0:N] = convolve_back(buffer, grads, kernel_ref, grad_kernel_ref)
    grad_ref[:, N : 2 * N] = step_ref[...]


def map_backward(proj, mine, theirs, steps, kernel, column):
    length = mine.shape[0]
    count = length // BLOCK
    place = lambda i: count - 1 - i
    edge = lambda i: jnp.maximum(place(i) * (BLOCK // EDGE) - 1, 0)
    back = lambda i: (place(i), 0)
    whole = lambda i: (0, 0)
    narrow = pl.BlockSpec((BLOCK, N), back)
    return pl.pallas_call(
        map_backward_body,
        grid=(count,),
        in_specs=[
            pl.BlockSpec((BLOCK, N), lambda i: (place(i), column // N)),
            pl.BlockSpec((EDGE, N), lambda i: (edge(i), column // N)),
            narrow,
            narrow,
            narrow,
            pl.BlockSpec(kernel.shape, whole),
        ],
        out_specs=[pl.BlockSpec((BLOCK, 2 * N), back), pl.BlockSpec(kernel.shape, whole)],
        out_shape=[jax.ShapeDtypeStruct((length, 2 * N), BF16), jax.ShapeDtypeStruct(kernel.shape, F32)],
        scratch_shapes=[pltpu.VMEM((BLOCK + EDGE, N), F32), pltpu.VMEM((BLOCK + EDGE, N), F32)],
        name="map_backward",
    )(proj, proj, mine, theirs, steps, kernel)


def remote(src, dst, send, recv, device):
    return pltpu.make_async_remote_copy(
        src_ref=src, dst_ref=dst, send_sem=send, recv_sem=recv, device_id=device, device_id_type=MESH
    )


def gather_body(order, sizes, parts, *refs):
    nctx, ndp, ntp = sizes
    ntok, nin, nw = 2, parts[-1][0] + 1, parts[-1][2] + 1
    toks, weights = refs[:ntok], refs[ntok : ntok + nin]
    tok_outs = refs[ntok + nin : 2 * ntok + nin]
    weight_outs = refs[2 * ntok + nin : 2 * ntok + nin + nw]
    z_send, z_recv, t_send, t_recv, w_send, w_recv, x_send, x_recv, own = refs[2 * ntok + nin + nw :]
    c, d, t = lax.axis_index("ctx"), lax.axis_index("dp"), lax.axis_index("tp")
    near = t + 1 - 2 * lax.rem(t, 2)
    far = lax.rem(t + 2, ntp)
    length = toks[0].shape[0]
    part = length // ntp

    barrier = pltpu.get_barrier_semaphore()
    peers = [{"ctx": lax.rem(c + s, nctx)} for s in range(1, nctx)]
    peers += [{"dp": lax.rem(d + s, ndp)} for s in range(1, ndp)]
    peers += [{"tp": near}, {"tp": far}]
    for peer in peers:
        pl.semaphore_signal(barrier, inc=1, device_id=peer, device_id_type=MESH)
    pl.semaphore_wait(barrier, len(peers))

    def piece(p, to):
        array, column, _, _, width = parts[p]
        return weights[array].at[:, pl.ds(pl.multiple_of(column(to), N), width)]

    def landing(p, block):
        _, _, out, start, width = parts[p]
        return weight_outs[out].at[d, block, :, start : start + width]

    def of(out):
        return [p for p in range(len(parts)) if parts[p][2] == out]

    def rows(a, block, quarter):
        return tok_outs[a].at[pl.ds(pl.multiple_of(block * length + quarter * part, 16), part), :]

    def hop(a, j, side):
        block = c - j if side == 0 else c + j
        to = c + 1 if side == 0 else c - 1
        valid = (block >= 0) & (to < nctx) if side == 0 else (block < nctx) & (to >= 0)
        safe = jnp.clip(block, 0, nctx - 1)
        source = toks[a].at[pl.ds(pl.multiple_of(t * part, 16), part), :] if j == 0 else rows(a, safe, t)
        copy = remote(source, rows(a, safe, t), z_send.at[a, j, side], z_recv.at[a, safe], {"ctx": jnp.clip(to, 0, nctx - 1)})
        return valid, copy

    def arrival(j, side):
        block = c - 1 - j if side == 0 else c + 1 + j
        valid = block >= 0 if side == 0 else block < nctx
        return valid, jnp.clip(block, 0, nctx - 1)

    def tp_copy(a, block, kind):
        quarter = t if kind < 2 else far
        view = rows(a, block, quarter)
        return remote(view, view, t_send.at[a, block, kind], t_recv.at[a, block, kind], {"tp": far if kind == 0 else near})

    def tp_arrival(a, block, kind):
        quarter = far if kind == 0 else (near if kind == 1 else lax.rem(near + 2, ntp))
        view = rows(a, block, quarter)
        return remote(view, view, t_send.at[a, block, kind], t_recv.at[a, block, kind], {"tp": near})

    def w_copy(p, s):
        to = lax.rem(c + s, nctx)
        return remote(piece(p, to), landing(p, c), w_send.at[p, s], w_recv.at[p, s], {"ctx": to})

    def w_arrival(p, s):
        view = landing(p, lax.rem(c - s + nctx, nctx))
        return remote(view, view, w_send.at[p, s], w_recv.at[p, s], {"ctx": c})

    def x_copy(a, s, e):
        view = weight_outs[a].at[d, lax.rem(c - s + nctx, nctx)]
        return remote(view, view, x_send.at[a, s, e], x_recv.at[a, s, e], {"dp": lax.rem(d + e, ndp)})

    def x_arrival(a, s, e):
        view = weight_outs[a].at[lax.rem(d - e + ndp, ndp), lax.rem(c - s + nctx, nctx)]
        return remote(view, view, x_send.at[a, s, e], x_recv.at[a, s, e], {"dp": d})

    def own_tok(a):
        return pltpu.make_async_copy(toks[a], tok_outs[a].at[pl.ds(pl.multiple_of(c * length, 16), length), :], own.at[a])

    def own_piece(p):
        return pltpu.make_async_copy(piece(p, c), landing(p, c), own.at[ntok + p])

    def launch(step):
        kind, a, j = step
        if kind == "tok":
            for side in (0, 1):
                valid, copy = hop(a, j, side)

                @pl.when(valid)
                def _():
                    copy.start()
        else:
            for p in of(a):
                w_copy(p, j).start()

    def settle(step):
        kind, a, j = step
        if kind == "tok":
            for side in (0, 1):
                valid, block = arrival(j, side)

                @pl.when(valid)
                def _():
                    view = rows(a, block, t)
                    remote(view, view, z_send.at[a, j, side], z_recv.at[a, block], {"ctx": c}).wait_recv()
                    tp_copy(a, block, 0).start()
                    tp_copy(a, block, 1).start()
        else:
            for p in of(a):
                w_arrival(p, j).wait_recv()
            for e in range(1, ndp):
                x_copy(a, j, e).start()

    def settle_far(step):
        kind, a, j = step
        if kind == "tok":
            for side in (0, 1):
                valid, block = arrival(j, side)

                @pl.when(valid)
                def _():
                    tp_arrival(a, block, 0).wait_recv()
                    tp_copy(a, block, 2).start()

    for step in order[:DEPTH]:
        launch(step)
    for p in range(len(parts)):
        own_piece(p).start()
    for p in range(len(parts)):
        own_piece(p).wait()
    for a in range(nw):
        for e in range(1, ndp):
            x_copy(a, 0, e).start()
    for a in range(ntok):
        own_tok(a).start()
    for index, step in enumerate(order):
        settle(step)
        if index + DEPTH < len(order):
            launch(order[index + DEPTH])
        if index >= 2:
            settle_far(order[index - 2])
    for step in order[-2:]:
        settle_far(step)
    for kind, a, j in order:
        if kind == "tok":
            for side in (0, 1):
                valid, copy = hop(a, j, side)
                here, block = arrival(j, side)

                @pl.when(valid)
                def _():
                    copy.wait_send()

                @pl.when(here)
                def _():
                    for part_kind in range(3):
                        tp_copy(a, block, part_kind).wait_send()
                    tp_arrival(a, block, 1).wait_recv()
                    tp_arrival(a, block, 2).wait_recv()
        else:
            for p in of(a):
                w_copy(p, j).wait_send()
            for e in range(1, ndp):
                x_copy(a, j, e).wait_send()
                x_arrival(a, j, e).wait_recv()
    for a in range(nw):
        for e in range(1, ndp):
            x_copy(a, 0, e).wait_send()
            x_arrival(a, 0, e).wait_recv()
    for a in range(ntok):
        own_tok(a).wait()


def gather_all(toks, weights, parts, sizes):
    nctx, ndp, ntp = sizes
    turns = range(1, nctx)
    nw = parts[-1][2] + 1
    widths = [sum(p[4] for p in parts if p[2] == out) for out in range(nw)]
    shard_rows = weights[0].shape[0]
    tok = lambda a, j: [("tok", a, j)] if j < nctx - 1 else []
    per = lambda a: [("w", a, s) for s in turns]
    order = tok(0, 0) + tok(1, 0) + per(0) + tok(0, 1) + tok(1, 1) + per(1)[:1] + tok(0, 2) + tok(1, 2) + per(1)[1:]
    any_space = pl.BlockSpec(memory_space=pl.ANY)
    length, model = toks[0].shape
    out_shape = [jax.ShapeDtypeStruct((nctx * length, model), BF16) for _ in toks]
    out_shape += [jax.ShapeDtypeStruct((ndp, nctx, shard_rows, width), BF16) for width in widths]
    dma = pltpu.SemaphoreType.DMA
    return pl.pallas_call(
        functools.partial(gather_body, order, sizes, parts),
        out_shape=out_shape,
        in_specs=[any_space] * (len(toks) + len(weights)),
        out_specs=[any_space] * len(out_shape),
        scratch_shapes=[
            dma((2, nctx, 2)), dma((2, nctx)), dma((2, nctx, 3)), dma((2, nctx, 3)),
            dma((len(parts), nctx)), dma((len(parts), nctx)), dma((nw, nctx, ndp)), dma((nw, nctx, ndp)), dma((2 + len(parts),)),
        ],
        compiler_params=pltpu.CompilerParams(collective_id=1, has_side_effects=True),
        name="gather_inputs",
    )(*toks, *weights)


def add_rows(target, sources, rows, step):
    def some(index, _):
        here = pl.ds(pl.multiple_of(index * step, step), step)
        total = sources[0][here, :].astype(F32)
        for source in sources[1:]:
            total = total + source[here, :].astype(F32)
        target[here, :] = total.astype(target.dtype)
        return 0

    lax.fori_loop(0, rows // step, some, 0)


def output_body(order, sizes, nw, parts, *refs):
    nctx, ndp, ntp = sizes
    nout = len(parts)
    partial, small, grads = refs[0], refs[1], refs[2 : 2 + nw]
    sum_out, small_out, grad_outs = refs[2 + nw], refs[3 + nw], refs[4 + nw : 4 + nw + nout]
    rest = refs[4 + nw + nout :]
    (near_in, far_out, far_in, z_out, z_in, held, acc, done) = rest[:8]
    x_ins, x_sums = rest[8 : 8 + nw], rest[8 + nw : 8 + 2 * nw]
    (near_s, near_r, far_s, far_r, z_s, z_r, x_s, x_r, w_s, w_r, fin_s, fin_r, local, small_s, small_r) = rest[8 + 2 * nw :]
    c, d, t = lax.axis_index("ctx"), lax.axis_index("dp"), lax.axis_index("tp")
    near = t + 1 - 2 * lax.rem(t, 2)
    far = lax.rem(t + 2, ntp)
    far_near = lax.rem(near + 2, ntp)
    length = sum_out.shape[0]
    part = length // ntp
    wrap = lambda i: lax.rem(i + nctx, nctx)

    barrier = pltpu.get_barrier_semaphore()
    others = [(e, s) for e in range(ndp) for s in range(nctx) if e or s]
    place = lambda e, s: {"dp": lax.rem(d + e, ndp), "ctx": lax.rem(c + s, nctx)}
    peers = [place(e, s) for e, s in others] + [{"tp": near}, {"tp": far}]
    for peer in peers:
        pl.semaphore_signal(barrier, inc=1, device_id=peer, device_id_type=MESH)
    pl.semaphore_wait(barrier, len(peers))

    def small_copy(e, s):
        return remote(small, small_out.at[d, c], small_s.at[e, s], small_r.at[e, s], place(e, s))

    def small_arrival(e, s):
        view = small_out.at[lax.rem(d - e + ndp, ndp), wrap(c - s)]
        return remote(view, view, small_s.at[e, s], small_r.at[e, s], place(e, s))

    def rows(s, quarter):
        return partial.at[pl.ds(pl.multiple_of(wrap(c + s) * length + quarter * part, 16), part), :]

    def near_copy(s, slot):
        return remote(rows(s, near if slot == 0 else far_near), near_in.at[s, slot], near_s.at[s, slot], near_r.at[s, slot], {"tp": near})

    def far_copy(s):
        return remote(far_out.at[s], far_in.at[s], far_s.at[s], far_r.at[s], {"tp": far})

    def z_copy(s):
        return remote(z_out.at[s], z_in.at[s], z_s.at[s], z_r.at[s], {"ctx": wrap(c + s)})

    def x_copy(a, s, e):
        to = lax.rem(d + e, ndp)
        return remote(grads[a].at[to, wrap(c + s)], x_ins[a].at[s, e - 1], x_s.at[a, s, e], x_r.at[a, s, e], {"dp": to})

    def piece(p, s):
        a, start, width, _, _ = parts[p]
        return x_sums[a].at[s, :, start : start + width]

    def landing(p, block):
        _, _, width, out, split_columns = parts[p]
        if split_columns:
            return grad_outs[out].at[:, pl.ds(pl.multiple_of(block * width, N), width)]
        return grad_outs[out].at[block]

    def w_copy(p, s):
        return remote(piece(p, s), landing(p, c), w_s.at[p, s], w_r.at[p, s], {"ctx": wrap(c + s)})

    def w_arrival(p, s):
        view = landing(p, wrap(c - s))
        return remote(view, view, w_s.at[p, s], w_r.at[p, s], {"ctx": c})

    def w_own(p):
        return pltpu.make_async_copy(piece(p, 0), landing(p, c), local.at[2 + nw * nctx + p])

    def load(s, quarter, slot):
        return pltpu.make_async_copy(rows(s, quarter), held.at[slot], local.at[slot])

    def load_grad(a, s):
        return pltpu.make_async_copy(grads[a].at[d, wrap(c + s)], x_sums[a].at[s], local.at[2 + a * nctx + s])

    def start_x(s):
        for a in range(nw):
            for e in range(1, ndp):
                x_copy(a, s, e).start()

    def near_sum(s):
        load(s, far, 0).start()
        near_copy(s, 1).wait_recv()
        load(s, far, 0).wait()
        add_rows(far_out.at[s], [held.at[0], near_in.at[s, 1]], part, 16)
        far_copy(s).start()

    def far_sum(s):
        load(s, t, 1).start()
        near_copy(s, 0).wait_recv()
        far_copy(s).wait_recv()
        load(s, t, 1).wait()
        add_rows(acc if s == 0 else z_out.at[s], [held.at[1], near_in.at[s, 0], far_in.at[s]], part, 16)
        if s > 0:
            z_copy(s).start()

    def grad_sum(s):
        for a in range(nw):
            load_grad(a, s).wait()
            for e in range(1, ndp):
                x_copy(a, s, e).wait_recv()
            add_rows(x_sums[a].at[s], [x_sums[a].at[s]] + [x_ins[a].at[s, e - 1] for e in range(1, ndp)], x_sums[a].shape[1], 16)
        for p in range(nout):
            if s > 0:
                w_copy(p, s).start()
            else:
                w_own(p).start()

    for s in order:
        for slot in (1, 0):
            near_copy(s, slot).start()
        for a in range(nw):
            load_grad(a, s).start()
    ahead = 2
    for s in order[:ahead]:
        start_x(s)
    for e, s in others:
        small_copy(e, s).start()
    small_own = pltpu.make_async_copy(small, small_out.at[d, c], local.at[2 + nw * nctx + nout])
    small_own.start()
    for s in order[:ahead]:
        near_sum(s)
    for index, s in enumerate(order):
        far_sum(s)
        if index + ahead < nctx:
            near_sum(order[index + ahead])
        grad_sum(s)
        if index + ahead < nctx:
            start_x(order[index + ahead])
    for s in range(1, nctx):
        z_copy(s).wait_recv()
    add_rows(done, [acc] + [z_in.at[s] for s in range(1, nctx)], part, 16)

    def mine(quarter):
        return sum_out.at[pl.ds(pl.multiple_of(quarter * part, 16), part), :]

    finals = [
        remote(done, mine(t), fin_s.at[0], fin_r.at[0], {"tp": far}),
        remote(done, mine(t), fin_s.at[1], fin_r.at[1], {"tp": near}),
        remote(mine(far), mine(far), fin_s.at[2], fin_r.at[2], {"tp": near}),
    ]
    keep = pltpu.make_async_copy(done, mine(t), local.at[0])
    finals[0].start()
    finals[1].start()
    keep.start()
    remote(mine(far), mine(far), fin_s.at[0], fin_r.at[0], {"tp": far}).wait_recv()
    finals[2].start()
    remote(mine(near), mine(near), fin_s.at[1], fin_r.at[1], {"tp": near}).wait_recv()
    remote(mine(far_near), mine(far_near), fin_s.at[2], fin_r.at[2], {"tp": near}).wait_recv()
    keep.wait()
    for copy in finals:
        copy.wait_send()
    for s in order:
        for slot in (1, 0):
            near_copy(s, slot).wait_send()
        far_copy(s).wait_send()
        for a in range(nw):
            for e in range(1, ndp):
                x_copy(a, s, e).wait_send()
        for p in range(nout):
            if s > 0:
                w_copy(p, s).wait_send()
                w_arrival(p, s).wait_recv()
            else:
                w_own(p).wait()
        if s > 0:
            z_copy(s).wait_send()
    for e, s in others:
        small_copy(e, s).wait_send()
        small_arrival(e, s).wait_recv()
    small_own.wait()


def return_all(partial, small, grads, parts, sizes):
    nctx, ndp, ntp = sizes
    length = partial.shape[0] // nctx
    part, model = length // ntp, partial.shape[1]
    nw, nout = len(grads), len(parts)
    outs = [(nctx,) + grads[p[0]].shape[2:] if not p[4] else (grads[0].shape[2], nctx * p[2]) for p in parts]
    order = [nctx // 2] + [s for s in range(1, nctx) if s != nctx // 2] + [0]
    any_space = pl.BlockSpec(memory_space=pl.ANY)
    dma = pltpu.SemaphoreType.DMA
    vmem = pltpu.VMEM
    strip = lambda *lead: vmem(lead + (part, model), BF16)
    return pl.pallas_call(
        functools.partial(output_body, order, sizes, nw, parts),
        out_shape=[jax.ShapeDtypeStruct((length, model), BF16), jax.ShapeDtypeStruct((ndp, nctx) + small.shape, F32)]
        + [jax.ShapeDtypeStruct(out, BF16) for out in outs],
        in_specs=[any_space] * (2 + nw),
        out_specs=[any_space] * (2 + nout),
        scratch_shapes=[
            strip(nctx, 2), strip(nctx), strip(nctx), strip(nctx), strip(nctx), strip(2), vmem((part, model), F32), strip(),
        ]
        + [vmem((nctx, max(ndp - 1, 1)) + g.shape[2:], BF16) for g in grads]
        + [vmem((nctx,) + g.shape[2:], BF16) for g in grads]
        + [
            dma((nctx, 2)), dma((nctx, 2)), dma((nctx,)), dma((nctx,)), dma((nctx,)), dma((nctx,)),
            dma((nw, nctx, ndp)), dma((nw, nctx, ndp)), dma((nout, nctx)), dma((nout, nctx)), dma((3,)), dma((3,)),
            dma((2 + nw * nctx + nout + 1,)), dma((ndp, nctx)), dma((ndp, nctx)),
        ],
        compiler_params=pltpu.CompilerParams(collective_id=2, has_side_effects=True, vmem_limit_bytes=60 << 20),
        name="return_outputs",
    )(partial, small, *grads)


def small_body(sizes, value, total, gathered, send, recv):
    nctx, ndp = sizes
    c, d = lax.axis_index("ctx"), lax.axis_index("dp")
    others = [(e, s) for e in range(ndp) for s in range(nctx) if e or s]
    place = lambda e, s: {"dp": lax.rem(d + e, ndp), "ctx": lax.rem(c + s, nctx)}
    barrier = pltpu.get_barrier_semaphore()
    for e, s in others:
        pl.semaphore_signal(barrier, inc=1, device_id=place(e, s), device_id_type=MESH)
    pl.semaphore_wait(barrier, len(others))
    gathered[d, c] = value[...]
    for e, s in others:
        remote(value, gathered.at[d, c], send.at[e, s], recv.at[e, s], place(e, s)).start()
    for e, s in others:
        view = gathered.at[lax.rem(d - e + ndp, ndp), lax.rem(c - s + nctx, nctx)]
        remote(view, view, send.at[e, s], recv.at[e, s], place(e, s)).wait_recv()
        remote(value, gathered.at[d, c], send.at[e, s], recv.at[e, s], place(e, s)).wait_send()
    running = jnp.zeros(value.shape, F32)
    for e in range(ndp):
        for s in range(nctx):
            running = running + gathered[e, s]
    total[...] = running


def sum_small(value, sizes):
    nctx, ndp = sizes
    vmem = pl.BlockSpec(memory_space=pltpu.VMEM)
    dma = pltpu.SemaphoreType.DMA
    return pl.pallas_call(
        functools.partial(small_body, sizes),
        out_shape=jax.ShapeDtypeStruct(value.shape, F32),
        in_specs=[vmem],
        out_specs=vmem,
        scratch_shapes=[pltpu.VMEM((ndp, nctx) + value.shape, F32), dma((ndp, nctx)), dma((ndp, nctx))],
        compiler_params=pltpu.CompilerParams(collective_id=3, has_side_effects=True),
        name="sum_small",
    )(value)


def dot_last(left_side, right_side):
    return lax.dot_general(left_side, right_side, (((1,), (1,)), ((), ())), preferred_element_type=F32)


def dot_first(left_side, right_side):
    return lax.dot_general(left_side, right_side, (((0,), (0,)), ((), ())), preferred_element_type=F32)


def sum_rows(partial):
    return lax.psum_scatter(partial.astype(BF16), ("ctx", "tp"), scatter_dimension=0, tiled=True).astype(F32)


def shards(tokens, norm_gain, zx_weight, bc_weight, dt_weight, conv_x, conv_bc, head_params, gate_gain, out_weight, cotangent):
    seq_count, length, model_width = tokens.shape
    assert seq_count == 1
    nctx, ntp, ndp = lax.axis_size("ctx"), lax.axis_size("tp"), lax.axis_size("dp")
    ctx = lax.axis_index("ctx")
    rows = dt_weight.shape[0]
    inner = conv_x.shape[1]
    pair_width = bc_weight.shape[2]
    groups = pair_width // N
    share = nctx // groups
    assert share == 2 and groups * share == nctx
    width = inner // nctx
    heads = dt_weight.shape[1] // nctx
    taps = conv_x.shape[0] - 1
    group_width = inner // groups

    def mine(value):
        return lax.dynamic_index_in_dim(value, ctx, 0, False)

    def partner(value):
        return lax.ppermute(value, "ctx", [(i, i ^ 1) for i in range(nctx)])

    hidden = tokens.astype(F32).reshape(length, model_width)
    cot = cotangent.reshape(length, model_width)
    rscale = lax.rsqrt(jnp.mean(hidden * hidden, axis=-1, keepdims=True) + EPS)
    normed = (hidden * rscale * norm_gain).astype(BF16)

    steps = jnp.pad(dt_weight.reshape(rows, nctx, heads), ((0, 0), (0, 0), (0, N - heads))).reshape(rows, nctx * N)
    map_at = lambda which: lambda to: (lax.rem(to + which, 2) * groups + to // share) * N
    parts = (
        (0, lambda to: to * width, 0, 0, width),
        (0, lambda to: inner + to * width, 0, width, width),
        (1, map_at(0), 0, 2 * width, N),
        (2, lambda to: to * N, 0, 2 * width + N, N),
        (1, map_at(1), 0, 2 * width + 2 * N, N),
        (3, lambda to: to * width, 1, 0, width),
    )
    sources = (zx_weight.reshape(rows, 2 * inner), bc_weight.reshape(rows, 2 * pair_width), steps, out_weight)
    normed_all, cot_all, weight_in, weight_out = gather_all((normed, cot), sources, parts, (nctx, ndp, ntp))
    weight_in = weight_in.reshape(model_width, -1)
    weight_out = weight_out.reshape(model_width, width)

    grad_gated = jnp.dot(cot_all, weight_out, preferred_element_type=F32)
    proj = jnp.dot(normed_all, weight_in, preferred_element_type=F32)
    odd = lax.rem(ctx, 2)
    kernel_x = mine(conv_x.reshape(taps + 1, nctx, width).transpose(1, 0, 2))
    kernel_maps = conv_bc.reshape(taps + 1, 2, groups, N).transpose(2, 1, 0, 3).reshape(nctx, taps + 1, N)
    kernel_own = mine(kernel_maps)
    kernel_other = lax.dynamic_index_in_dim(kernel_maps, ctx + 1 - 2 * odd, 0, False)
    kernel = jnp.concatenate([kernel_x, kernel_own, kernel_other], axis=1)
    odd = odd.astype(jnp.int32).reshape(1, 1)
    heads_mine = mine(head_params.reshape(3, nctx, heads).transpose(1, 0, 2))
    gain = mine(gate_gain.reshape(nctx, 1, width))
    low, ssd, states, sums = mixer_forward(odd, proj, grad_gated, kernel, heads_mine, gain)
    sums = (sums + partner(sums)) / group_width
    inverse = lax.rsqrt(sums[0] + EPS)
    norms = jnp.stack([inverse, inverse * inverse * inverse * sums[1]], axis=1)
    gate_pre = proj[:, :width]
    gated_norm = (ssd * (gate_pre * jax.nn.sigmoid(gate_pre)) * norms[:, 0:1] * gain).astype(BF16)
    branch = sum_rows(dot_last(gated_norm, weight_out))
    grad_zx, grad_steps, grad_own, grad_other, grad_kernel_x, grad_heads, gate_gain_grad = mixer_backward(
        odd, proj, low, grad_gated, ssd, states, norms, kernel, heads_mine, gain
    )
    theirs = partner(grad_other)
    grad_rest, grad_kernel_own = map_backward(proj, grad_own, theirs, grad_steps, kernel_own, 2 * width)
    grad_all = jnp.concatenate([grad_zx, grad_rest], axis=1)
    blocks = lambda grad: grad.astype(BF16).reshape(ndp, nctx, rows, -1)
    weight_grads = (
        blocks(dot_first(normed_all, grad_zx)),
        blocks(dot_first(normed_all, grad_rest)),
        blocks(dot_first(cot_all, gated_norm)),
    )
    partial = dot_last(grad_all, weight_in[:, : grad_all.shape[1]]).astype(BF16)
    pieces = (grad_kernel_x, grad_kernel_own, grad_heads, gate_gain_grad)
    small = jnp.concatenate([piece.reshape(-1) for piece in pieces])
    lines = -(-small.shape[0] // (8 * N)) * 8
    small = jnp.pad(small, (0, lines * N - small.shape[0])).reshape(lines, N)
    out_parts = (
        (0, 0, width, 0, True),
        (0, width, width, 1, True),
        (1, 0, 2 * N, 2, False),
        (2, 0, width, 3, True),
    )
    grad_normed, table, back_z, back_x, back_rest, back_out = return_all(
        partial, small, weight_grads, out_parts, (nctx, ndp, ntp)
    )
    grad_normed, branch = lax.optimization_barrier((grad_normed, branch))
    part = length // ntp
    token_part = lax.dynamic_slice_in_dim(tokens.reshape(length, model_width), lax.axis_index("tp") * part, part, 0)
    mixed = lax.all_gather((token_part.astype(F32) + branch).astype(BF16), "tp", axis=0, tiled=True)
    grad_normed = grad_normed.astype(F32)

    grad_hat = grad_normed * norm_gain
    norm_gain_grad = jnp.sum(grad_normed * hidden * rscale, axis=0)
    grad_hidden = rscale * grad_hat - hidden * (rscale * rscale * rscale) * jnp.mean(
        grad_hat * hidden, axis=1, keepdims=True
    )
    tokens_grad = cot.astype(F32) + grad_hidden

    upper = lax.broadcasted_iota(jnp.int32, (rows, 2, inner), 1) == 0
    zx_weight_grad = jnp.where(upper, back_z[:, None, :], back_x[:, None, :]).astype(F32)
    back_rest = back_rest.astype(F32)
    bc_weight_grad = back_rest[:, :, :N].reshape(groups, 2, rows, N).transpose(2, 1, 0, 3).reshape(rows, 2, groups * N)
    dt_weight_grad = back_rest[:, :, N : N + heads].transpose(1, 0, 2).reshape(rows, nctx * heads)
    out_weight_grad = back_out.astype(F32)

    table = jnp.sum(table, axis=0).reshape(nctx, lines * N)
    ends = [0]
    for piece in pieces:
        ends.append(ends[-1] + piece.size)
    kernel_x, kernel_own, head_grad, gain_grad = [table[:, a:b] for a, b in zip(ends[:-1], ends[1:])]
    conv_x_grad = kernel_x.reshape(nctx, taps + 1, width).transpose(1, 0, 2).reshape(taps + 1, inner)
    conv_bc_grad = kernel_own.reshape(groups, 2, taps + 1, N).transpose(2, 1, 0, 3).reshape(taps + 1, 2, groups * N)
    head_grad = head_grad.reshape(nctx, 3, heads).transpose(1, 0, 2).reshape(3, nctx * heads)
    gate_gain_grad = gain_grad.reshape(inner)
    norm_gain_grad = sum_small(norm_gain_grad.reshape(-1, N), (nctx, ndp)).reshape(model_width)
    return (
        mixed.reshape(tokens.shape),
        tokens_grad.reshape(tokens.shape),
        norm_gain_grad,
        zx_weight_grad,
        bc_weight_grad,
        dt_weight_grad,
        conv_x_grad,
        conv_bc_grad,
        head_grad,
        gate_gain_grad,
        out_weight_grad,
    )


def solution(mesh):
    wide = P(("dp", "ctx"), None, "tp")
    flat = P(("dp", "ctx"), "tp")
    rows = P("dp", "ctx", None)
    return jax.shard_map(
        shards,
        mesh=mesh,
        in_specs=(rows, P(), wide, wide, flat, P(None, "tp"), P(None, None, "tp"), P(None, "tp"), P("tp"), flat, rows),
        out_specs=(rows, rows, P(), wide, wide, flat, P(None, "tp"), P(None, None, "tp"), P(None, "tp"), P("tp"), flat),
        check_vma=False,
    )
```
